32 devices in a mesh: group: 16 (over z, y, core), shard: 2 (over x).
Axes of the slice: x: 2, y: 2, z: 4, core: 2. Of those that a mesh axis runs over, the one named last changes fastest.
Arguments:
- frames: bfloat16 [64, 256, 512], P(('group', 'shard')), may hold values from -6 to 6
- lengths: int32 [64], P(('group', 'shard')), may hold values from 128 to 256, as said below
- cotangent: bfloat16 [64, 256, 512], P(('group', 'shard')), may hold values from -6 to 6
- ffn_in: float32 [2, 512, 2048], P(None, 'shard'), may hold values from -0.25 to 0.25
- ffn_in_moment: float32 [2, 512, 2048], P(None, 'shard'), may hold values from -10 to 10
- ffn_in_square: float32 [2, 512, 2048], P(None, 'shard'), may hold values from 0.2768896 to 1.1075584
- ffn_out: float32 [2, 2048, 512], P(None, 'shard'), may hold values from -0.25 to 0.25
- ffn_out_moment: float32 [2, 2048, 512], P(None, 'shard'), may hold values from -10 to 10
- ffn_out_square: float32 [2, 2048, 512], P(None, 'shard'), may hold values from 0.2768896 to 1.1075584
- attn_proj: float32 [4, 512, 512], P(None, 'shard')
- attn_moment: float32 [4, 512, 512], P(None, 'shard')
- attn_square: float32 [4, 512, 512], P(None, 'shard')
- conv_proj: float32 [512, 1536], P('shard')
- conv_moment: float32 [512, 1536], P('shard'), may hold values from -32 to 32
- conv_square: float32 [512, 1536], P('shard'), may hold values from 2.62144 to 10.48576
- vectors: float32 [37, 512], P(None, 'shard')
- vectors_moment: float32 [37, 512], P(None, 'shard'), may hold values from -32 to 32
- vectors_square: float32 [37, 512], P(None, 'shard'), may hold values from 2.62144 to 10.48576
- rel_keys: float32 [73, 64], replicated, may hold values from -4 to 4
- rel_moment: float32 [73, 64], replicated, may hold values from -40 to 40
- rel_square: float32 [73, 64], replicated, may hold values from 4.096 to 16.384
Outputs:
- output: bfloat16 [64, 256, 512], P(('group', 'shard'))
- input_grad: bfloat16 [64, 256, 512], P(('group', 'shard'))
- grad_ffn_in: float32 [2, 512, 2048], P(None, 'shard')
- new_ffn_in: float32 [2, 512, 2048], P(None, 'shard')
- new_ffn_in_moment: float32 [2, 512, 2048], P(None, 'shard')
- new_ffn_in_square: float32 [2, 512, 2048], P(None, 'shard')
- grad_ffn_out: float32 [2, 2048, 512], P(None, 'shard')
- new_ffn_out: float32 [2, 2048, 512], P(None, 'shard')
- new_ffn_out_moment: float32 [2, 2048, 512], P(None, 'shard')
- new_ffn_out_square: float32 [2, 2048, 512], P(None, 'shard')
- grad_attn_proj: float32 [4, 512, 512], P(None, 'shard')
- new_attn_proj: float32 [4, 512, 512], P(None, 'shard')
- new_attn_moment: float32 [4, 512, 512], P(None, 'shard')
- new_attn_square: float32 [3, 512, 512], P(None, 'shard')
- new_attn_out_square: float32 [512, 512], P('shard')
- grad_conv_proj: float32 [512, 1536], P('shard')
- new_conv_proj: float32 [512, 1536], P('shard')
- new_conv_moment: float32 [512, 1536], P('shard')
- new_conv_square: float32 [512, 1536], P('shard')
- grad_vectors: float32 [37, 512], P(None, 'shard')
- new_vectors: float32 [37, 512], P(None, 'shard')
- new_vectors_moment: float32 [37, 512], P(None, 'shard')
- new_vectors_square: float32 [37, 512], P(None, 'shard')
- grad_rel_keys: float32 [73, 64], replicated
- new_rel_keys: float32 [73, 64], replicated
- new_rel_moment: float32 [73, 64], replicated
- new_rel_square: float32 [73, 64], replicated
- trust_norms: float32 [2, 18], replicated
The draws below stay inside these ranges and needn't reach their ends.
Inputs may be any that keep to these rules, and one draw needn't show every extreme that they name: `lengths`: every sequence has at least 128 valid frames; the first sequence has all 256.
All inputs are finite; a program needn't handle non-finite values.
Results may differ from the reference program's by a relative error of at most 0.02.
Values may be sent and summed in bfloat16 or wider, within the bound.
No kernel may reach another device: no remote copies, remote signals or barrier semaphores. Data moves between devices by JAX's collectives and lax.ppermute only.
A program may use at most 320 MiB of HBM per device.

```python
import math
import jax
import jax.numpy as jnp
from jax import lax

D = 512
HEADS = 8
HEAD = 64
FF = 2048
KERNEL = 31
BACK = 64
AHEAD = 8
RELS = 73
LEN = 256
STEP = 10
SEQS = 64


def draw_lengths(key, part):
    drawn = jax.random.randint(key, (SEQS,), LEN // 2, LEN + 1)
    return jnp.where(jnp.arange(SEQS) == 0, LEN, drawn).astype(jnp.int32)


def matrix_entries(key, layout):
    return jax.random.truncated_normal(key, -4.0, 4.0, layout, jnp.float32)


def draw_attn_proj(key, part):
    base = matrix_entries(key, (4, D, D)) / math.sqrt(D)
    widen = jnp.array([1.0, 1.0, 1.0, math.sqrt(LEN / 2.0)], jnp.float32)
    return base * widen[:, None, None]


def draw_conv_proj(key, part):
    base = matrix_entries(key, (D, 3 * D)) / math.sqrt(D)
    widen = jnp.where(jnp.arange(3 * D) >= 2 * D, math.sqrt(2.0), 1.0).astype(jnp.float32)
    return base * widen[None, :]


def draw_vectors(key, part):
    first_key, second_key = jax.random.split(key)
    taps = matrix_entries(first_key, (KERNEL, D)) / math.sqrt(KERNEL)
    gains = jax.random.uniform(second_key, (6, D), jnp.float32, 0.5, 1.5)
    return jnp.concatenate([taps, gains], axis=0)


def attn_levels():
    level = 0.5 * math.sqrt(SEQS * LEN)
    return jnp.array([1.0, 1.0, 1.0, 0.06], jnp.float32) * level


def draw_attn_moment(key, part):
    entries = jax.random.truncated_normal(key, -4.0, 4.0, (4, D, D), jnp.float32)
    return entries * (0.11 * attn_levels())[:, None, None]


def draw_attn_square(key, part):
    factor = jnp.exp(jax.random.uniform(key, (4, D, D), jnp.float32, 0.0, math.log(4.0)))
    levels = attn_levels()
    return factor * (0.001 * levels * levels)[:, None, None]


def shard_levels(key, extent, shards, low, largest):
    def one(position, shards_of):
        heights = jax.random.uniform(jax.random.fold_in(jax.random.fold_in(key, 6), position), (shards_of,), jnp.float32, low / len(shards), largest / len(shards))
        return jnp.repeat(jnp.exp(heights), extent[position] // shards_of).reshape((-1,) + (1,) * (len(extent) - position - 1))

    level = one(*shards[0])
    for cut in shards[1:]:
        level = level * one(*cut)
    return level


def normal_values(own_key, dims, spread, bound, cuts=(), kind=jnp.bfloat16):
    values = jax.random.normal(own_key, dims, jnp.float32) * spread
    if len(cuts) > 0:
        values = shard_levels(own_key, dims, cuts, -0.22, 0.18) * values
    return jnp.clip(values, min=-bound, max=bound).astype(kind)


def setup_inputs(seed: int = 0) -> dict:
    seeds = jax.random.split(jax.random.key(seed), 22)
    frames = normal_values(seeds[0], (SEQS, LEN, D), 1.0, 6.0, ((0, 32),))
    lengths = draw_lengths(jax.random.fold_in(seeds[21], 71), 0)
    cotangent = normal_values(seeds[2], (SEQS, LEN, D), 1.0, 6.0, ((0, 32),))
    ffn_in = normal_values(seeds[3], (2, D, FF), D ** -0.5, 0.25, ((1, 2),), jnp.float32)
    ffn_in_moment = normal_values(seeds[4], (2, D, FF), (0.0143 * (SEQS * LEN) ** 0.5), 10.0, ((1, 2),), jnp.float32)
    ffn_in_square = jnp.clip(jnp.exp(math.log(1.1075584) - 1.3862944 * jax.random.uniform(seeds[5], (2, D, FF), jnp.float32) ** shard_levels(seeds[5], (2, D, FF), ((1, 2),), -0.2, 0.2)), 0.2768896, 1.1075584)
    ffn_out = normal_values(seeds[6], (2, FF, D), (FF // 4) ** -0.5, 0.25, ((1, 2),), jnp.float32)
    ffn_out_moment = normal_values(seeds[7], (2, FF, D), (0.0143 * (SEQS * LEN) ** 0.5), 10.0, ((1, 2),), jnp.float32)
    ffn_out_square = jnp.clip(jnp.exp(math.log(1.1075584) - 1.3862944 * jax.random.uniform(seeds[8], (2, FF, D), jnp.float32) ** shard_levels(seeds[8], (2, FF, D), ((1, 2),), -0.2, 0.2)), 0.2768896, 1.1075584)
    attn_proj = draw_attn_proj(jax.random.fold_in(seeds[21], 71), 0)
    attn_moment = draw_attn_moment(jax.random.fold_in(seeds[21], 71), 0)
    attn_square = draw_attn_square(jax.random.fold_in(seeds[21], 71), 0)
    conv_proj = draw_conv_proj(jax.random.fold_in(seeds[21], 71), 0)
    conv_moment = normal_values(seeds[13], (D, 3 * D), (0.044 * (SEQS * LEN) ** 0.5), 32.0, ((0, 2),), jnp.float32)
    conv_square = jnp.clip(jnp.exp(math.log(10.48576) - 1.3862944 * jax.random.uniform(seeds[14], (D, 3 * D), jnp.float32) ** shard_levels(seeds[14], (D, 3 * D), ((0, 2),), -0.2, 0.2)), 2.62144, 10.48576)
    vectors = draw_vectors(jax.random.fold_in(seeds[21], 71), 0)
    vectors_moment = normal_values(seeds[16], (KERNEL + 6, D), (0.044 * (SEQS * LEN) ** 0.5), 32.0, ((1, 2),), jnp.float32)
    vectors_square = jnp.clip(jnp.exp(math.log(10.48576) - 1.3862944 * jax.random.uniform(seeds[17], (KERNEL + 6, D), jnp.float32) ** shard_levels(seeds[17], (KERNEL + 6, D), ((1, 2),), -0.2, 0.2)), 2.62144, 10.48576)
    rel_keys = normal_values(seeds[18], (RELS, HEAD), 1.0, 4.0, (), jnp.float32)
    rel_moment = normal_values(seeds[19], (RELS, HEAD), (0.055 * (SEQS * LEN) ** 0.5), 40.0, (), jnp.float32)
    rel_square = jnp.clip(jnp.exp(jax.random.uniform(seeds[20], (RELS, HEAD), jnp.float32, math.log(4.096), math.log(16.384))), 4.096, 16.384)
    return dict(frames=frames, lengths=lengths, cotangent=cotangent, ffn_in=ffn_in, ffn_in_moment=ffn_in_moment, ffn_in_square=ffn_in_square, ffn_out=ffn_out, ffn_out_moment=ffn_out_moment, ffn_out_square=ffn_out_square, attn_proj=attn_proj, attn_moment=attn_moment, attn_square=attn_square, conv_proj=conv_proj, conv_moment=conv_moment, conv_square=conv_square, vectors=vectors, vectors_moment=vectors_moment, vectors_square=vectors_square, rel_keys=rel_keys, rel_moment=rel_moment, rel_square=rel_square)


@jax.custom_vjp
def low(v):
    return lax.optimization_barrier(v.astype(jnp.bfloat16)).astype(jnp.float32)

@jax.custom_vjp
def low_back(v):
    return v

def low_keep(v):
    return (low(v), None)

def low_pass(kept, grad):
    return (grad,)

def back_keep(v):
    return (v, None)

def back_low(kept, grad):
    return (low(grad),)
low.defvjp(low_keep, low_pass)
low_back.defvjp(back_keep, back_low)
NORM_EPSILON = 1e-05
ADAM_EPSILON = 1e-06
RATIO_EPSILON = 1e-06
BETA_FIRST = 0.9
BETA_SECOND = 0.999
WEIGHT_DECAY = 0.01
LEARN_RATE = 0.5
MASKED_SCORE = -1e+30
HIGHEST = lax.Precision.HIGHEST

def matmul(left_side, right_side):
    return jnp.dot(left_side, right_side, precision=HIGHEST, preferred_element_type=jnp.float32)

def layer_norm(values, gain_row):
    centred = values - lax.optimization_barrier(jnp.mean(values, axis=-1, keepdims=True))
    return centred * lax.rsqrt(lax.optimization_barrier(jnp.mean(centred * centred, axis=-1, keepdims=True)) + NORM_EPSILON) * gain_row

def feed_forward(values, gain_row, weight_in, weight_out):
    entry_low = low(layer_norm(values, gain_row))
    hidden = low(jax.nn.silu(low_back(matmul(entry_low, weight_in))))
    return low_back(matmul(hidden, weight_out))

def attention(values, gain_row, attn_weights, rel_weights, length):
    row_count = values.shape[0]
    entry_low = low(layer_norm(values, gain_row))
    query_heads = low(low_back(matmul(entry_low, attn_weights[0]))).reshape(row_count, HEADS, HEAD)
    key_heads = low(low_back(matmul(entry_low, attn_weights[1]))).reshape(row_count, HEADS, HEAD)
    value_heads = low(low_back(matmul(entry_low, attn_weights[2]))).reshape(row_count, HEADS, HEAD)
    relative = low_back(jnp.einsum('ihe,re->hir', query_heads, rel_weights, precision=HIGHEST))
    positions = jnp.arange(row_count)
    places = jnp.clip(positions[None, :] - positions[:, None], -BACK, AHEAD) + BACK
    places = jnp.broadcast_to(places[None], (HEADS, row_count, row_count)).astype(jnp.int32)
    bias = jnp.take_along_axis(relative, places, axis=2)
    raw_scores = jnp.einsum('ihe,jhe->hij', query_heads, key_heads, precision=HIGHEST)
    scores = low_back((raw_scores + bias) * (1.0 / math.sqrt(HEAD)))
    valid = positions < length
    scores = jnp.where(valid[None, None, :], scores, MASKED_SCORE)
    prob_low = low(jax.nn.softmax(scores, axis=-1))
    mixed = jnp.einsum('hij,jhe->ihe', prob_low, value_heads, precision=HIGHEST)
    mixed_low = low(low_back(mixed)).reshape(row_count, HEADS * HEAD)
    return low_back(matmul(mixed_low, attn_weights[3]))

def convolve(values, gain_outer, gain_inner, depth_taps, conv_weights):
    row_count, feat_width = values.shape
    entry_low = low(layer_norm(values, gain_outer))
    both_halves = low_back(matmul(entry_low, conv_weights[:, :2 * feat_width]))
    gated = both_halves[:, :feat_width] * jax.nn.sigmoid(both_halves[:, feat_width:])
    padded = jnp.pad(gated, ((KERNEL - 1, 0), (0, 0)))
    conved = depth_taps[0] * padded[0:row_count]
    for offset in range(1, KERNEL):
        conved = conved + depth_taps[offset] * padded[offset:offset + row_count]
    act_low = low(jax.nn.silu(layer_norm(conved, gain_inner)))
    return low_back(matmul(act_low, conv_weights[:, 2 * feat_width:]))

def forward(frame_row, length, ffn_in, ffn_out, attn_proj, conv_proj, vectors, rel_keys):
    weight_in = low(ffn_in)
    weight_out = low(ffn_out)
    attn_weights = low(attn_proj)
    conv_weights = low(conv_proj)
    vec_full = low(vectors)
    rel_weights = low(rel_keys)
    depth_taps = vec_full[:KERNEL]
    gain_rows = vec_full[KERNEL:]
    after_ffn = frame_row + 0.5 * feed_forward(frame_row, gain_rows[0], weight_in[0], weight_out[0])
    after_attn = after_ffn + attention(after_ffn, gain_rows[1], attn_weights, rel_weights, length)
    after_conv = after_attn + convolve(after_attn, gain_rows[2], gain_rows[3], depth_taps, conv_weights)
    after_last = after_conv + 0.5 * feed_forward(after_conv, gain_rows[4], weight_in[1], weight_out[1])
    return layer_norm(after_last, gain_rows[5])

def adam_update(weight, moment, square, grad_sum):
    new_moment = BETA_FIRST * moment + (1.0 - BETA_FIRST) * grad_sum
    new_square = BETA_SECOND * square + (1.0 - BETA_SECOND) * grad_sum * grad_sum
    first_hat = new_moment / (1.0 - BETA_FIRST ** STEP)
    second_hat = new_square / (1.0 - BETA_SECOND ** STEP)
    update = first_hat / (jnp.sqrt(second_hat) + ADAM_EPSILON) + WEIGHT_DECAY * weight
    return (new_moment, new_square, update)

def unit_sums(ffn_in_part, ffn_out_part, attn_part, conv_part, vector_part):
    return jnp.concatenate([lax.optimization_barrier(jnp.sum(ffn_in_part * ffn_in_part, axis=(1, 2))), lax.optimization_barrier(jnp.sum(ffn_out_part * ffn_out_part, axis=(1, 2))), lax.optimization_barrier(jnp.sum(attn_part * attn_part, axis=(1, 2))), jnp.stack([jnp.sum(conv_part[:, :2 * D] * conv_part[:, :2 * D]), jnp.sum(conv_part[:, 2 * D:] * conv_part[:, 2 * D:])]), jnp.sum(vector_part[:KERNEL] * vector_part[:KERNEL])[None], lax.optimization_barrier(jnp.sum(vector_part[KERNEL:] * vector_part[KERNEL:], axis=1))])

def apply_ratios(masters, updates, ratios):
    conv_factor = jnp.where(jnp.arange(3 * D) < 2 * D, ratios[8], ratios[9])[None, :]
    vector_factor = jnp.concatenate([jnp.full((KERNEL,), ratios[10]), ratios[11:17]])[:, None]
    factors = (ratios[0:2][:, None, None], ratios[2:4][:, None, None], ratios[4:8][:, None, None], conv_factor, vector_factor)
    return tuple((weight - LEARN_RATE * factor * update for weight, factor, update in zip(masters, factors, updates)))

def reference(frames, lengths, cotangent, ffn_in, ffn_in_moment, ffn_in_square, ffn_out, ffn_out_moment, ffn_out_square, attn_proj, attn_moment, attn_square, conv_proj, conv_moment, conv_square, vectors, vectors_moment, vectors_square, rel_keys, rel_moment, rel_square):
    params = (ffn_in, ffn_out, attn_proj, conv_proj, vectors, rel_keys)
    positions = jnp.arange(LEN)

    def one_step(carry, item):
        frame_low, length, cot_row = item
        result, pullback = jax.vjp(lambda inputs, *weights: forward(inputs, length, *weights), frame_low.astype(jnp.float32), *params)
        valid = (positions < length)[:, None]
        pulled = pullback(jnp.where(valid, cot_row.astype(jnp.float32), 0.0))
        carry = tuple((total + part for total, part in zip(carry, pulled[1:])))
        return (carry, (result.astype(jnp.bfloat16), pulled[0].astype(jnp.bfloat16)))
    start_sums = tuple((jnp.zeros_like(param) for param in params))
    totals, (output, input_grad) = lax.scan(one_step, start_sums, (frames, lengths, cotangent))
    masters = (ffn_in, ffn_out, attn_proj, conv_proj, vectors)
    moments = (ffn_in_moment, ffn_out_moment, attn_moment, conv_moment, vectors_moment)
    squares = (ffn_in_square, ffn_out_square, attn_square, conv_square, vectors_square)
    states = [adam_update(weight, moment, square, grad_sum) for weight, moment, square, grad_sum in zip(masters, moments, squares, totals[:5])]
    updates = tuple((state[2] for state in states))
    weight_sums = unit_sums(masters[0], masters[1], masters[2], masters[3], masters[4])
    update_sums = unit_sums(updates[0], updates[1], updates[2], updates[3], updates[4])
    rel_moment_new, rel_square_new, rel_update = adam_update(rel_keys, rel_moment, rel_square, totals[5])
    all_sums = jnp.concatenate([jnp.stack([weight_sums, update_sums]), jnp.stack([jnp.sum(rel_keys * rel_keys), jnp.sum(rel_update * rel_update)])[:, None]], axis=1)
    trust_norms = jnp.sqrt(all_sums)
    ratios = trust_norms[0] / jnp.sqrt(all_sums[1] + RATIO_EPSILON)
    new_masters = apply_ratios(masters, updates, ratios)
    new_rel = rel_keys - LEARN_RATE * ratios[17] * rel_update
    return (output, input_grad, totals[0], new_masters[0], states[0][0], states[0][1], totals[1], new_masters[1], states[1][0], states[1][1], totals[2], new_masters[2], states[2][0], states[2][1][:3], states[2][1][3], totals[3], new_masters[3], states[3][0], states[3][1], totals[4], new_masters[4], states[4][0], states[4][1], totals[5], new_rel, rel_moment_new, rel_square_new, trust_norms)
```

```python
import math

import jax
import jax.numpy as jnp
from jax import lax
from jax.experimental import pallas as pl
from jax.experimental.pallas import tpu as pltpu
from jax.sharding import PartitionSpec as P

D = 512
FF = 2048
HEADS = 8
HEAD = 64
KERNEL = 31
BACK = 64
AHEAD = 8
RELS = 73
STEP = 10
PIECES = 32
LEAD = 32
FFN_ROWS = 128
ATTN_ROWS = 64
CONV_ROWS = 48

NORM_EPSILON = 1e-05
ADAM_EPSILON = 1e-06
RATIO_EPSILON = 1e-06
BETA_FIRST = 0.9
BETA_SECOND = 0.999
WEIGHT_DECAY = 0.01
LEARN_RATE = 0.5
MASKED_SCORE = -1e30

bf16 = jnp.bfloat16
f32 = jnp.float32
VMEM_LIMIT = 60 * 1024 * 1024


def vmem():
    return pl.BlockSpec(memory_space=pltpu.VMEM)


def smem():
    return pl.BlockSpec(memory_space=pltpu.SMEM)


def shape(dims, kind):
    return jax.ShapeDtypeStruct(dims, kind)


def dot(left, right):
    return jnp.dot(left, right, preferred_element_type=f32)


def dot_rows(left, right):
    return lax.dot_general(left, right, (((0,), (0,)), ((), ())), preferred_element_type=f32)


def dot_cols(left, right):
    return lax.dot_general(left, right, (((1,), (1,)), ((), ())), preferred_element_type=f32)


def stats(values):
    centred = values - jnp.mean(values, axis=-1, keepdims=True)
    scale = lax.rsqrt(jnp.mean(centred * centred, axis=-1, keepdims=True) + NORM_EPSILON)
    return centred * scale, scale


def norm_back(grad, normed, scale, gain):
    grad_gain = jnp.sum(grad * normed, axis=0, keepdims=True)
    scaled = grad * gain
    inner = jnp.mean(scaled * normed, axis=-1, keepdims=True)
    back = scale * (scaled - jnp.mean(scaled, axis=-1, keepdims=True) - normed * inner)
    return back, grad_gain


def logistic(values):
    return 1.0 / (1.0 + jnp.exp(-values))


def slope_of(values, sig):
    return sig * (1.0 + values * (1.0 - sig))


class Plan:
    def __init__(self, groups, shards):
        self.groups, self.shards = groups, shards
        shard_bits = shards.bit_length() - 1
        group_bits = groups.bit_length() - 1
        self.used = min(5 - shard_bits, group_bits)
        self.owned = PIECES // shards
        order = [("group", 0)] + [("shard", b) for b in range(shard_bits)]
        order += [("group", b) for b in range(1, self.used)]
        self.order = order
        self.rest = [("group", b) for b in range(self.used, group_bits)]
        self.shard_bits = [("shard", b) for b in range(shard_bits)]
        self.kept = [step for step in order if step[0] == "group"]

    def piece_bit(self, step):
        return step[1] if step[0] == "group" else self.used + step[1]

    def place(self, piece):
        out = 0
        for step in self.order:
            out = out * 2 + ((piece >> self.piece_bit(step)) & 1)
        return out

    def kept_place(self, piece):
        out = 0
        for step in self.kept:
            out = out * 2 + ((piece >> step[1]) & 1)
        return out


def swap(values, step):
    axis, bit = step
    count = lax.axis_size(axis)
    return lax.ppermute(values, axis, [(i, i ^ (1 << bit)) for i in range(count)])


def add_low(left, right):
    return (left.astype(f32) + right.astype(f32)).astype(bf16)


def sum_pieces(pieces, plan):
    for step in plan.order:
        half = pieces.shape[0] // 2
        pieces = add_low(pieces[:half], swap(pieces[half:], step))
    for step in plan.rest:
        pieces = add_low(pieces, swap(pieces, step))
    for step in reversed(plan.kept):
        pieces = jnp.concatenate([pieces, swap(pieces, step)], axis=0)
    return pieces


def sum_everywhere(values, plan):
    for step in plan.order + plan.rest:
        values = values + swap(values, step)
    return values


def sum_shards(values, plan):
    for step in plan.shard_bits:
        values = values + swap(values, step)
    return values


def fetch(own, dim, plan, core):
    low = own.astype(bf16)
    if plan.shards != 2:
        return (lax.all_gather(low, "shard", axis=dim, tiled=True),)
    half = own.shape[dim] // 2
    mine = lax.dynamic_slice_in_dim(own, core * half, half, axis=dim).astype(bf16)
    near = swap(mine, ("shard", 0))
    far = swap(near, ("group", 0))
    return (low, near, far)


def join(place_ref, part_refs, whole_ref):
    if len(part_refs) == 1:
        whole_ref[...] = part_refs[0][...]
        return
    own, near, far = part_refs
    rows = own.shape[-2]
    half = rows // 2
    shard, core = place_ref[0], place_ref[1]
    first = pl.multiple_of(shard * rows, half)
    second = pl.multiple_of((1 - shard) * rows + core * half, half)
    third = pl.multiple_of((1 - shard) * rows + (1 - core) * half, half)
    if len(own.shape) == 2:
        whole_ref[pl.ds(first, rows), :] = own[...]
        whole_ref[pl.ds(second, half), :] = near[...]
        whole_ref[pl.ds(third, half), :] = far[...]
    else:
        for k in range(own.shape[0]):
            whole_ref[k, pl.ds(first, rows), :] = own[k]
            whole_ref[k, pl.ds(second, half), :] = near[k]
            whole_ref[k, pl.ds(third, half), :] = far[k]


def put(out_ref, plan, mine, value, row, rows_each, first):
    low = value.astype(bf16)
    for k in range(value.shape[0] // rows_each):
        spot = jnp.bitwise_xor(jnp.int32(plan.place(first + k)), mine)
        out_ref[spot, row : row + rows_each, :] = low[k * rows_each : (k + 1) * rows_each]


def call(kernel, outs, ins, specs=None, scratch=(), name=None, flops=0, nbytes=0, aliases=None):
    if specs is None:
        specs = [vmem()] * len(ins)
    cost = pl.CostEstimate(flops=int(flops), transcendentals=0, bytes_accessed=int(nbytes))
    return pl.pallas_call(
        kernel,
        out_shape=outs,
        in_specs=specs,
        out_specs=[vmem() for _ in outs],
        scratch_shapes=list(scratch),
        compiler_params=pltpu.CompilerParams(vmem_limit_bytes=VMEM_LIMIT),
        cost_estimate=cost,
        name=name,
    )(*ins)


def ffn_ahead(values, gain, win, wout, entry_ref, hidden_ref, slope_ref):
    normed, _ = stats(values)
    entry = (normed * gain).astype(bf16)
    entry_ref[...] = entry
    total = jnp.zeros(values.shape, f32)
    for b in range(FF // D):
        cols = slice(b * D, (b + 1) * D)
        before = dot(entry, win[:, cols])
        sig = logistic(before)
        hidden = (before * sig).astype(bf16)
        hidden_ref[:, cols] = hidden
        slope_ref[:, cols] = slope_of(before, sig).astype(bf16)
        total = total + dot(hidden, wout[cols, :])
    return total


def ffn_behind(grad, values, gain, win, wout, entry_ref, hidden_ref, slope_ref, out_ref, plan, mine):
    normed, scale = stats(values)
    entry = entry_ref[...]
    branch = (0.5 * grad).astype(bf16)
    grad_entry = jnp.zeros(values.shape, f32)
    for b in range(FF // D):
        cols = slice(b * D, (b + 1) * D)
        put(out_ref, plan, mine, dot_rows(hidden_ref[:, cols], branch), 64, 64, 8 * b)
        grad_before = (dot_cols(branch, wout[cols, :]) * slope_ref[:, cols].astype(f32)).astype(bf16)
        put(out_ref, plan, mine, dot_rows(entry, grad_before), 16 * b, 16, 0)
        grad_entry = grad_entry + dot_cols(grad_before, win[:, cols])
    back, grad_gain = norm_back(grad_entry, normed, scale, gain)
    return grad + back, grad_gain


def ffn_first(frames, vec, win_parts, wout_parts, place, plan):
    rows = frames.shape[0]
    n = len(win_parts)

    def kernel(place_ref, x_ref, vec_ref, *rest):
        wins, wouts = rest[:n], rest[n : 2 * n]
        out_ref, entry_ref, hidden_ref, slope_ref, win, wout = rest[2 * n :]
        join(place_ref, wins, win)
        join(place_ref, wouts, wout)
        values = x_ref[...].astype(f32)
        total = ffn_ahead(values, vec_ref[31:32, :], win, wout, entry_ref, hidden_ref, slope_ref)
        out_ref[...] = values + 0.5 * total

    return call(
        kernel,
        [shape((rows, D), f32), shape((rows, D), bf16), shape((rows, FF), bf16), shape((rows, FF), bf16)],
        [place, frames, vec, *win_parts, *wout_parts],
        [smem()] + [vmem()] * (2 + 2 * n),
        [pltpu.VMEM((D, FF), bf16), pltpu.VMEM((FF, D), bf16)],
        "ffn_first",
        4 * rows * D * FF,
        12e6,
    )


def ffn_last(values, vec, cotangent, lengths, win_parts, wout_parts, place, plan):
    rows = values.shape[0]
    count = lengths.shape[0]
    n = len(win_parts)

    def kernel(place_ref, len_ref, x_ref, vec_ref, cot_ref, *rest):
        wins, wouts = rest[:n], rest[n : 2 * n]
        y_ref, dx_ref, gain_ref, g_ref, win, wout, entry_ref, hidden_ref, slope_ref = rest[2 * n :]
        join(place_ref, wins, win)
        join(place_ref, wouts, wout)
        x = x_ref[...]
        gain = vec_ref[35:36, :]
        total = ffn_ahead(x, gain, win, wout, entry_ref, hidden_ref, slope_ref)
        normed, scale = stats(x + 0.5 * total)
        top = vec_ref[36:37, :]
        y_ref[...] = (normed * top).astype(bf16)
        each = rows // count
        grads = []
        for s in range(count):
            spot = lax.broadcasted_iota(jnp.int32, (each, 1), 0)
            part = cot_ref[s * each : (s + 1) * each, :].astype(f32)
            grads.append(jnp.where(spot < len_ref[s], part, 0.0))
        back, grad_top = norm_back(jnp.concatenate(grads, axis=0), normed, scale, top)
        grad, grad_gain = ffn_behind(
            back, x, gain, win, wout, entry_ref, hidden_ref, slope_ref, g_ref, plan, place_ref[2]
        )
        dx_ref[...] = grad
        gain_ref[...] = jnp.concatenate([grad_gain, grad_top, jnp.zeros((6, D), f32)], axis=0)

    return call(
        kernel,
        [shape((rows, D), bf16), shape((rows, D), f32), shape((8, D), f32), shape((PIECES, FFN_ROWS, D), bf16)],
        [place, lengths, values, vec, cotangent, *win_parts, *wout_parts],
        [smem(), smem()] + [vmem()] * (3 + 2 * n),
        [
            pltpu.VMEM((D, FF), bf16),
            pltpu.VMEM((FF, D), bf16),
            pltpu.VMEM((rows, D), bf16),
            pltpu.VMEM((rows, FF), bf16),
            pltpu.VMEM((rows, FF), bf16),
        ],
        "ffn_last",
        12 * rows * D * FF,
        16e6,
    )


def ffn_first_back(grad, frames, vec, kept, win_parts, wout_parts, place, plan):
    rows = frames.shape[0]
    n = len(win_parts)
    entry, hidden, slope = kept

    def kernel(place_ref, grad_ref, x_ref, vec_ref, entry_ref, hidden_ref, slope_ref, *rest):
        wins, wouts = rest[:n], rest[n : 2 * n]
        dx_ref, gain_ref, g_ref, win, wout = rest[2 * n :]
        join(place_ref, wins, win)
        join(place_ref, wouts, wout)
        back, grad_gain = ffn_behind(
            grad_ref[...],
            x_ref[...].astype(f32),
            vec_ref[31:32, :],
            win,
            wout,
            entry_ref,
            hidden_ref,
            slope_ref,
            g_ref,
            plan,
            place_ref[2],
        )
        dx_ref[...] = back.astype(bf16)
        gain_ref[...] = jnp.concatenate([grad_gain, jnp.zeros((7, D), f32)], axis=0)

    return call(
        kernel,
        [shape((rows, D), bf16), shape((8, D), f32), shape((PIECES, FFN_ROWS, D), bf16)],
        [place, grad, frames, vec, entry, hidden, slope, *win_parts, *wout_parts],
        [smem()] + [vmem()] * (6 + 2 * n),
        [pltpu.VMEM((D, FF), bf16), pltpu.VMEM((FF, D), bf16)],
        "ffn_first_back",
        8 * rows * D * FF,
        16e6,
    )


def attend(values, vec, rel_table, lengths, parts, place, plan):
    rows = values.shape[0]
    count = lengths.shape[0]
    each = rows // count
    n = len(parts)
    pairs = HEADS // 2

    def kernel(place_ref, len_ref, x_ref, vec_ref, rel_ref, *rest):
        ws = rest[:n]
        out_ref, entry_ref, qkv_ref, prob_ref, mix_ref, weight, mixed = rest[n:]
        join(place_ref, ws, weight)
        x = x_ref[...]
        normed, _ = stats(x)
        entry = (normed * vec_ref[32:33, :]).astype(bf16)
        entry_ref[...] = entry
        for k in range(3):
            heads = dot(entry, weight[k]).astype(bf16)
            for p in range(pairs):
                qkv_ref[k, p] = heads[:, p * 128 : (p + 1) * 128]
        lane = lax.broadcasted_iota(jnp.int32, (1, 128), 1)
        table = rel_ref[...]
        spot = lax.broadcasted_iota(jnp.int32, (1, each), 1)

        def step(i, carry):
            s = i // pairs
            p = i % pairs
            span = pl.ds(pl.multiple_of(s * each, each), each)
            query = qkv_ref[0, p, span, :]
            keys = qkv_ref[1, p, span, :]
            vals = qkv_ref[2, p, span, :]
            valid = spot < len_ref[s]
            both = []
            for h in range(2):
                mask = (lane < HEAD) if h == 0 else (lane >= HEAD)
                mine = jnp.where(mask, query, jnp.zeros_like(query))
                raw = dot_cols(mine, keys)
                skew = pltpu.roll(dot_cols(mine, table), 0, 1, stride=1, stride_axis=0)[:, :each]
                scores = jnp.where(valid, (raw + skew) * 0.125, MASKED_SCORE)
                grown = jnp.exp(scores - jnp.max(scores, axis=-1, keepdims=True))
                low = (grown * (1.0 / jnp.sum(grown, axis=-1, keepdims=True))).astype(bf16)
                prob_ref[2 * i + h] = low
                both.append(dot(low, vals))
            mixed[p, span, :] = jnp.where(lane < HEAD, both[0], both[1]).astype(bf16)
            return carry

        lax.fori_loop(0, count * pairs, step, 0)
        mix = jnp.concatenate([mixed[p] for p in range(pairs)], axis=1)
        mix_ref[...] = mix
        out_ref[...] = x + dot(mix, weight[3])

    return call(
        kernel,
        [
            shape((rows, D), f32),
            shape((rows, D), bf16),
            shape((3, pairs, rows, 128), bf16),
            shape((count * HEADS, each, each), bf16),
            shape((rows, D), bf16),
        ],
        [place, lengths, values, vec, rel_table, *parts],
        [smem(), smem()] + [vmem()] * (3 + n),
        [pltpu.VMEM((4, D, D), bf16), pltpu.VMEM((pairs, rows, 128), bf16)],
        "attend",
        16 * rows * D * D,
        20e6,
    )


def attend_back(grad, values, vec, kept, rel_table, parts, place, plan, count):
    rows = values.shape[0]
    each = rows // count
    n = len(parts)
    pairs = HEADS // 2
    entry, qkv, prob, mix = kept
    width = rel_table.shape[0]

    def kernel(place_ref, grad_ref, x_ref, vec_ref, entry_ref, qkv_ref, prob_ref, mix_ref, rel_ref, *rest):
        ws = rest[:n]
        dx_ref, gain_ref, rel_out, g_ref, weight, dmix, dqkv = rest[n:]
        mine_spot = place_ref[2]
        join(place_ref, ws, weight)
        down = grad_ref[...]
        low = down.astype(bf16)
        put(g_ref, plan, mine_spot, dot_rows(mix_ref[...], low), 48, 16, 0)
        spread = dot_cols(low, weight[3]).astype(bf16)
        for p in range(pairs):
            dmix[p] = spread[:, p * 128 : (p + 1) * 128]
        lane = lax.broadcasted_iota(jnp.int32, (1, 128), 1)
        table = rel_ref[...]
        flip = (
            lax.broadcasted_iota(jnp.int32, (each, each), 0)
            + lax.broadcasted_iota(jnp.int32, (each, each), 1)
            == each - 1
        ).astype(bf16)
        rel_out[...] = jnp.zeros_like(rel_out)

        def step(i, carry):
            s = i // pairs
            p = i % pairs
            span = pl.ds(pl.multiple_of(s * each, each), each)
            query = qkv_ref[0, p, span, :]
            keys = qkv_ref[1, p, span, :]
            vals = qkv_ref[2, p, span, :]
            outer = dmix[p, span, :]
            grad_q = jnp.zeros((each, 128), f32)
            grad_k = jnp.zeros((each, 128), f32)
            grad_v = jnp.zeros((each, 128), f32)
            grad_r = jnp.zeros((width, 128), f32)
            for h in range(2):
                mask = (lane < HEAD) if h == 0 else (lane >= HEAD)

                def pick(v):
                    return jnp.where(mask, v, jnp.zeros_like(v))

                dout = pick(outer)
                q_own = pick(query)
                prob_low = prob_ref[2 * i + h]
                prob_wide = prob_low.astype(f32)
                dprob = dot_cols(dout, vals)
                inner = jnp.sum(prob_wide * dprob, axis=-1, keepdims=True)
                dscore = (prob_wide * (dprob - inner)).astype(bf16)
                grad_v = grad_v + dot_rows(prob_low, dout)
                grad_k = grad_k + dot_rows(dscore, q_own)
                turned = dot(flip, dscore)
                wide = jnp.concatenate([turned, jnp.zeros((each, width - each), f32)], axis=1)
                skew = pltpu.roll(wide, width - each + 1, 1, stride=1, stride_axis=0).astype(bf16)
                along = dot(flip, skew).astype(bf16)
                grad_q = grad_q + dot(dscore, pick(keys)) + dot(along, pick(table))
                grad_r = grad_r + dot_rows(along, q_own)
            dqkv[0, p, span, :] = (grad_q * 0.125).astype(bf16)
            dqkv[1, p, span, :] = (grad_k * 0.125).astype(bf16)
            dqkv[2, p, span, :] = grad_v.astype(bf16)
            rel_out[...] += grad_r * 0.125
            return carry

        lax.fori_loop(0, count * pairs, step, 0)
        entry_low = entry_ref[...]
        grad_entry = jnp.zeros((rows, D), f32)
        for k in range(3):
            heads = jnp.concatenate([dqkv[k, p] for p in range(pairs)], axis=1)
            put(g_ref, plan, mine_spot, dot_rows(entry_low, heads), 16 * k, 16, 0)
            grad_entry = grad_entry + dot_cols(heads, weight[k])
        normed, scale = stats(x_ref[...])
        back, grad_gain = norm_back(grad_entry, normed, scale, vec_ref[32:33, :])
        dx_ref[...] = down + back
        gain_ref[...] = jnp.concatenate([grad_gain, jnp.zeros((7, D), f32)], axis=0)

    return call(
        kernel,
        [
            shape((rows, D), f32),
            shape((8, D), f32),
            shape((width, 128), f32),
            shape((PIECES, ATTN_ROWS, D), bf16),
        ],
        [place, grad, values, vec, entry, qkv, prob, mix, rel_table, *parts],
        [smem()] + [vmem()] * (8 + n),
        [
            pltpu.VMEM((4, D, D), bf16),
            pltpu.VMEM((pairs, rows, 128), bf16),
            pltpu.VMEM((3, pairs, rows, 128), bf16),
        ],
        "attend_back",
        50 * rows * D * D,
        24e6,
    )


def convolve(values, vec, parts, place, plan, count):
    rows = values.shape[0]
    each = rows // count
    n = len(parts)
    cols = D // 128
    chunk = 64

    def kernel(place_ref, x_ref, vec_ref, *rest):
        ws = rest[:n]
        out_ref, entry_ref, gated_ref, sig_ref, conv_ref, act_ref, weight = rest[n:]
        join(place_ref, ws, weight)
        x = x_ref[...]
        normed, _ = stats(x)
        entry = (normed * vec_ref[33:34, :]).astype(bf16)
        entry_ref[...] = entry
        linear = dot(entry, weight[:, :D])
        sig = logistic(dot(entry, weight[:, D : 2 * D]))
        sig_ref[...] = sig
        gated = linear * sig
        for s in range(count):
            for c in range(cols):
                gated_ref[s, c, :LEAD, :] = jnp.zeros((LEAD, 128), f32)
                gated_ref[s, c, LEAD:, :] = gated[s * each : (s + 1) * each, c * 128 : (c + 1) * 128]
        for c in range(cols):
            taps = vec_ref[0:32, c * 128 : (c + 1) * 128]

            def step(i, carry):
                s = i // (each // chunk)
                t = (i % (each // chunk)) * chunk
                total = jnp.zeros((chunk, 128), f32)
                for k in range(KERNEL):
                    total = total + taps[k : k + 1] * gated_ref[s, c, pl.ds(t + k + LEAD - KERNEL + 1, chunk), :]
                conv_ref[pl.ds(pl.multiple_of(i * chunk, chunk), chunk), c * 128 : (c + 1) * 128] = total
                return carry

            lax.fori_loop(0, rows // chunk, step, 0)
        inner, _ = stats(conv_ref[...])
        act = inner * vec_ref[34:35, :]
        low = (act * logistic(act)).astype(bf16)
        act_ref[...] = low
        out_ref[...] = x + dot(low, weight[:, 2 * D :])

    return call(
        kernel,
        [
            shape((rows, D), f32),
            shape((rows, D), bf16),
            shape((count, cols, each + LEAD, 128), f32),
            shape((rows, D), f32),
            shape((rows, D), f32),
            shape((rows, D), bf16),
        ],
        [place, values, vec, *parts],
        [smem()] + [vmem()] * (2 + n),
        [pltpu.VMEM((D, 3 * D), bf16)],
        "convolve",
        12 * rows * D * D,
        16e6,
    )


def convolve_back(grad, values, vec, kept, parts, place, plan, count):
    rows = values.shape[0]
    each = rows // count
    n = len(parts)
    cols = D // 128
    entry, gated, sig, conved, act = kept

    def kernel(place_ref, grad_ref, x_ref, vec_ref, entry_ref, gated_ref, sig_ref, conv_ref, act_ref, *rest):
        ws = rest[:n]
        dx_ref, gain_ref, taps_out, g_ref, weight, dconv, dgated = rest[n:]
        mine = place_ref[1 + 1]
        join(place_ref, ws, weight)
        down = grad_ref[...]
        low = down.astype(bf16)
        put(g_ref, plan, mine, dot_rows(act_ref[...], low), 32, 16, 0)
        inner, inner_scale = stats(conv_ref[...])
        inner_gain = vec_ref[34:35, :]
        act_in = inner * inner_gain
        grad_act = dot_cols(low, weight[:, 2 * D :]) * slope_of(act_in, logistic(act_in))
        grad_conv, gain_inner = norm_back(grad_act, inner, inner_scale, inner_gain)
        for s in range(count):
            for c in range(cols):
                dconv[s, c, :each, :] = grad_conv[s * each : (s + 1) * each, c * 128 : (c + 1) * 128]
                dconv[s, c, each:, :] = jnp.zeros((LEAD, 128), f32)
        for c in range(cols):
            lanes = slice(c * 128, (c + 1) * 128)
            taps = vec_ref[0:32, lanes]

            def step(i, sums):
                s = i // (each // 8)
                t = (i % (each // 8)) * 8
                here = dconv[s, c, pl.ds(pl.multiple_of(t, 8), 8), :]
                total = jnp.zeros((8, 128), f32)
                new = []
                for k in range(KERNEL):
                    new.append(sums[k] + here * gated_ref[s, c, pl.ds(t + k + LEAD - KERNEL + 1, 8), :])
                    total = total + taps[k : k + 1] * dconv[s, c, pl.ds(t + KERNEL - 1 - k, 8), :]
                dgated[pl.ds(pl.multiple_of(i * 8, 8), 8), lanes] = total
                return tuple(new)

            sums = lax.fori_loop(0, rows // 8, step, tuple(jnp.zeros((8, 128), f32) for _ in range(KERNEL)))
            found = [jnp.sum(v, axis=0, keepdims=True) for v in sums]
            taps_out[:, lanes] = jnp.concatenate(found + [jnp.zeros((1, 128), f32)], axis=0)
        grad_gated = dgated[...]
        sig_wide = sig_ref[...]
        linear_sig = jnp.concatenate(
            [
                jnp.concatenate([gated_ref[s, c, LEAD:, :] for c in range(cols)], axis=1)
                for s in range(count)
            ],
            axis=0,
        )
        grad_one = (grad_gated * sig_wide).astype(bf16)
        grad_two = (grad_gated * linear_sig * (1.0 - sig_wide)).astype(bf16)
        entry_low = entry_ref[...]
        put(g_ref, plan, mine, dot_rows(entry_low, grad_one), 0, 16, 0)
        put(g_ref, plan, mine, dot_rows(entry_low, grad_two), 16, 16, 0)
        grad_entry = dot_cols(grad_one, weight[:, :D]) + dot_cols(grad_two, weight[:, D : 2 * D])
        normed, scale = stats(x_ref[...])
        back, gain_outer = norm_back(grad_entry, normed, scale, vec_ref[33:34, :])
        dx_ref[...] = down + back
        gain_ref[...] = jnp.concatenate([gain_outer, gain_inner, jnp.zeros((6, D), f32)], axis=0)

    return call(
        kernel,
        [
            shape((rows, D), f32),
            shape((8, D), f32),
            shape((32, D), f32),
            shape((PIECES, CONV_ROWS, D), bf16),
        ],
        [place, grad, values, vec, entry, gated, sig, conved, act, *parts],
        [smem()] + [vmem()] * (8 + n),
        [
            pltpu.VMEM((D, 3 * D), bf16),
            pltpu.VMEM((count, cols, each + LEAD, 128), f32),
            pltpu.VMEM((rows, D), f32),
        ],
        "convolve_back",
        40 * rows * D * D,
        20e6,
    )


def adam(weight, moment, square, grad):
    new_moment = BETA_FIRST * moment + (1.0 - BETA_FIRST) * grad
    new_square = BETA_SECOND * square + (1.0 - BETA_SECOND) * grad * grad
    first = new_moment * (1.0 / (1.0 - BETA_FIRST**STEP))
    second = new_square * (1.0 / (1.0 - BETA_SECOND**STEP))
    update = first / (jnp.sqrt(second) + ADAM_EPSILON) + WEIGHT_DECAY * weight
    return new_moment, new_square, update


def folded(values):
    squares = jnp.sum((values * values).reshape(-1, values.shape[-1]), axis=0, keepdims=True)
    total = squares[:, :128]
    for c in range(1, values.shape[-1] // 128):
        total = total + squares[:, c * 128 : (c + 1) * 128]
    return total


def update_ffn(layer, pieces, spots, states, given):
    count = pieces.shape[0]
    win, wout = states[0], states[3]
    in_rows, out_rows = win.shape[1] // count, wout.shape[1] // count
    outs = [win.shape] * 4 + [wout.shape] * 4
    if given is None:
        given = ()

    def kernel(spot_ref, g_ref, w0, m0, q0, w1, m1, q1, *rest):
        g0_out, u0_out, m0_out, q0_out, g1_out, u1_out, m1_out, q1_out, sums = rest[len(given) :]
        index = pl.program_id(0)

        @pl.when(index == 0)
        def _():
            sums[...] = jnp.zeros_like(sums)

        raw = g_ref[0].astype(f32)
        rows = []
        wide = jnp.concatenate([raw[k * 16 : k * 16 + 16] for k in range(FF // D)], axis=1)
        for weight, moment, square, grad, g_out, u_out, m_out, q_out in (
            (w0[0], m0[0], q0[0], wide, g0_out, u0_out, m0_out, q0_out),
            (w1[0], m1[0], q1[0], raw[64:128], g1_out, u1_out, m1_out, q1_out),
        ):
            new_moment, new_square, update = adam(weight, moment, square, grad)
            g_out[0] = grad
            u_out[0] = update
            m_out[0] = new_moment
            q_out[0] = new_square
            rows += [folded(weight), folded(update)]
        sums[...] += jnp.concatenate(rows + [jnp.zeros((4, 128), f32)], axis=0)

    def at_in(p, spot):
        return (layer, p, 0)

    in_block = pl.BlockSpec((1, in_rows, FF), at_in)
    out_block = pl.BlockSpec((1, out_rows, D), at_in)
    return pl.pallas_call(
        kernel,
        out_shape=[shape(dims, f32) for dims in outs] + [shape((8, 128), f32)],
        grid_spec=pltpu.PrefetchScalarGridSpec(
            num_scalar_prefetch=1,
            grid=(count,),
            in_specs=[pl.BlockSpec((1, FFN_ROWS, D), lambda p, spot: (spot[p], 0, 0))]
            + [in_block] * 3
            + [out_block] * 3
            + [pl.BlockSpec(memory_space=pl.ANY)] * len(given),
            out_specs=[in_block] * 4 + [out_block] * 4 + [pl.BlockSpec((8, 128), lambda p, spot: (0, 0))],
        ),
        input_output_aliases={8 + k: k for k in range(len(given))},
        compiler_params=pltpu.CompilerParams(vmem_limit_bytes=VMEM_LIMIT),
        cost_estimate=pl.CostEstimate(flops=0, transcendentals=0, bytes_accessed=32000000),
        name="update_ffn",
    )(spots, pieces, *states, *given)


def update_rest(attn_pieces, conv_pieces, spots, attn, conv):
    count = attn_pieces.shape[0]
    rows = attn[0].shape[1] // count

    def kernel(spot_ref, ga_ref, gc_ref, wa, ma, qa, wc, mc, qc, *outs):
        ga_out, ua_out, ma_out, qa_out, qo_out, gc_out, uc_out, mc_out, qc_out, sums = outs
        index = pl.program_id(0)

        @pl.when(index == 0)
        def _():
            sums[...] = jnp.zeros_like(sums)

        found = []
        for k in range(4):
            grad = ga_ref[0, k * 16 : (k + 1) * 16].astype(f32)
            weight = wa[k]
            new_moment, new_square, update = adam(weight, ma[k], qa[k], grad)
            ga_out[k] = grad
            ua_out[k] = update
            ma_out[k] = new_moment
            if k < 3:
                qa_out[k] = new_square
            else:
                qo_out[...] = new_square
            found += [folded(weight), folded(update)]
        for low, high in ((0, 2), (2, 3)):
            lanes = slice(low * D, high * D)
            grad = jnp.concatenate([gc_ref[0, k * 16 : (k + 1) * 16] for k in range(low, high)], axis=1)
            grad = grad.astype(f32)
            weight = wc[:, lanes]
            new_moment, new_square, update = adam(weight, mc[:, lanes], qc[:, lanes], grad)
            gc_out[:, lanes] = grad
            uc_out[:, lanes] = update
            mc_out[:, lanes] = new_moment
            qc_out[:, lanes] = new_square
            found += [folded(weight), folded(update)]
        sums[...] += jnp.concatenate(found + [jnp.zeros((4, 128), f32)], axis=0)

    attn_block = pl.BlockSpec((4, rows, D), lambda p, spot: (0, p, 0))
    conv_block = pl.BlockSpec((rows, 3 * D), lambda p, spot: (p, 0))
    three = pl.BlockSpec((3, rows, D), lambda p, spot: (0, p, 0))
    one = pl.BlockSpec((rows, D), lambda p, spot: (p, 0))
    side = attn[0].shape[1]
    return pl.pallas_call(
        kernel,
        out_shape=[shape(attn[0].shape, f32)] * 3
        + [shape((3, side, D), f32), shape((side, D), f32)]
        + [shape(conv[0].shape, f32)] * 4
        + [shape((16, 128), f32)],
        grid_spec=pltpu.PrefetchScalarGridSpec(
            num_scalar_prefetch=1,
            grid=(count,),
            in_specs=[
                pl.BlockSpec((1, ATTN_ROWS, D), lambda p, spot: (spot[p], 0, 0)),
                pl.BlockSpec((1, CONV_ROWS, D), lambda p, spot: (spot[p], 0, 0)),
            ]
            + [attn_block] * 3
            + [conv_block] * 3,
            out_specs=[attn_block] * 3
            + [three, one]
            + [conv_block] * 4
            + [pl.BlockSpec((16, 128), lambda p, spot: (0, 0))],
        ),
        compiler_params=pltpu.CompilerParams(vmem_limit_bytes=VMEM_LIMIT),
        cost_estimate=pl.CostEstimate(flops=0, transcendentals=0, bytes_accessed=28000000),
        name="update_rest",
    )(spots, attn_pieces, conv_pieces, *attn, *conv)


def move(weight, update, factor):
    return weight - LEARN_RATE * factor * update


def ratio_of(sums):
    weight, update = sums[0::2], sums[1::2]
    return jnp.sqrt(weight), jnp.sqrt(update), jnp.sqrt(weight) / jnp.sqrt(update + RATIO_EPSILON)


def body(
    frames,
    lengths,
    cotangent,
    ffn_in,
    ffn_in_moment,
    ffn_in_square,
    ffn_out,
    ffn_out_moment,
    ffn_out_square,
    attn_proj,
    attn_moment,
    attn_square,
    conv_proj,
    conv_moment,
    conv_square,
    vectors,
    vectors_moment,
    vectors_square,
    rel_keys,
    rel_moment,
    rel_square,
):
    groups, shards = lax.axis_size("group"), lax.axis_size("shard")
    plan = Plan(groups, shards)
    group, shard = lax.axis_index("group"), lax.axis_index("shard")
    core = jnp.bitwise_and(group, 1)
    count, each, _ = frames.shape
    mine = jnp.int32(0)
    for step in plan.order:
        bit = jnp.right_shift(group if step[0] == "group" else shard, step[1]) & 1
        mine = mine * 2 + bit
    kept = jnp.int32(0)
    for step in plan.kept:
        kept = kept * 2 + (jnp.right_shift(group, step[1]) & 1)
    spots = jnp.array([plan.kept_place(p) for p in range(plan.owned)], jnp.int32) ^ kept
    place = jnp.stack([shard, core, mine]).astype(jnp.int32)

    win0 = fetch(ffn_in[0], 0, plan, core)
    wout0 = fetch(ffn_out[0], 0, plan, core)
    vec = lax.all_gather(vectors.astype(bf16), "shard", axis=1, tiled=True) if shards != 2 else None
    if vec is None:
        low = vectors.astype(bf16)
        other = swap(low, ("shard", 0))
        vec = jnp.where(shard == 0, jnp.concatenate([low, other], 1), jnp.concatenate([other, low], 1))
    vec = jnp.concatenate([vec.astype(f32), jnp.zeros((3, D), f32)], axis=0)
    watt = fetch(attn_proj, 1, plan, core)
    wconv = fetch(conv_proj, 0, plan, core)
    win1 = fetch(ffn_in[1], 0, plan, core)
    wout1 = fetch(ffn_out[1], 0, plan, core)

    rel_low = rel_keys.astype(bf16)
    table = jnp.concatenate(
        [
            rel_low[BACK:],
            jnp.broadcast_to(rel_low[RELS - 1 :], (each - AHEAD - 1, HEAD)),
            jnp.broadcast_to(rel_low[:1], (each - BACK, HEAD)),
            rel_low[:BACK],
        ],
        axis=0,
    )
    table = jnp.concatenate([table, table], axis=1)

    flat = frames.reshape(count * each, D)
    x1, *kept_ffn = ffn_first(flat, vec, win0, wout0, place, plan)
    x2, *kept_attn = attend(x1, vec, table, lengths, watt, place, plan)
    x3, *kept_conv = convolve(x2, vec, wconv, place, plan, count)
    output, d3, gains_last, pieces_last = ffn_last(
        x3, vec, cotangent.reshape(count * each, D), lengths, win1, wout1, place, plan
    )
    owned_last = sum_pieces(pieces_last, plan)
    d2, gains_conv, taps, pieces_conv = convolve_back(d3, x2, vec, kept_conv, wconv, place, plan, count)
    owned_conv = sum_pieces(pieces_conv, plan)
    d1, gains_attn, rel_wide, pieces_attn = attend_back(d2, x1, vec, kept_attn, table, watt, place, plan, count)
    owned_attn = sum_pieces(pieces_attn, plan)
    d0, gains_first, pieces_first = ffn_first_back(d1, flat, vec, kept_ffn, win0, wout0, place, plan)
    owned_first = sum_pieces(pieces_first, plan)

    rel_half = rel_wide[:, :HEAD] + rel_wide[:, HEAD:]
    edge = 2 * each - BACK
    rel_local = jnp.concatenate(
        [
            jnp.sum(rel_half[each : edge + 1], axis=0, keepdims=True),
            rel_half[edge + 1 :],
            rel_half[:AHEAD],
            jnp.sum(rel_half[AHEAD:each], axis=0, keepdims=True),
        ],
        axis=0,
    )
    vec_local = jnp.concatenate(
        [taps[:KERNEL], gains_first[:1], gains_attn[:1], gains_conv[:2], gains_last[:2]], axis=0
    )
    rel_lines = jnp.pad(rel_local.reshape(-1), (0, 10 * D - RELS * HEAD)).reshape(10, D)
    small = sum_everywhere(jnp.concatenate([vec_local, rel_lines, jnp.zeros((1, D), f32)], axis=0), plan)
    wide = vectors.shape[1]
    vec_grad = lax.dynamic_slice(small, (0, shard * wide), (KERNEL + 6, wide))
    rel_grad = small[KERNEL + 6 : KERNEL + 16].reshape(-1)[: RELS * HEAD].reshape(RELS, HEAD)

    states = (ffn_in, ffn_in_moment, ffn_in_square, ffn_out, ffn_out_moment, ffn_out_square)
    *half_ffn, sums_last = update_ffn(1, owned_last, spots, states, None)
    (attn_grad, attn_up, attn_m, attn_q, attn_qo, conv_grad, conv_up, conv_m, conv_q, sums_rest) = update_rest(
        owned_attn,
        owned_conv,
        spots,
        (attn_proj, attn_moment, attn_square),
        (conv_proj, conv_moment, conv_square),
    )
    *full_ffn, sums_first = update_ffn(0, owned_first, spots, states, half_ffn)
    in_grad, in_up, in_m, in_q, out_grad, out_up, out_m, out_q = full_ffn
    vec_m, vec_q, vec_up = adam(vectors, vectors_moment, vectors_square, vec_grad)
    rel_m, rel_q, rel_up = adam(rel_keys, rel_moment, rel_square, rel_grad)

    vec_sums = []
    for part in (vectors, vec_up):
        squares = jnp.sum(part * part, axis=1)
        vec_sums.append(jnp.concatenate([jnp.sum(squares[:KERNEL])[None], squares[KERNEL:]]))
    early = sum_shards(jnp.sum(jnp.concatenate([sums_last, sums_rest], axis=0), axis=1), plan)
    late = sum_shards(
        jnp.concatenate([jnp.sum(sums_first[:4], axis=1), jnp.stack(vec_sums, axis=1).reshape(-1)]), plan
    )
    rel_sums = jnp.stack([jnp.sum(rel_keys * rel_keys), jnp.sum(rel_up * rel_up)])
    sums = jnp.concatenate(
        [
            jnp.stack([late[0], late[1], early[0], early[1], late[2], late[3], early[2], early[3]]),
            early[8:20],
            late[4:18],
            rel_sums,
        ]
    )
    weight_norms, update_norms, ratios = ratio_of(sums)
    conv_factor = jnp.where(jnp.arange(3 * D) < 2 * D, ratios[8], ratios[9])[None, :]
    vec_factor = jnp.concatenate([jnp.full((KERNEL,), ratios[10]), ratios[11:17]])[:, None]
    return (
        output.reshape(frames.shape),
        d0.reshape(frames.shape),
        in_grad,
        move(ffn_in, in_up, ratios[0:2][:, None, None]),
        in_m,
        in_q,
        out_grad,
        move(ffn_out, out_up, ratios[2:4][:, None, None]),
        out_m,
        out_q,
        attn_grad,
        move(attn_proj, attn_up, ratios[4:8][:, None, None]),
        attn_m,
        attn_q,
        attn_qo,
        conv_grad,
        move(conv_proj, conv_up, conv_factor),
        conv_m,
        conv_q,
        vec_grad,
        move(vectors, vec_up, vec_factor),
        vec_m,
        vec_q,
        rel_grad,
        move(rel_keys, rel_up, ratios[17]),
        rel_m,
        rel_q,
        jnp.stack([weight_norms, update_norms]),
    )


def solution(mesh):
    return jax.shard_map(
        body,
        mesh=mesh,
        in_specs=(
            P(("group", "shard"), None, None),
            P(("group", "shard")),
            P(("group", "shard"), None, None),
            P(None, "shard", None),
            P(None, "shard", None),
            P(None, "shard", None),
            P(None, "shard", None),
            P(None, "shard", None),
            P(None, "shard", None),
            P(None, "shard", None),
            P(None, "shard", None),
            P(None, "shard", None),
            P("shard", None),
            P("shard", None),
            P("shard", None),
            P(None, "shard"),
            P(None, "shard"),
            P(None, "shard"),
            P(),
            P(),
            P(),
        ),
        out_specs=(
            P(("group", "shard"), None, None),
            P(("group", "shard"), None, None),
            P(None, "shard", None),
            P(None, "shard", None),
            P(None, "shard", None),
            P(None, "shard", None),
            P(None, "shard", None),
            P(None, "shard", None),
            P(None, "shard", None),
            P(None, "shard", None),
            P(None, "shard", None),
            P(None, "shard", None),
            P(None, "shard", None),
            P(None, "shard", None),
            P("shard", None),
            P("shard", None),
            P("shard", None),
            P("shard", None),
            P("shard", None),
            P(None, "shard"),
            P(None, "shard"),
            P(None, "shard"),
            P(None, "shard"),
            P(),
            P(),
            P(),
            P(),
            P(),
        ),
        check_vma=False,
    )
```

```python
import math

import jax
import jax.numpy as jnp
from jax import lax
from jax.experimental import pallas as pl
from jax.experimental.pallas import tpu as pltpu
from jax.sharding import PartitionSpec as P

D = 512
FF = 2048
HEADS = 8
HEAD = 64
KERNEL = 31
BACK = 64
AHEAD = 8
RELS = 73
STEP = 10
PIECES = 32
LEAD = 32
FFN_ROWS = 128
ATTN_ROWS = 64
CONV_ROWS = 48

NORM_EPSILON = 1e-05
ADAM_EPSILON = 1e-06
RATIO_EPSILON = 1e-06
BETA_FIRST = 0.9
BETA_SECOND = 0.999
WEIGHT_DECAY = 0.01
LEARN_RATE = 0.5
MASKED_SCORE = -1e30

bf16 = jnp.bfloat16
f32 = jnp.float32
VMEM_LIMIT = 60 * 1024 * 1024


def vmem():
    return pl.BlockSpec(memory_space=pltpu.VMEM)


def smem():
    return pl.BlockSpec(memory_space=pltpu.SMEM)


def shape(dims, kind):
    return jax.ShapeDtypeStruct(dims, kind)


def dot(left, right):
    return jnp.dot(left, right, preferred_element_type=f32)


def dot_rows(left, right):
    return lax.dot_general(left, right, (((0,), (0,)), ((), ())), preferred_element_type=f32)


def dot_cols(left, right):
    return lax.dot_general(left, right, (((1,), (1,)), ((), ())), preferred_element_type=f32)


def stats(values):
    centred = values - jnp.mean(values, axis=-1, keepdims=True)
    scale = lax.rsqrt(jnp.mean(centred * centred, axis=-1, keepdims=True) + NORM_EPSILON)
    return centred * scale, scale


def norm_back(grad, normed, scale, gain):
    grad_gain = jnp.sum(grad * normed, axis=0, keepdims=True)
    scaled = grad * gain
    inner = jnp.mean(scaled * normed, axis=-1, keepdims=True)
    back = scale * (scaled - jnp.mean(scaled, axis=-1, keepdims=True) - normed * inner)
    return back, grad_gain


def logistic(values):
    return 1.0 / (1.0 + jnp.exp(-values))


def slope_of(values, sig):
    return sig * (1.0 + values * (1.0 - sig))


class Plan:
    def __init__(self, groups, shards):
        self.groups, self.shards = groups, shards
        shard_bits = shards.bit_length() - 1
        group_bits = groups.bit_length() - 1
        self.used = min(5 - shard_bits, group_bits)
        self.owned = PIECES // shards
        order = [("group", 0)] + [("shard", b) for b in range(shard_bits)]
        order += [("group", b) for b in range(1, self.used)]
        self.order = order
        self.rest = [("group", b) for b in range(self.used, group_bits)]
        self.shard_bits = [("shard", b) for b in range(shard_bits)]
        self.kept = [step for step in order if step[0] == "group"]

    def piece_bit(self, step):
        return step[1] if step[0] == "group" else self.used + step[1]

    def place(self, piece):
        out = 0
        for step in self.order:
            out = out * 2 + ((piece >> self.piece_bit(step)) & 1)
        return out

    def kept_place(self, piece):
        out = 0
        for step in self.kept:
            out = out * 2 + ((piece >> step[1]) & 1)
        return out


def swap(values, step):
    axis, bit = step
    count = lax.axis_size(axis)
    return lax.ppermute(values, axis, [(i, i ^ (1 << bit)) for i in range(count)])


def add_low(left, right):
    return (left.astype(f32) + right.astype(f32)).astype(bf16)


class Chain:
    def __init__(self, pieces, plan):
        self.todo = [("halve", s) for s in plan.order] + [("add", s) for s in plan.rest]
        self.todo += [("keep", s) for s in reversed(plan.kept)]
        half = pieces[0].shape[0] // 2
        self.kept = list(pieces)
        self.sent = join_rows([v[half:] for v in pieces])
        self.half = half

    def start(self):
        if self.todo:
            self.found = swap(self.sent, self.todo[0][1])

    def finish(self):
        if not self.todo:
            return
        kind, _ = self.todo.pop(0)
        kept = join_rows([v[: self.half] for v in self.kept])
        if kind == "keep":
            value = jnp.concatenate([kept, self.found], axis=0)
            low, high = value, value
        else:
            half = self.half // 2 if self.todo[0][0] == "halve" else self.half
            low = add_low(kept[:half], self.found[:half])
            high = low
            if half < self.half:
                high = add_low(kept[half:], self.found[half:])
        self.kept, self.sent, self.half = [low], high, low.shape[0]

    def end(self):
        while self.todo:
            self.start()
            self.finish()
        return self.sent


def join_rows(parts):
    return parts[0] if len(parts) == 1 else jnp.concatenate(parts, axis=1)


def beside(chains, run):
    for chain in chains:
        chain.start()
    outs = list(run([v for chain in chains for v in chain.kept]))
    for chain in reversed(chains):
        size = len(chain.kept)
        outs, chain.kept = outs[:-size], outs[-size:]
    for chain in chains:
        chain.finish()
    return outs


def sum_everywhere(values, plan):
    for step in plan.order + plan.rest:
        values = values + swap(values, step)
    return values


def sum_shards(values, plan):
    for step in plan.shard_bits:
        values = values + swap(values, step)
    return values


def hold(later, sooner):
    if later[0].plan.shards == 2:
        held = lax.optimization_barrier((*[f.mine for f in later], *[f.value for f in sooner]))
        for fetch, value in zip(later, held):
            fetch.mine = value
        for fetch, value in zip(sooner, held[len(later) :]):
            fetch.value = value


def ahead(near_one, near_two, later_one, later_two):
    if near_one.plan.shards == 2:
        return (near_one.value, near_two.value, later_one.mine, later_two.mine)
    return (near_one.value, near_two.value)


def settle(values, *fetches):
    for fetch, value in zip(fetches, values[:2]):
        fetch.value = value
    for fetch, value in zip(fetches[2:], values[2:]):
        fetch.mine = value


class Fetch:
    def __init__(self, own, dim, plan, core):
        self.own, self.plan, self.dim = own, plan, dim
        if plan.shards == 2:
            half = own.shape[dim] // 2
            self.mine = lax.dynamic_slice_in_dim(own, core * half, half, axis=dim).astype(bf16)

    def near(self):
        if self.plan.shards == 2:
            self.value = swap(self.mine, ("shard", 0))
        else:
            self.value = lax.all_gather(self.own.astype(bf16), "shard", axis=self.dim, tiled=True)

    def far(self):
        if self.plan.shards == 2:
            self.parts = (self.own, self.value, swap(self.value, ("group", 0)))
        else:
            self.parts = (self.value,)
        return self.parts


def join(place_ref, part_refs, whole_ref):
    if len(part_refs) == 1:
        whole_ref[...] = part_refs[0][...]
        return
    own, near, far = part_refs
    rows = own.shape[-2]
    half = rows // 2
    shard, core = place_ref[0], place_ref[1]
    first = pl.multiple_of(shard * rows, half)
    second = pl.multiple_of((1 - shard) * rows + core * half, half)
    third = pl.multiple_of((1 - shard) * rows + (1 - core) * half, half)
    if len(own.shape) == 2:
        whole_ref[pl.ds(first, rows), :] = own[...].astype(bf16)
        whole_ref[pl.ds(second, half), :] = near[...]
        whole_ref[pl.ds(third, half), :] = far[...]
    else:
        for k in range(own.shape[0]):
            whole_ref[k, pl.ds(first, rows), :] = own[k].astype(bf16)
            whole_ref[k, pl.ds(second, half), :] = near[k]
            whole_ref[k, pl.ds(third, half), :] = far[k]


def put(out_ref, plan, mine, value, row, rows_each, first):
    low = value.astype(bf16)
    for k in range(value.shape[0] // rows_each):
        spot = jnp.bitwise_xor(jnp.int32(plan.place(first + k)), mine)
        out_ref[spot, row : row + rows_each, :] = low[k * rows_each : (k + 1) * rows_each]


def call(kernel, outs, ins, specs, scratch=(), name=None, flops=0, nbytes=0, thread=()):
    taken, given, passed = len(ins), len(outs), len(thread)
    inner = kernel

    def outer(*refs):
        inner(*refs[:taken], *refs[taken + passed : taken + passed + given], *refs[taken + 2 * passed + given :])

    cost = pl.CostEstimate(flops=int(flops), transcendentals=0, bytes_accessed=int(nbytes))
    found = pl.pallas_call(
        outer,
        out_shape=[*outs, *[shape(v.shape, v.dtype) for v in thread]],
        in_specs=[*specs, *[pl.BlockSpec(memory_space=pl.ANY)] * passed],
        out_specs=[vmem()] * given + [pl.BlockSpec(memory_space=pl.ANY)] * passed,
        input_output_aliases={taken + k: given + k for k in range(passed)},
        scratch_shapes=list(scratch),
        compiler_params=pltpu.CompilerParams(vmem_limit_bytes=VMEM_LIMIT),
        cost_estimate=cost,
        name=name,
    )(*ins, *thread)
    return found


def ffn_ahead(values, gain, win, wout, entry_ref, hidden_ref, slope_ref):
    normed, _ = stats(values)
    entry = (normed * gain).astype(bf16)
    entry_ref[...] = entry
    total = jnp.zeros(values.shape, f32)
    for b in range(FF // D):
        cols = slice(b * D, (b + 1) * D)
        before = dot(entry, win[:, cols])
        sig = logistic(before)
        hidden = (before * sig).astype(bf16)
        hidden_ref[:, cols] = hidden
        slope_ref[:, cols] = slope_of(before, sig).astype(bf16)
        total = total + dot(hidden, wout[cols, :])
    return total


def ffn_behind(grad, values, gain, win, wout, entry_ref, hidden_ref, slope_ref, out_ref, plan, mine):
    normed, scale = stats(values)
    entry = entry_ref[...]
    branch = (0.5 * grad).astype(bf16)
    grad_entry = jnp.zeros(values.shape, f32)
    for b in range(FF // D):
        cols = slice(b * D, (b + 1) * D)
        put(out_ref, plan, mine, dot_rows(hidden_ref[:, cols], branch), 64, 64, 8 * b)
        grad_before = (dot_cols(branch, wout[cols, :]) * slope_ref[:, cols].astype(f32)).astype(bf16)
        put(out_ref, plan, mine, dot_rows(entry, grad_before), 16 * b, 16, 0)
        grad_entry = grad_entry + dot_cols(grad_before, win[:, cols])
    back, grad_gain = norm_back(grad_entry, normed, scale, gain)
    return grad + back, grad_gain


def ffn_first(frames, vec, win_parts, wout_parts, place, plan, thread=()):
    rows = frames.shape[0]
    n = len(win_parts)

    def kernel(place_ref, x_ref, vec_ref, *rest):
        wins, wouts = rest[:n], rest[n : 2 * n]
        out_ref, entry_ref, hidden_ref, slope_ref, win, wout = rest[2 * n :]
        join(place_ref, wins, win)
        join(place_ref, wouts, wout)
        values = x_ref[...].astype(f32)
        total = ffn_ahead(values, vec_ref[31:32, :], win, wout, entry_ref, hidden_ref, slope_ref)
        out_ref[...] = values + 0.5 * total

    return call(
        kernel,
        [shape((rows, D), f32), shape((rows, D), bf16), shape((rows, FF), bf16), shape((rows, FF), bf16)],
        [place, frames, vec, *win_parts, *wout_parts],
        [smem()] + [vmem()] * (2 + 2 * n),
        [pltpu.VMEM((D, FF), bf16), pltpu.VMEM((FF, D), bf16)],
        "ffn_first",
        4 * rows * D * FF,
        12e6,
        thread,
    )


def ffn_last(values, vec, cotangent, lengths, win_parts, wout_parts, place, plan, thread=()):
    rows = values.shape[0]
    count = lengths.shape[0]
    n = len(win_parts)

    def kernel(place_ref, len_ref, x_ref, vec_ref, cot_ref, *rest):
        wins, wouts = rest[:n], rest[n : 2 * n]
        y_ref, dx_ref, gain_ref, g_ref, win, wout, entry_ref, hidden_ref, slope_ref = rest[2 * n :]
        join(place_ref, wins, win)
        join(place_ref, wouts, wout)
        x = x_ref[...]
        gain = vec_ref[35:36, :]
        total = ffn_ahead(x, gain, win, wout, entry_ref, hidden_ref, slope_ref)
        normed, scale = stats(x + 0.5 * total)
        top = vec_ref[36:37, :]
        y_ref[...] = (normed * top).astype(bf16)
        each = rows // count
        grads = []
        for s in range(count):
            spot = lax.broadcasted_iota(jnp.int32, (each, 1), 0)
            part = cot_ref[s * each : (s + 1) * each, :].astype(f32)
            grads.append(jnp.where(spot < len_ref[s], part, 0.0))
        back, grad_top = norm_back(jnp.concatenate(grads, axis=0), normed, scale, top)
        grad, grad_gain = ffn_behind(
            back, x, gain, win, wout, entry_ref, hidden_ref, slope_ref, g_ref, plan, place_ref[2]
        )
        dx_ref[...] = grad
        gain_ref[...] = jnp.concatenate([grad_gain, grad_top, jnp.zeros((6, D), f32)], axis=0)

    return call(
        kernel,
        [shape((rows, D), bf16), shape((rows, D), f32), shape((8, D), f32), shape((PIECES, FFN_ROWS, D), bf16)],
        [place, lengths, values, vec, cotangent, *win_parts, *wout_parts],
        [smem(), smem()] + [vmem()] * (3 + 2 * n),
        [
            pltpu.VMEM((D, FF), bf16),
            pltpu.VMEM((FF, D), bf16),
            pltpu.VMEM((rows, D), bf16),
            pltpu.VMEM((rows, FF), bf16),
            pltpu.VMEM((rows, FF), bf16),
        ],
        "ffn_last",
        12 * rows * D * FF,
        16e6,
        thread,
    )


def ffn_first_out(grad, hidden, slope, wout_parts, place, plan, thread=()):
    rows = grad.shape[0]
    n = len(wout_parts)

    def kernel(place_ref, grad_ref, hidden_ref, slope_ref, *rest):
        wouts = rest[:n]
        before_ref, g_ref, wout = rest[n:]
        join(place_ref, wouts, wout)
        branch = (0.5 * grad_ref[...]).astype(bf16)
        for b in range(FF // D):
            cols = slice(b * D, (b + 1) * D)
            put(g_ref, plan, place_ref[2], dot_rows(hidden_ref[:, cols], branch), 0, 64, 8 * b)
            spread = dot_cols(branch, wout[cols, :])
            before_ref[:, cols] = (spread * slope_ref[:, cols].astype(f32)).astype(bf16)

    return call(
        kernel,
        [shape((rows, FF), bf16), shape((PIECES, 64, D), bf16)],
        [place, grad, hidden, slope, *wout_parts],
        [smem()] + [vmem()] * (3 + n),
        [pltpu.VMEM((FF, D), bf16)],
        "ffn_first_out",
        4 * rows * D * FF,
        12e6,
        thread,
    )


def ffn_first_in(grad, frames, vec, entry, before, win_parts, place, plan, thread=()):
    rows = frames.shape[0]
    n = len(win_parts)

    def kernel(place_ref, grad_ref, x_ref, vec_ref, entry_ref, before_ref, *rest):
        wins = rest[:n]
        dx_ref, gain_ref, g_ref, win = rest[n:]
        join(place_ref, wins, win)
        low = entry_ref[...]
        grad_entry = jnp.zeros((rows, D), f32)
        for b in range(FF // D):
            cols = slice(b * D, (b + 1) * D)
            put(g_ref, plan, place_ref[2], dot_rows(low, before_ref[:, cols]), 16 * b, 16, 0)
            grad_entry = grad_entry + dot_cols(before_ref[:, cols], win[:, cols])
        normed, scale = stats(x_ref[...].astype(f32))
        back, grad_gain = norm_back(grad_entry, normed, scale, vec_ref[31:32, :])
        dx_ref[...] = (grad_ref[...] + back).astype(bf16)
        gain_ref[...] = jnp.concatenate([grad_gain, jnp.zeros((7, D), f32)], axis=0)

    return call(
        kernel,
        [shape((rows, D), bf16), shape((8, D), f32), shape((PIECES, 64, D), bf16)],
        [place, grad, frames, vec, entry, before, *win_parts],
        [smem()] + [vmem()] * (5 + n),
        [pltpu.VMEM((D, FF), bf16)],
        "ffn_first_in",
        4 * rows * D * FF,
        12e6,
        thread,
    )


def attend(values, vec, rel_table, lengths, parts, place, plan, thread=()):
    rows = values.shape[0]
    count = lengths.shape[0]
    each = rows // count
    n = len(parts)
    pairs = HEADS // 2

    def kernel(place_ref, len_ref, x_ref, vec_ref, rel_ref, *rest):
        ws = rest[:n]
        out_ref, entry_ref, qkv_ref, prob_ref, mix_ref, weight, mixed = rest[n:]
        join(place_ref, ws, weight)
        x = x_ref[...]
        normed, _ = stats(x)
        entry = (normed * vec_ref[32:33, :]).astype(bf16)
        entry_ref[...] = entry
        for k in range(3):
            heads = dot(entry, weight[k]).astype(bf16)
            for p in range(pairs):
                qkv_ref[k, p] = heads[:, p * 128 : (p + 1) * 128]
        lane = lax.broadcasted_iota(jnp.int32, (1, 128), 1)
        table = rel_ref[...]
        spot = lax.broadcasted_iota(jnp.int32, (1, each), 1)

        def step(i, carry):
            s = i // pairs
            p = i % pairs
            span = pl.ds(pl.multiple_of(s * each, each), each)
            query = qkv_ref[0, p, span, :]
            keys = qkv_ref[1, p, span, :]
            vals = qkv_ref[2, p, span, :]
            valid = spot < len_ref[s]
            both = []
            for h in range(2):
                mask = (lane < HEAD) if h == 0 else (lane >= HEAD)
                mine = jnp.where(mask, query, jnp.zeros_like(query))
                raw = dot_cols(mine, keys)
                skew = pltpu.roll(dot_cols(mine, table), 0, 1, stride=1, stride_axis=0)[:, :each]
                scores = jnp.where(valid, (raw + skew) * 0.125, MASKED_SCORE)
                grown = jnp.exp(scores - jnp.max(scores, axis=-1, keepdims=True))
                low = (grown * (1.0 / jnp.sum(grown, axis=-1, keepdims=True))).astype(bf16)
                prob_ref[2 * i + h] = low
                both.append(dot(low, vals))
            mixed[p, span, :] = jnp.where(lane < HEAD, both[0], both[1]).astype(bf16)
            return carry

        lax.fori_loop(0, count * pairs, step, 0)
        mix = jnp.concatenate([mixed[p] for p in range(pairs)], axis=1)
        mix_ref[...] = mix
        out_ref[...] = x + dot(mix, weight[3])

    return call(
        kernel,
        [
            shape((rows, D), f32),
            shape((rows, D), bf16),
            shape((3, pairs, rows, 128), bf16),
            shape((count * HEADS, each, each), bf16),
            shape((rows, D), bf16),
        ],
        [place, lengths, values, vec, rel_table, *parts],
        [smem(), smem()] + [vmem()] * (3 + n),
        [pltpu.VMEM((4, D, D), bf16), pltpu.VMEM((pairs, rows, 128), bf16)],
        "attend",
        16 * rows * D * D,
        20e6,
        thread,
    )


def attend_back(grad, values, vec, kept, rel_table, parts, place, plan, count, thread=()):
    rows = values.shape[0]
    each = rows // count
    n = len(parts)
    pairs = HEADS // 2
    entry, qkv, prob, mix = kept
    width = rel_table.shape[0]

    def kernel(place_ref, grad_ref, x_ref, vec_ref, entry_ref, qkv_ref, prob_ref, mix_ref, rel_ref, *rest):
        ws = rest[:n]
        dx_ref, gain_ref, rel_out, g_ref, weight, dmix, dqkv = rest[n:]
        mine_spot = place_ref[2]
        join(place_ref, ws, weight)
        down = grad_ref[...]
        low = down.astype(bf16)
        put(g_ref, plan, mine_spot, dot_rows(mix_ref[...], low), 48, 16, 0)
        spread = dot_cols(low, weight[3]).astype(bf16)
        for p in range(pairs):
            dmix[p] = spread[:, p * 128 : (p + 1) * 128]
        lane = lax.broadcasted_iota(jnp.int32, (1, 128), 1)
        table = rel_ref[...]
        flip = (
            lax.broadcasted_iota(jnp.int32, (each, each), 0)
            + lax.broadcasted_iota(jnp.int32, (each, each), 1)
            == each - 1
        ).astype(bf16)
        rel_out[...] = jnp.zeros_like(rel_out)

        def step(i, carry):
            s = i // pairs
            p = i % pairs
            span = pl.ds(pl.multiple_of(s * each, each), each)
            query = qkv_ref[0, p, span, :]
            keys = qkv_ref[1, p, span, :]
            vals = qkv_ref[2, p, span, :]
            outer = dmix[p, span, :]
            grad_q = jnp.zeros((each, 128), f32)
            grad_k = jnp.zeros((each, 128), f32)
            grad_v = jnp.zeros((each, 128), f32)
            grad_r = jnp.zeros((width, 128), f32)
            for h in range(2):
                mask = (lane < HEAD) if h == 0 else (lane >= HEAD)

                def pick(v):
                    return jnp.where(mask, v, jnp.zeros_like(v))

                dout = pick(outer)
                q_own = pick(query)
                prob_low = prob_ref[2 * i + h]
                prob_wide = prob_low.astype(f32)
                dprob = dot_cols(dout, vals)
                inner = jnp.sum(prob_wide * dprob, axis=-1, keepdims=True)
                dscore = (prob_wide * (dprob - inner)).astype(bf16)
                grad_v = grad_v + dot_rows(prob_low, dout)
                grad_k = grad_k + dot_rows(dscore, q_own)
                turned = dot(flip, dscore)
                wide = jnp.concatenate([turned, jnp.zeros((each, width - each), f32)], axis=1)
                skew = pltpu.roll(wide, width - each + 1, 1, stride=1, stride_axis=0).astype(bf16)
                along = dot(flip, skew).astype(bf16)
                grad_q = grad_q + dot(dscore, pick(keys)) + dot(along, pick(table))
                grad_r = grad_r + dot_rows(along, q_own)
            dqkv[0, p, span, :] = (grad_q * 0.125).astype(bf16)
            dqkv[1, p, span, :] = (grad_k * 0.125).astype(bf16)
            dqkv[2, p, span, :] = grad_v.astype(bf16)
            rel_out[...] += grad_r * 0.125
            return carry

        lax.fori_loop(0, count * pairs, step, 0)
        entry_low = entry_ref[...]
        grad_entry = jnp.zeros((rows, D), f32)
        for k in range(3):
            heads = jnp.concatenate([dqkv[k, p] for p in range(pairs)], axis=1)
            put(g_ref, plan, mine_spot, dot_rows(entry_low, heads), 16 * k, 16, 0)
            grad_entry = grad_entry + dot_cols(heads, weight[k])
        normed, scale = stats(x_ref[...])
        back, grad_gain = norm_back(grad_entry, normed, scale, vec_ref[32:33, :])
        dx_ref[...] = down + back
        gain_ref[...] = jnp.concatenate([grad_gain, jnp.zeros((7, D), f32)], axis=0)

    return call(
        kernel,
        [
            shape((rows, D), f32),
            shape((8, D), f32),
            shape((width, 128), f32),
            shape((PIECES, ATTN_ROWS, D), bf16),
        ],
        [place, grad, values, vec, entry, qkv, prob, mix, rel_table, *parts],
        [smem()] + [vmem()] * (8 + n),
        [
            pltpu.VMEM((4, D, D), bf16),
            pltpu.VMEM((pairs, rows, 128), bf16),
            pltpu.VMEM((3, pairs, rows, 128), bf16),
        ],
        "attend_back",
        50 * rows * D * D,
        24e6,
        thread,
    )


def convolve(values, vec, parts, place, plan, count, thread=()):
    rows = values.shape[0]
    each = rows // count
    n = len(parts)
    cols = D // 128
    chunk = 64

    def kernel(place_ref, x_ref, vec_ref, *rest):
        ws = rest[:n]
        out_ref, entry_ref, gated_ref, sig_ref, conv_ref, act_ref, weight = rest[n:]
        join(place_ref, ws, weight)
        x = x_ref[...]
        normed, _ = stats(x)
        entry = (normed * vec_ref[33:34, :]).astype(bf16)
        entry_ref[...] = entry
        linear = dot(entry, weight[:, :D])
        sig = logistic(dot(entry, weight[:, D : 2 * D]))
        sig_ref[...] = sig
        gated = linear * sig
        for s in range(count):
            for c in range(cols):
                gated_ref[s, c, :LEAD, :] = jnp.zeros((LEAD, 128), f32)
                gated_ref[s, c, LEAD:, :] = gated[s * each : (s + 1) * each, c * 128 : (c + 1) * 128]
        for c in range(cols):
            taps = vec_ref[0:32, c * 128 : (c + 1) * 128]

            def step(i, carry):
                s = i // (each // chunk)
                t = (i % (each // chunk)) * chunk
                total = jnp.zeros((chunk, 128), f32)
                for k in range(KERNEL):
                    total = total + taps[k : k + 1] * gated_ref[s, c, pl.ds(t + k + LEAD - KERNEL + 1, chunk), :]
                conv_ref[pl.ds(pl.multiple_of(i * chunk, chunk), chunk), c * 128 : (c + 1) * 128] = total
                return carry

            lax.fori_loop(0, rows // chunk, step, 0)
        inner, _ = stats(conv_ref[...])
        act = inner * vec_ref[34:35, :]
        low = (act * logistic(act)).astype(bf16)
        act_ref[...] = low
        out_ref[...] = x + dot(low, weight[:, 2 * D :])

    return call(
        kernel,
        [
            shape((rows, D), f32),
            shape((rows, D), bf16),
            shape((count, cols, each + LEAD, 128), f32),
            shape((rows, D), f32),
            shape((rows, D), f32),
            shape((rows, D), bf16),
        ],
        [place, values, vec, *parts],
        [smem()] + [vmem()] * (2 + n),
        [pltpu.VMEM((D, 3 * D), bf16)],
        "convolve",
        12 * rows * D * D,
        16e6,
        thread,
    )


def convolve_back(grad, values, vec, kept, parts, place, plan, count, thread=()):
    rows = values.shape[0]
    each = rows // count
    n = len(parts)
    cols = D // 128
    entry, gated, sig, conved, act = kept

    def kernel(place_ref, grad_ref, x_ref, vec_ref, entry_ref, gated_ref, sig_ref, conv_ref, act_ref, *rest):
        ws = rest[:n]
        dx_ref, gain_ref, taps_out, g_ref, weight, dconv, dgated = rest[n:]
        mine = place_ref[1 + 1]
        join(place_ref, ws, weight)
        down = grad_ref[...]
        low = down.astype(bf16)
        put(g_ref, plan, mine, dot_rows(act_ref[...], low), 32, 16, 0)
        inner, inner_scale = stats(conv_ref[...])
        inner_gain = vec_ref[34:35, :]
        act_in = inner * inner_gain
        grad_act = dot_cols(low, weight[:, 2 * D :]) * slope_of(act_in, logistic(act_in))
        grad_conv, gain_inner = norm_back(grad_act, inner, inner_scale, inner_gain)
        for s in range(count):
            for c in range(cols):
                dconv[s, c, :each, :] = grad_conv[s * each : (s + 1) * each, c * 128 : (c + 1) * 128]
                dconv[s, c, each:, :] = jnp.zeros((LEAD, 128), f32)
        for c in range(cols):
            lanes = slice(c * 128, (c + 1) * 128)
            taps = vec_ref[0:32, lanes]

            def step(i, sums):
                s = i // (each // 8)
                t = (i % (each // 8)) * 8
                here = dconv[s, c, pl.ds(pl.multiple_of(t, 8), 8), :]
                total = jnp.zeros((8, 128), f32)
                new = []
                for k in range(KERNEL):
                    new.append(sums[k] + here * gated_ref[s, c, pl.ds(t + k + LEAD - KERNEL + 1, 8), :])
                    total = total + taps[k : k + 1] * dconv[s, c, pl.ds(t + KERNEL - 1 - k, 8), :]
                dgated[pl.ds(pl.multiple_of(i * 8, 8), 8), lanes] = total
                return tuple(new)

            sums = lax.fori_loop(0, rows // 8, step, tuple(jnp.zeros((8, 128), f32) for _ in range(KERNEL)))
            found = [jnp.sum(v, axis=0, keepdims=True) for v in sums]
            taps_out[:, lanes] = jnp.concatenate(found + [jnp.zeros((1, 128), f32)], axis=0)
        grad_gated = dgated[...]
        sig_wide = sig_ref[...]
        linear_sig = jnp.concatenate(
            [
                jnp.concatenate([gated_ref[s, c, LEAD:, :] for c in range(cols)], axis=1)
                for s in range(count)
            ],
            axis=0,
        )
        grad_one = (grad_gated * sig_wide).astype(bf16)
        grad_two = (grad_gated * linear_sig * (1.0 - sig_wide)).astype(bf16)
        entry_low = entry_ref[...]
        put(g_ref, plan, mine, dot_rows(entry_low, grad_one), 0, 16, 0)
        put(g_ref, plan, mine, dot_rows(entry_low, grad_two), 16, 16, 0)
        grad_entry = dot_cols(grad_one, weight[:, :D]) + dot_cols(grad_two, weight[:, D : 2 * D])
        normed, scale = stats(x_ref[...])
        back, gain_outer = norm_back(grad_entry, normed, scale, vec_ref[33:34, :])
        dx_ref[...] = down + back
        gain_ref[...] = jnp.concatenate([gain_outer, gain_inner, jnp.zeros((6, D), f32)], axis=0)

    return call(
        kernel,
        [
            shape((rows, D), f32),
            shape((8, D), f32),
            shape((32, D), f32),
            shape((PIECES, CONV_ROWS, D), bf16),
        ],
        [place, grad, values, vec, entry, gated, sig, conved, act, *parts],
        [smem()] + [vmem()] * (8 + n),
        [
            pltpu.VMEM((D, 3 * D), bf16),
            pltpu.VMEM((count, cols, each + LEAD, 128), f32),
            pltpu.VMEM((rows, D), f32),
        ],
        "convolve_back",
        40 * rows * D * D,
        20e6,
        thread,
    )


def adam(weight, moment, square, grad):
    new_moment = BETA_FIRST * moment + (1.0 - BETA_FIRST) * grad
    new_square = BETA_SECOND * square + (1.0 - BETA_SECOND) * grad * grad
    first = new_moment * (1.0 / (1.0 - BETA_FIRST**STEP))
    second = new_square * (1.0 / (1.0 - BETA_SECOND**STEP))
    update = first / (jnp.sqrt(second) + ADAM_EPSILON) + WEIGHT_DECAY * weight
    return new_moment, new_square, update


def folded(values):
    squares = jnp.sum((values * values).reshape(-1, values.shape[-1]), axis=0, keepdims=True)
    total = squares[:, :128]
    for c in range(1, values.shape[-1] // 128):
        total = total + squares[:, c * 128 : (c + 1) * 128]
    return total


def update_matrix(layer, pieces, block, spots, states, given, name):
    count = spots.shape[0]
    rows, cols = states[0].shape[1] // count, states[0].shape[2]
    given = given or ()

    def kernel(spot_ref, g_ref, w_ref, m_ref, q_ref, *rest):
        g_out, u_out, m_out, q_out, sums = rest[len(given) :]

        @pl.when(pl.program_id(0) == 0)
        def _():
            sums[...] = jnp.zeros_like(sums)

        raw = g_ref[0].astype(f32)
        grad = jnp.concatenate([raw[k * rows : (k + 1) * rows] for k in range(cols // D)], axis=1)
        weight = w_ref[0]
        new_moment, new_square, update = adam(weight, m_ref[0], q_ref[0], grad)
        g_out[0] = grad
        u_out[0] = update
        m_out[0] = new_moment
        q_out[0] = new_square
        sums[...] += jnp.concatenate([folded(weight), folded(update), jnp.zeros((6, 128), f32)], axis=0)

    tile = pl.BlockSpec((1, rows, cols), lambda p, spot: (layer, p, 0))
    return pl.pallas_call(
        kernel,
        out_shape=[shape(states[0].shape, f32)] * 4 + [shape((8, 128), f32)],
        grid_spec=pltpu.PrefetchScalarGridSpec(
            num_scalar_prefetch=1,
            grid=(count,),
            in_specs=[pl.BlockSpec((1, 64, D), lambda p, spot: (spot[p], block, 0))]
            + [tile] * 3
            + [pl.BlockSpec(memory_space=pl.ANY)] * len(given),
            out_specs=[tile] * 4 + [pl.BlockSpec((8, 128), lambda p, spot: (0, 0))],
        ),
        input_output_aliases={5 + k: k for k in range(len(given))},
        compiler_params=pltpu.CompilerParams(vmem_limit_bytes=VMEM_LIMIT),
        cost_estimate=pl.CostEstimate(flops=0, transcendentals=0, bytes_accessed=30000000),
        name=name,
    )(spots, pieces, *states, *given)


def move_matrix(layer, weight, update, factor, name):
    _, rows, cols = weight.shape
    steps = 4
    tile = pl.BlockSpec((1, rows // steps, cols), lambda p: (layer, p, 0))

    def kernel(factor_ref, w_ref, u_ref, out_ref):
        out_ref[...] = w_ref[...] - (LEARN_RATE * factor_ref[0]) * u_ref[...]

    return pl.pallas_call(
        kernel,
        out_shape=shape(weight.shape, f32),
        grid=(steps,),
        in_specs=[smem(), tile, tile],
        out_specs=tile,
        input_output_aliases={2: 0},
        cost_estimate=pl.CostEstimate(flops=0, transcendentals=0, bytes_accessed=12000000),
        name=name,
    )(factor.reshape(1), weight, update)


def update_rest(pieces, spots, attn, conv):
    count = spots.shape[0]
    rows = attn[0].shape[1] // count

    def kernel(spot_ref, g_ref, wa, ma, qa, wc, mc, qc, *outs):
        ga_out, ua_out, ma_out, qa_out, qo_out, gc_out, uc_out, mc_out, qc_out, sums = outs
        index = pl.program_id(0)

        @pl.when(index == 0)
        def _():
            sums[...] = jnp.zeros_like(sums)

        found = []
        for k in range(4):
            grad = g_ref[0, CONV_ROWS + k * 16 : CONV_ROWS + (k + 1) * 16].astype(f32)
            weight = wa[k]
            new_moment, new_square, update = adam(weight, ma[k], qa[k], grad)
            ga_out[k] = grad
            ua_out[k] = update
            ma_out[k] = new_moment
            if k < 3:
                qa_out[k] = new_square
            else:
                qo_out[...] = new_square
            found += [folded(weight), folded(update)]
        for low, high in ((0, 2), (2, 3)):
            lanes = slice(low * D, high * D)
            grad = jnp.concatenate([g_ref[0, k * 16 : (k + 1) * 16] for k in range(low, high)], axis=1)
            grad = grad.astype(f32)
            weight = wc[:, lanes]
            new_moment, new_square, update = adam(weight, mc[:, lanes], qc[:, lanes], grad)
            gc_out[:, lanes] = grad
            uc_out[:, lanes] = update
            mc_out[:, lanes] = new_moment
            qc_out[:, lanes] = new_square
            found += [folded(weight), folded(update)]
        sums[...] += jnp.concatenate(found + [jnp.zeros((4, 128), f32)], axis=0)

    attn_block = pl.BlockSpec((4, rows, D), lambda p, spot: (0, p, 0))
    conv_block = pl.BlockSpec((rows, 3 * D), lambda p, spot: (p, 0))
    three = pl.BlockSpec((3, rows, D), lambda p, spot: (0, p, 0))
    one = pl.BlockSpec((rows, D), lambda p, spot: (p, 0))
    side = attn[0].shape[1]
    return pl.pallas_call(
        kernel,
        out_shape=[shape(attn[0].shape, f32)] * 3
        + [shape((3, side, D), f32), shape((side, D), f32)]
        + [shape(conv[0].shape, f32)] * 4
        + [shape((16, 128), f32)],
        grid_spec=pltpu.PrefetchScalarGridSpec(
            num_scalar_prefetch=1,
            grid=(count,),
            in_specs=[
                pl.BlockSpec((1, CONV_ROWS + ATTN_ROWS, D), lambda p, spot: (spot[p], 0, 0)),
            ]
            + [attn_block] * 3
            + [conv_block] * 3,
            out_specs=[attn_block] * 3
            + [three, one]
            + [conv_block] * 4
            + [pl.BlockSpec((16, 128), lambda p, spot: (0, 0))],
        ),
        compiler_params=pltpu.CompilerParams(vmem_limit_bytes=VMEM_LIMIT),
        cost_estimate=pl.CostEstimate(flops=0, transcendentals=0, bytes_accessed=28000000),
        name="update_rest",
    )(spots, pieces, *attn, *conv)


def move(weight, update, factor):
    return weight - LEARN_RATE * factor * update


def ratio_of(sums):
    weight, update = sums[0::2], sums[1::2]
    return jnp.sqrt(weight), jnp.sqrt(update), jnp.sqrt(weight) / jnp.sqrt(update + RATIO_EPSILON)


def split_last(values):
    return values[:-1], values[-1]


def body(
    frames,
    lengths,
    cotangent,
    ffn_in,
    ffn_in_moment,
    ffn_in_square,
    ffn_out,
    ffn_out_moment,
    ffn_out_square,
    attn_proj,
    attn_moment,
    attn_square,
    conv_proj,
    conv_moment,
    conv_square,
    vectors,
    vectors_moment,
    vectors_square,
    rel_keys,
    rel_moment,
    rel_square,
):
    groups, shards = lax.axis_size("group"), lax.axis_size("shard")
    plan = Plan(groups, shards)
    group, shard = lax.axis_index("group"), lax.axis_index("shard")
    core = jnp.bitwise_and(group, 1)
    count, each, _ = frames.shape
    mine = jnp.int32(0)
    for step in plan.order:
        bit = jnp.right_shift(group if step[0] == "group" else shard, step[1]) & 1
        mine = mine * 2 + bit
    kept = jnp.int32(0)
    for step in plan.kept:
        kept = kept * 2 + (jnp.right_shift(group, step[1]) & 1)
    spots = jnp.array([plan.kept_place(p) for p in range(plan.owned)], jnp.int32) ^ kept
    place = jnp.stack([shard, core, mine]).astype(jnp.int32)

    win0, wout0, win1, wout1 = (
        Fetch(w[k], 0, plan, core) for k in range(2) for w in (ffn_in, ffn_out)
    )
    watt, wconv = Fetch(attn_proj, 1, plan, core), Fetch(conv_proj, 0, plan, core)
    win0.near()
    wout0.near()
    vec = lax.all_gather(vectors.astype(bf16), "shard", axis=1, tiled=True) if shards != 2 else None
    if vec is None:
        low = vectors.astype(bf16)
        other = swap(low, ("shard", 0))
        vec = jnp.where(shard == 0, jnp.concatenate([low, other], 1), jnp.concatenate([other, low], 1))
    vec = jnp.concatenate([vec.astype(f32), jnp.zeros((3, D), f32)], axis=0)
    rel_low = rel_keys.astype(bf16)
    table = jnp.concatenate(
        [
            rel_low[BACK:],
            jnp.broadcast_to(rel_low[RELS - 1 :], (each - AHEAD - 1, HEAD)),
            jnp.broadcast_to(rel_low[:1], (each - BACK, HEAD)),
            rel_low[:BACK],
        ],
        axis=0,
    )
    table = jnp.concatenate([table, table], axis=1)

    flat = frames.reshape(count * each, D)
    hold((watt, wconv), (win0, wout0))
    win0, wout0 = win0.far(), wout0.far()
    watt.near()
    wconv.near()
    x1, entry0, hidden0, slope0, *through = ffn_first(
        flat, vec, win0, wout0, place, plan, ahead(watt, wconv, win1, wout1)
    )
    settle(through, watt, wconv, win1, wout1)
    watt, wconv = watt.far(), wconv.far()
    win1.near()
    wout1.near()
    x2, *kept_attn, through = attend(x1, vec, table, lengths, watt, place, plan, (win1.value,))
    win1.value = through
    win1 = win1.far()
    x3, *kept_conv, through = convolve(x2, vec, wconv, place, plan, count, (wout1.value,))
    wout1.value = through
    wout1 = wout1.far()
    output, d3, gains_last, pieces_last = ffn_last(
        x3, vec, cotangent.reshape(count * each, D), lengths, win1, wout1, place, plan
    )
    last = Chain([pieces_last], plan)
    d2, gains_conv, taps, pieces_conv = beside(
        [last], lambda t: convolve_back(d3, x2, vec, kept_conv, wconv, place, plan, count, t)
    )
    d1, gains_attn, rel_wide, pieces_attn = beside(
        [last], lambda t: attend_back(d2, x1, vec, kept_attn, table, watt, place, plan, count, t)
    )
    middle = Chain([pieces_conv, pieces_attn], plan)
    before0, pieces_out = beside(
        [last, middle], lambda t: ffn_first_out(d1, hidden0, slope0, wout0, place, plan, t)
    )
    first_out = Chain([pieces_out], plan)
    d0, gains_first, pieces_in = beside(
        [last, middle, first_out], lambda t: ffn_first_in(d1, flat, vec, entry0, before0, win0, place, plan, t)
    )
    first_in = Chain([pieces_in], plan)
    owned_last = last.end()
    owned_middle = middle.end()
    owned_out = first_out.end()
    owned_in = first_in.end()

    rel_half = rel_wide[:, :HEAD] + rel_wide[:, HEAD:]
    edge = 2 * each - BACK
    rel_local = jnp.concatenate(
        [
            jnp.sum(rel_half[each : edge + 1], axis=0, keepdims=True),
            rel_half[edge + 1 :],
            rel_half[:AHEAD],
            jnp.sum(rel_half[AHEAD:each], axis=0, keepdims=True),
        ],
        axis=0,
    )
    vec_local = jnp.concatenate(
        [taps[:KERNEL], gains_first[:1], gains_attn[:1], gains_conv[:2], gains_last[:2]], axis=0
    )
    rel_lines = jnp.pad(rel_local.reshape(-1), (0, 10 * D - RELS * HEAD)).reshape(10, D)
    small = sum_everywhere(jnp.concatenate([vec_local, rel_lines, jnp.zeros((1, D), f32)], axis=0), plan)
    wide = vectors.shape[1]
    vec_grad = lax.dynamic_slice(small, (0, shard * wide), (KERNEL + 6, wide))
    rel_grad = small[KERNEL + 6 : KERNEL + 16].reshape(-1)[: RELS * HEAD].reshape(RELS, HEAD)

    in_states = (ffn_in, ffn_in_moment, ffn_in_square)
    out_states = (ffn_out, ffn_out_moment, ffn_out_square)
    *half_in, sums_in1 = update_matrix(1, owned_last, 0, spots, in_states, None, "update_in1")
    *half_out, sums_out1 = update_matrix(1, owned_last, 1, spots, out_states, None, "update_out1")
    (attn_grad, attn_up, attn_m, attn_q, attn_qo, conv_grad, conv_up, conv_m, conv_q, sums_rest) = update_rest(
        owned_middle,
        spots,
        (attn_proj, attn_moment, attn_square),
        (conv_proj, conv_moment, conv_square),
    )
    (out_grad, out_up, out_m, out_q), sums_out0 = split_last(
        update_matrix(0, owned_out, 0, spots, out_states, half_out, "update_out0")
    )
    (in_grad, in_up, in_m, in_q), sums_in0 = split_last(
        update_matrix(0, owned_in, 0, spots, in_states, half_in, "update_in0")
    )
    vec_m, vec_q, vec_up = adam(vectors, vectors_moment, vectors_square, vec_grad)
    rel_m, rel_q, rel_up = adam(rel_keys, rel_moment, rel_square, rel_grad)

    vec_sums = []
    for part in (vectors, vec_up):
        squares = jnp.sum(part * part, axis=1)
        vec_sums.append(jnp.concatenate([jnp.sum(squares[:KERNEL])[None], squares[KERNEL:]]))
    early = sum_shards(jnp.sum(jnp.concatenate([sums_in1[:2], sums_out1[:2], sums_rest[:12]], axis=0), axis=1), plan)
    late = sum_shards(jnp.concatenate([jnp.sum(sums_out0[:2], axis=1), jnp.stack(vec_sums, axis=1).reshape(-1)]), plan)
    final = sum_shards(jnp.sum(sums_in0[:2], axis=1), plan)
    rel_sums = jnp.stack([jnp.sum(rel_keys * rel_keys), jnp.sum(rel_up * rel_up)])
    early_ratio = ratio_of(early)
    late_ratio = ratio_of(jnp.concatenate([late, rel_sums]))
    final_ratio = ratio_of(final)

    def spread(n):
        e, l, f = early_ratio[n], late_ratio[n], final_ratio[n]
        return jnp.concatenate([f, e[0:1], l[0:1], e[1:2], e[2:8], l[1:9]])

    weight_norms, update_norms = spread(0), spread(1)
    fast = early_ratio[2]
    slow = late_ratio[2]
    ffn_in_new = move_matrix(1, ffn_in, in_up, fast[0], "move_in1")
    ffn_in_new = move_matrix(0, ffn_in, ffn_in_new, final_ratio[2][0], "move_in0")
    ffn_out_new = move_matrix(1, ffn_out, out_up, fast[1], "move_out1")
    ffn_out_new = move_matrix(0, ffn_out, ffn_out_new, slow[0], "move_out0")
    conv_factor = jnp.where(jnp.arange(3 * D) < 2 * D, fast[6], fast[7])[None, :]
    vec_factor = jnp.concatenate([jnp.full((KERNEL,), slow[1]), slow[2:8]])[:, None]
    return (
        output.reshape(frames.shape),
        d0.reshape(frames.shape),
        in_grad,
        ffn_in_new,
        in_m,
        in_q,
        out_grad,
        ffn_out_new,
        out_m,
        out_q,
        attn_grad,
        move(attn_proj, attn_up, fast[2:6][:, None, None]),
        attn_m,
        attn_q,
        attn_qo,
        conv_grad,
        move(conv_proj, conv_up, conv_factor),
        conv_m,
        conv_q,
        vec_grad,
        move(vectors, vec_up, vec_factor),
        vec_m,
        vec_q,
        rel_grad,
        move(rel_keys, rel_up, slow[8]),
        rel_m,
        rel_q,
        jnp.stack([weight_norms, update_norms]),
    )


def solution(mesh):
    return jax.shard_map(
        body,
        mesh=mesh,
        in_specs=(
            P(("group", "shard"), None, None),
            P(("group", "shard")),
            P(("group", "shard"), None, None),
            P(None, "shard", None),
            P(None, "shard", None),
            P(None, "shard", None),
            P(None, "shard", None),
            P(None, "shard", None),
            P(None, "shard", None),
            P(None, "shard", None),
            P(None, "shard", None),
            P(None, "shard", None),
            P("shard", None),
            P("shard", None),
            P("shard", None),
            P(None, "shard"),
            P(None, "shard"),
            P(None, "shard"),
            P(),
            P(),
            P(),
        ),
        out_specs=(
            P(("group", "shard"), None, None),
            P(("group", "shard"), None, None),
            P(None, "shard", None),
            P(None, "shard", None),
            P(None, "shard", None),
            P(None, "shard", None),
            P(None, "shard", None),
            P(None, "shard", None),
            P(None, "shard", None),
            P(None, "shard", None),
            P(None, "shard", None),
            P(None, "shard", None),
            P(None, "shard", None),
            P(None, "shard", None),
            P("shard", None),
            P("shard", None),
            P("shard", None),
            P("shard", None),
            P("shard", None),
            P(None, "shard"),
            P(None, "shard"),
            P(None, "shard"),
            P(None, "shard"),
            P(),
            P(),
            P(),
            P(),
            P(),
        ),
        check_vma=False,
    )
```

```python
import math

import jax
import jax.numpy as jnp
from jax import lax
from jax.experimental import pallas as pl
from jax.experimental.pallas import tpu as pltpu
from jax.sharding import PartitionSpec as P

D = 512
FF = 2048
HEADS = 8
HEAD = 64
KERNEL = 31
BACK = 64
AHEAD = 8
RELS = 73
STEP = 10
PIECES = 32
LEAD = 32
FFN_ROWS = 128
ATTN_ROWS = 64
CONV_ROWS = 48

NORM_EPSILON = 1e-05
ADAM_EPSILON = 1e-06
RATIO_EPSILON = 1e-06
BETA_FIRST = 0.9
BETA_SECOND = 0.999
WEIGHT_DECAY = 0.01
LEARN_RATE = 0.5
MASKED_SCORE = -1e30

bf16 = jnp.bfloat16
f32 = jnp.float32
VMEM_LIMIT = 60 * 1024 * 1024


def vmem():
    return pl.BlockSpec(memory_space=pltpu.VMEM)


def smem():
    return pl.BlockSpec(memory_space=pltpu.SMEM)


def shape(dims, kind):
    return jax.ShapeDtypeStruct(dims, kind)


def dot(left, right):
    return jnp.dot(left, right, preferred_element_type=f32)


def dot_rows(left, right):
    return lax.dot_general(left, right, (((0,), (0,)), ((), ())), preferred_element_type=f32)


def dot_cols(left, right):
    return lax.dot_general(left, right, (((1,), (1,)), ((), ())), preferred_element_type=f32)


def stats(values):
    centred = values - jnp.mean(values, axis=-1, keepdims=True)
    scale = lax.rsqrt(jnp.mean(centred * centred, axis=-1, keepdims=True) + NORM_EPSILON)
    return centred * scale, scale


def norm_back(grad, normed, scale, gain):
    grad_gain = jnp.sum(grad * normed, axis=0, keepdims=True)
    scaled = grad * gain
    inner = jnp.mean(scaled * normed, axis=-1, keepdims=True)
    back = scale * (scaled - jnp.mean(scaled, axis=-1, keepdims=True) - normed * inner)
    return back, grad_gain


def logistic(values):
    return 1.0 / (1.0 + jnp.exp(-values))


def slope_of(values, sig):
    return sig * (1.0 + values * (1.0 - sig))


class Plan:
    def __init__(self, groups, shards):
        self.groups, self.shards = groups, shards
        shard_bits = shards.bit_length() - 1
        group_bits = groups.bit_length() - 1
        self.used = min(5 - shard_bits, group_bits)
        self.owned = PIECES // shards
        order = [("group", 0)] + [("shard", b) for b in range(shard_bits)]
        order += [("group", b) for b in range(1, self.used)]
        self.order = order
        self.rest = [("group", b) for b in range(self.used, group_bits)]
        self.shard_bits = [("shard", b) for b in range(shard_bits)]
        self.kept = [step for step in order if step[0] == "group"]

    def piece_bit(self, step):
        return step[1] if step[0] == "group" else self.used + step[1]

    def place(self, piece):
        out = 0
        for step in self.order:
            out = out * 2 + ((piece >> self.piece_bit(step)) & 1)
        return out

    def kept_place(self, piece):
        out = 0
        for step in self.kept:
            out = out * 2 + ((piece >> step[1]) & 1)
        return out


def swap(values, step):
    axis, bit = step
    count = lax.axis_size(axis)
    return lax.ppermute(values, axis, [(i, i ^ (1 << bit)) for i in range(count)])


def add_low(left, right):
    return (left.astype(f32) + right.astype(f32)).astype(bf16)


class Chain:
    def __init__(self, kept, sent, plan):
        self.todo = [("halve", s) for s in plan.order] + [("add", s) for s in plan.rest]
        self.todo += [("keep", s) for s in reversed(plan.kept)]
        self.kept, self.sent = kept, sent

    def start(self):
        if self.todo:
            self.found = swap(self.sent, self.todo[0][1])

    def finish(self):
        if not self.todo:
            return
        kind, _ = self.todo.pop(0)
        if kind == "keep":
            self.kept = jnp.concatenate([self.kept, self.found], axis=0)
            self.sent = self.kept
        elif self.todo[0][0] == "halve":
            half = self.kept.shape[0] // 2
            low = add_low(self.kept[:half], self.found[:half])
            self.sent = add_low(self.kept[half:], self.found[half:])
            self.kept = low
        else:
            self.kept = add_low(self.kept, self.found)
            self.sent = self.kept


class Everywhere:
    def __init__(self, values, plan):
        self.todo = plan.order + plan.rest
        self.kept = self.sent = values

    def start(self):
        if self.todo:
            self.found = swap(self.sent, self.todo[0])

    def finish(self):
        if self.todo:
            self.todo = self.todo[1:]
            self.kept = self.sent = self.kept + self.found


def gate(values, signs):
    held = lax.optimization_barrier((tuple(values), tuple(signs)))
    return held[0]


def beside(chains, run, first, sign):
    chains = [chain for chain in chains if chain.todo]
    (first,) = gate([first], [chain.sent for chain in chains])
    for chain in chains:
        chain.start()
    outs = run(first)
    for chain, value in zip(chains, gate([chain.kept for chain in chains], [outs[sign]])):
        chain.kept = value
    for chain in chains:
        chain.finish()
    return outs


def advance(chains, rounds):
    for _ in range(rounds):
        busy = [chain for chain in chains if chain.todo]
        for chain, value in zip(busy, gate([chain.sent for chain in busy], [])):
            chain.sent = value
        for chain in busy:
            chain.start()
        for chain in busy:
            chain.finish()


def sum_shards(values, plan):
    for step in plan.shard_bits:
        values = values + swap(values, step)
    return values


class Fetch:
    def __init__(self, own, dim, plan, core, layer=None):
        self.own, self.plan, self.dim, self.layer = own, plan, dim, layer
        one = own if layer is None else own[layer]
        if plan.shards == 2:
            half = one.shape[dim] // 2
            self.value = lax.dynamic_slice_in_dim(one, core * half, half, axis=dim).astype(bf16)
        else:
            self.value = lax.all_gather(one.astype(bf16), "shard", axis=dim, tiled=True)

    def near(self):
        if self.plan.shards == 2:
            self.value = swap(self.value, ("shard", 0))

    def far(self):
        if self.plan.shards == 2:
            return (self.own, self.value, swap(self.value, ("group", 0)))
        return (self.value,)


def order(later, signs):
    for fetch, value in zip(later, gate([f.value for f in later], signs)):
        fetch.value = value


def part_specs(parts):
    return [pl.BlockSpec(memory_space=pl.ANY), vmem(), vmem()] if len(parts) == 3 else [vmem()]


def part_scratch(parts):
    if len(parts) == 1:
        return []
    return [pltpu.VMEM(parts[0].shape[1:], f32), pltpu.SemaphoreType.DMA]


def begin(layer, part_refs, extra):
    if len(part_refs) == 1:
        return part_refs, None
    buffer, semaphore = extra
    copy = pltpu.make_async_copy(part_refs[0].at[layer], buffer, semaphore)
    copy.start()
    return (buffer, *part_refs[1:]), copy


def join(place_ref, part_refs, whole_ref, copy=None):
    if len(part_refs) == 1:
        whole_ref[...] = part_refs[0][...]
        return
    own, near, far = part_refs
    rows = own.shape[-2]
    half = rows // 2
    shard, core = place_ref[0], place_ref[1]
    first = pl.multiple_of(shard * rows, half)
    second = pl.multiple_of((1 - shard) * rows + core * half, half)
    third = pl.multiple_of((1 - shard) * rows + (1 - core) * half, half)
    if len(own.shape) == 2:
        whole_ref[pl.ds(second, half), :] = near[...]
        whole_ref[pl.ds(third, half), :] = far[...]
        if copy is not None:
            copy.wait()
        whole_ref[pl.ds(first, rows), :] = own[...].astype(bf16)
    else:
        for k in range(own.shape[0]):
            whole_ref[k, pl.ds(first, rows), :] = own[k].astype(bf16)
            whole_ref[k, pl.ds(second, half), :] = near[k]
            whole_ref[k, pl.ds(third, half), :] = far[k]


def put(out_refs, plan, place_ref, value, row, rows_each, first):
    kept_ref, sent_ref = out_refs
    low = value.astype(bf16)
    core, mine = place_ref[1] == 0, place_ref[2]
    for k in range(0, value.shape[0] // rows_each, 2):
        even = low[k * rows_each : (k + 1) * rows_each]
        odd = low[(k + 1) * rows_each : (k + 2) * rows_each]
        spot = jnp.bitwise_xor(jnp.int32(plan.place(first + k)), jnp.bitwise_and(mine, PIECES // 2 - 1))
        kept_ref[spot, row : row + rows_each, :] = jnp.where(core, even, odd)
        sent_ref[spot, row : row + rows_each, :] = jnp.where(core, odd, even)


def halves(rows):
    return [shape((PIECES // 2, rows, D), bf16)] * 2


def call(kernel, outs, ins, specs, scratch=(), name=None):
    return pl.pallas_call(
        kernel,
        out_shape=list(outs),
        in_specs=specs,
        out_specs=[vmem()] * len(outs),
        scratch_shapes=list(scratch),
        compiler_params=pltpu.CompilerParams(vmem_limit_bytes=VMEM_LIMIT),
        name=name,
    )(*ins)


def load_pair(layer, place_ref, wins, wouts, win, wout, extra):
    split = len(extra) // 2
    in_refs, in_copy = begin(layer, wins, extra[:split])
    out_refs, out_copy = begin(layer, wouts, extra[split:])
    join(place_ref, in_refs, win, in_copy)
    join(place_ref, out_refs, wout, out_copy)


def ffn_ahead(values, gain, win, wout, entry_ref, hidden_ref, slope_ref):
    normed, _ = stats(values)
    entry = (normed * gain).astype(bf16)
    entry_ref[...] = entry
    total = jnp.zeros(values.shape, f32)
    for b in range(FF // D):
        cols = slice(b * D, (b + 1) * D)
        before = dot(entry, win[:, cols])
        sig = logistic(before)
        hidden = (before * sig).astype(bf16)
        hidden_ref[:, cols] = hidden
        slope_ref[:, cols] = slope_of(before, sig).astype(bf16)
        total = total + dot(hidden, wout[cols, :])
    return total


def ffn_behind(grad, values, gain, win, wout, entry_ref, hidden_ref, slope_ref, out_refs, plan, place_ref):
    normed, scale = stats(values)
    entry = entry_ref[...]
    branch = (0.5 * grad).astype(bf16)
    grad_entry = jnp.zeros(values.shape, f32)
    for b in range(FF // D):
        cols = slice(b * D, (b + 1) * D)
        put(out_refs, plan, place_ref, dot_rows(hidden_ref[:, cols], branch), 64, 64, 8 * b)
        grad_before = (dot_cols(branch, wout[cols, :]) * slope_ref[:, cols].astype(f32)).astype(bf16)
        put(out_refs, plan, place_ref, dot_rows(entry, grad_before), 16 * b, 16, 0)
        grad_entry = grad_entry + dot_cols(grad_before, win[:, cols])
    back, grad_gain = norm_back(grad_entry, normed, scale, gain)
    return grad + back, grad_gain


def ffn_first(frames, vec, win_parts, wout_parts, place, plan):
    rows = frames.shape[0]
    n = len(win_parts)

    def kernel(place_ref, x_ref, vec_ref, *rest):
        wins, wouts = rest[:n], rest[n : 2 * n]
        out_ref, entry_ref, hidden_ref, slope_ref, win, wout, *extra = rest[2 * n :]
        load_pair(0, place_ref, wins, wouts, win, wout, extra)
        values = x_ref[...].astype(f32)
        total = ffn_ahead(values, vec_ref[31:32, :], win, wout, entry_ref, hidden_ref, slope_ref)
        out_ref[...] = values + 0.5 * total

    return call(
        kernel,
        [shape((rows, D), f32), shape((rows, D), bf16), shape((rows, FF), bf16), shape((rows, FF), bf16)],
        [place, frames, vec, *win_parts, *wout_parts],
        [smem()] + [vmem()] * 2 + part_specs(win_parts) + part_specs(wout_parts),
        [pltpu.VMEM((D, FF), bf16), pltpu.VMEM((FF, D), bf16)] + part_scratch(win_parts) + part_scratch(wout_parts),
        "ffn_first",
    )


def ffn_last(values, vec, cotangent, lengths, win_parts, wout_parts, place, plan):
    rows = values.shape[0]
    count = lengths.shape[0]
    n = len(win_parts)

    def kernel(place_ref, len_ref, x_ref, vec_ref, cot_ref, *rest):
        wins, wouts = rest[:n], rest[n : 2 * n]
        y_ref, dx_ref, gain_ref, *g_refs = rest[2 * n : 2 * n + 5]
        win, wout, entry_ref, hidden_ref, slope_ref, *extra = rest[2 * n + 5 :]
        load_pair(1, place_ref, wins, wouts, win, wout, extra)
        x = x_ref[...]
        gain = vec_ref[35:36, :]
        total = ffn_ahead(x, gain, win, wout, entry_ref, hidden_ref, slope_ref)
        normed, scale = stats(x + 0.5 * total)
        top = vec_ref[36:37, :]
        y_ref[...] = (normed * top).astype(bf16)
        each = rows // count
        grads = []
        for s in range(count):
            spot = lax.broadcasted_iota(jnp.int32, (each, 1), 0)
            part = cot_ref[s * each : (s + 1) * each, :].astype(f32)
            grads.append(jnp.where(spot < len_ref[s], part, 0.0))
        back, grad_top = norm_back(jnp.concatenate(grads, axis=0), normed, scale, top)
        grad, grad_gain = ffn_behind(
            back, x, gain, win, wout, entry_ref, hidden_ref, slope_ref, g_refs, plan, place_ref
        )
        dx_ref[...] = grad
        gain_ref[...] = jnp.concatenate([grad_gain, grad_top, jnp.zeros((6, D), f32)], axis=0)

    return call(
        kernel,
        [shape((rows, D), bf16), shape((rows, D), f32), shape((8, D), f32), *halves(FFN_ROWS)],
        [place, lengths, values, vec, cotangent, *win_parts, *wout_parts],
        [smem(), smem()] + [vmem()] * 3 + part_specs(win_parts) + part_specs(wout_parts),
        [
            pltpu.VMEM((D, FF), bf16),
            pltpu.VMEM((FF, D), bf16),
            pltpu.VMEM((rows, D), bf16),
            pltpu.VMEM((rows, FF), bf16),
            pltpu.VMEM((rows, FF), bf16),
            *part_scratch(win_parts),
            *part_scratch(wout_parts),
        ],
        "ffn_last",
    )


def ffn_first_out(grad, hidden, slope, wout_parts, place, plan):
    rows = grad.shape[0]
    n = len(wout_parts)

    def kernel(place_ref, grad_ref, hidden_ref, slope_ref, *rest):
        wouts = rest[:n]
        before_ref, *g_refs = rest[n : n + 3]
        wout, *extra = rest[n + 3 :]
        refs, copy = begin(0, wouts, extra)
        join(place_ref, refs, wout, copy)
        branch = (0.5 * grad_ref[...]).astype(bf16)
        for b in range(FF // D):
            cols = slice(b * D, (b + 1) * D)
            put(g_refs, plan, place_ref, dot_rows(hidden_ref[:, cols], branch), 0, 64, 8 * b)
            spread = dot_cols(branch, wout[cols, :])
            before_ref[:, cols] = (spread * slope_ref[:, cols].astype(f32)).astype(bf16)

    return call(
        kernel,
        [shape((rows, FF), bf16), *halves(64)],
        [place, grad, hidden, slope, *wout_parts],
        [smem()] + [vmem()] * 3 + part_specs(wout_parts),
        [pltpu.VMEM((FF, D), bf16)] + part_scratch(wout_parts),
        "ffn_first_out",
    )


def ffn_first_in(grad, frames, vec, entry, before, win_parts, place, plan):
    rows = frames.shape[0]
    n = len(win_parts)

    def kernel(place_ref, grad_ref, x_ref, vec_ref, entry_ref, before_ref, *rest):
        wins = rest[:n]
        dx_ref, gain_ref, *g_refs = rest[n : n + 4]
        win, *extra = rest[n + 4 :]
        refs, copy = begin(0, wins, extra)
        join(place_ref, refs, win, copy)
        low = entry_ref[...]
        grad_entry = jnp.zeros((rows, D), f32)
        for b in range(FF // D):
            cols = slice(b * D, (b + 1) * D)
            put(g_refs, plan, place_ref, dot_rows(low, before_ref[:, cols]), 16 * b, 16, 0)
            grad_entry = grad_entry + dot_cols(before_ref[:, cols], win[:, cols])
        normed, scale = stats(x_ref[...].astype(f32))
        back, grad_gain = norm_back(grad_entry, normed, scale, vec_ref[31:32, :])
        dx_ref[...] = (grad_ref[...] + back).astype(bf16)
        gain_ref[...] = jnp.concatenate([grad_gain, jnp.zeros((7, D), f32)], axis=0)

    return call(
        kernel,
        [shape((rows, D), bf16), shape((8, D), f32), *halves(64)],
        [place, grad, frames, vec, entry, before, *win_parts],
        [smem()] + [vmem()] * 5 + part_specs(win_parts),
        [pltpu.VMEM((D, FF), bf16)] + part_scratch(win_parts),
        "ffn_first_in",
    )


def attend(values, vec, rel_table, lengths, parts, place, plan):
    rows = values.shape[0]
    count = lengths.shape[0]
    each = rows // count
    n = len(parts)
    pairs = HEADS // 2

    def kernel(place_ref, len_ref, x_ref, vec_ref, rel_ref, *rest):
        ws = rest[:n]
        out_ref, entry_ref, qkv_ref, prob_ref, mix_ref, weight, mixed = rest[n:]
        join(place_ref, ws, weight)
        x = x_ref[...]
        normed, _ = stats(x)
        entry = (normed * vec_ref[32:33, :]).astype(bf16)
        entry_ref[...] = entry
        for k in range(3):
            heads = dot(entry, weight[k]).astype(bf16)
            for p in range(pairs):
                qkv_ref[k, p] = heads[:, p * 128 : (p + 1) * 128]
        lane = lax.broadcasted_iota(jnp.int32, (1, 128), 1)
        table = rel_ref[...]
        spot = lax.broadcasted_iota(jnp.int32, (1, each), 1)

        def step(i, carry):
            s = i // pairs
            p = i % pairs
            span = pl.ds(pl.multiple_of(s * each, each), each)
            query = qkv_ref[0, p, span, :]
            keys = qkv_ref[1, p, span, :]
            vals = qkv_ref[2, p, span, :]
            valid = spot < len_ref[s]
            both = []
            for h in range(2):
                mask = (lane < HEAD) if h == 0 else (lane >= HEAD)
                mine = jnp.where(mask, query, jnp.zeros_like(query))
                raw = dot_cols(mine, keys)
                skew = pltpu.roll(dot_cols(mine, table), 0, 1, stride=1, stride_axis=0)[:, :each]
                scores = jnp.where(valid, (raw + skew) * 0.125, MASKED_SCORE)
                grown = jnp.exp(scores - jnp.max(scores, axis=-1, keepdims=True))
                low = (grown * (1.0 / jnp.sum(grown, axis=-1, keepdims=True))).astype(bf16)
                prob_ref[2 * i + h] = low
                both.append(dot(low, vals))
            mixed[p, span, :] = jnp.where(lane < HEAD, both[0], both[1]).astype(bf16)
            return carry

        lax.fori_loop(0, count * pairs, step, 0)
        mix = jnp.concatenate([mixed[p] for p in range(pairs)], axis=1)
        mix_ref[...] = mix
        out_ref[...] = x + dot(mix, weight[3])

    return call(
        kernel,
        [
            shape((rows, D), f32),
            shape((rows, D), bf16),
            shape((3, pairs, rows, 128), bf16),
            shape((count * HEADS, each, each), bf16),
            shape((rows, D), bf16),
        ],
        [place, lengths, values, vec, rel_table, *parts],
        [smem(), smem()] + [vmem()] * (3 + n),
        [pltpu.VMEM((4, D, D), bf16), pltpu.VMEM((pairs, rows, 128), bf16)],
        "attend",
    )


def attend_back(grad, values, vec, kept, rel_table, parts, place, plan, count):
    rows = values.shape[0]
    each = rows // count
    n = len(parts)
    pairs = HEADS // 2
    entry, qkv, prob, mix = kept
    width = rel_table.shape[0]

    def kernel(place_ref, grad_ref, x_ref, vec_ref, entry_ref, qkv_ref, prob_ref, mix_ref, rel_ref, *rest):
        ws = rest[:n]
        dx_ref, gain_ref, rel_out, *g_refs = rest[n : n + 5]
        weight, dmix, dqkv = rest[n + 5 :]
        join(place_ref, ws, weight)
        down = grad_ref[...]
        low = down.astype(bf16)
        put(g_refs, plan, place_ref, dot_rows(mix_ref[...], low), 48, 16, 0)
        spread = dot_cols(low, weight[3]).astype(bf16)
        for p in range(pairs):
            dmix[p] = spread[:, p * 128 : (p + 1) * 128]
        lane = lax.broadcasted_iota(jnp.int32, (1, 128), 1)
        table = rel_ref[...]
        flip = (
            lax.broadcasted_iota(jnp.int32, (each, each), 0)
            + lax.broadcasted_iota(jnp.int32, (each, each), 1)
            == each - 1
        ).astype(bf16)
        rel_out[...] = jnp.zeros_like(rel_out)

        def step(i, carry):
            s = i // pairs
            p = i % pairs
            span = pl.ds(pl.multiple_of(s * each, each), each)
            query = qkv_ref[0, p, span, :]
            keys = qkv_ref[1, p, span, :]
            vals = qkv_ref[2, p, span, :]
            outer = dmix[p, span, :]
            grad_q = jnp.zeros((each, 128), f32)
            grad_k = jnp.zeros((each, 128), f32)
            grad_v = jnp.zeros((each, 128), f32)
            grad_r = jnp.zeros((width, 128), f32)
            for h in range(2):
                mask = (lane < HEAD) if h == 0 else (lane >= HEAD)

                def pick(v):
                    return jnp.where(mask, v, jnp.zeros_like(v))

                dout = pick(outer)
                q_own = pick(query)
                prob_low = prob_ref[2 * i + h]
                prob_wide = prob_low.astype(f32)
                dprob = dot_cols(dout, vals)
                inner = jnp.sum(prob_wide * dprob, axis=-1, keepdims=True)
                dscore = (prob_wide * (dprob - inner)).astype(bf16)
                grad_v = grad_v + dot_rows(prob_low, dout)
                grad_k = grad_k + dot_rows(dscore, q_own)
                turned = dot(flip, dscore)
                wide = jnp.concatenate([turned, jnp.zeros((each, width - each), f32)], axis=1)
                skew = pltpu.roll(wide, width - each + 1, 1, stride=1, stride_axis=0).astype(bf16)
                along = dot(flip, skew).astype(bf16)
                grad_q = grad_q + dot(dscore, pick(keys)) + dot(along, pick(table))
                grad_r = grad_r + dot_rows(along, q_own)
            dqkv[0, p, span, :] = (grad_q * 0.125).astype(bf16)
            dqkv[1, p, span, :] = (grad_k * 0.125).astype(bf16)
            dqkv[2, p, span, :] = grad_v.astype(bf16)
            rel_out[...] += grad_r * 0.125
            return carry

        lax.fori_loop(0, count * pairs, step, 0)
        entry_low = entry_ref[...]
        grad_entry = jnp.zeros((rows, D), f32)
        for k in range(3):
            heads = jnp.concatenate([dqkv[k, p] for p in range(pairs)], axis=1)
            put(g_refs, plan, place_ref, dot_rows(entry_low, heads), 16 * k, 16, 0)
            grad_entry = grad_entry + dot_cols(heads, weight[k])
        normed, scale = stats(x_ref[...])
        back, grad_gain = norm_back(grad_entry, normed, scale, vec_ref[32:33, :])
        dx_ref[...] = down + back
        gain_ref[...] = jnp.concatenate([grad_gain, jnp.zeros((7, D), f32)], axis=0)

    return call(
        kernel,
        [
            shape((rows, D), f32),
            shape((8, D), f32),
            shape((width, 128), f32),
            *halves(ATTN_ROWS),
        ],
        [place, grad, values, vec, entry, qkv, prob, mix, rel_table, *parts],
        [smem()] + [vmem()] * (8 + n),
        [
            pltpu.VMEM((4, D, D), bf16),
            pltpu.VMEM((pairs, rows, 128), bf16),
            pltpu.VMEM((3, pairs, rows, 128), bf16),
        ],
        "attend_back",
    )


def convolve(values, vec, parts, place, plan, count):
    rows = values.shape[0]
    each = rows // count
    n = len(parts)
    cols = D // 128
    chunk = 64

    def kernel(place_ref, x_ref, vec_ref, *rest):
        ws = rest[:n]
        out_ref, entry_ref, gated_ref, sig_ref, conv_ref, act_ref, weight = rest[n:]
        join(place_ref, ws, weight)
        x = x_ref[...]
        normed, _ = stats(x)
        entry = (normed * vec_ref[33:34, :]).astype(bf16)
        entry_ref[...] = entry
        linear = dot(entry, weight[:, :D])
        sig = logistic(dot(entry, weight[:, D : 2 * D]))
        sig_ref[...] = sig
        gated = linear * sig
        for s in range(count):
            for c in range(cols):
                gated_ref[s, c, :LEAD, :] = jnp.zeros((LEAD, 128), f32)
                gated_ref[s, c, LEAD:, :] = gated[s * each : (s + 1) * each, c * 128 : (c + 1) * 128]
        for c in range(cols):
            taps = vec_ref[0:32, c * 128 : (c + 1) * 128]

            def step(i, carry):
                s = i // (each // chunk)
                t = (i % (each // chunk)) * chunk
                total = jnp.zeros((chunk, 128), f32)
                for k in range(KERNEL):
                    total = total + taps[k : k + 1] * gated_ref[s, c, pl.ds(t + k + LEAD - KERNEL + 1, chunk), :]
                conv_ref[pl.ds(pl.multiple_of(i * chunk, chunk), chunk), c * 128 : (c + 1) * 128] = total
                return carry

            lax.fori_loop(0, rows // chunk, step, 0)
        inner, _ = stats(conv_ref[...])
        act = inner * vec_ref[34:35, :]
        low = (act * logistic(act)).astype(bf16)
        act_ref[...] = low
        out_ref[...] = x + dot(low, weight[:, 2 * D :])

    return call(
        kernel,
        [
            shape((rows, D), f32),
            shape((rows, D), bf16),
            shape((count, cols, each + LEAD, 128), f32),
            shape((rows, D), f32),
            shape((rows, D), f32),
            shape((rows, D), bf16),
        ],
        [place, values, vec, *parts],
        [smem()] + [vmem()] * (2 + n),
        [pltpu.VMEM((D, 3 * D), bf16)],
        "convolve",
    )


def convolve_back(grad, values, vec, kept, parts, place, plan, count):
    rows = values.shape[0]
    each = rows // count
    n = len(parts)
    cols = D // 128
    entry, gated, sig, conved, act = kept

    def kernel(place_ref, grad_ref, x_ref, vec_ref, entry_ref, gated_ref, sig_ref, conv_ref, act_ref, *rest):
        ws = rest[:n]
        dx_ref, gain_ref, taps_out, *g_refs = rest[n : n + 5]
        weight, dconv, dgated = rest[n + 5 :]
        join(place_ref, ws, weight)
        down = grad_ref[...]
        low = down.astype(bf16)
        put(g_refs, plan, place_ref, dot_rows(act_ref[...], low), 32, 16, 0)
        inner, inner_scale = stats(conv_ref[...])
        inner_gain = vec_ref[34:35, :]
        act_in = inner * inner_gain
        grad_act = dot_cols(low, weight[:, 2 * D :]) * slope_of(act_in, logistic(act_in))
        grad_conv, gain_inner = norm_back(grad_act, inner, inner_scale, inner_gain)
        for s in range(count):
            for c in range(cols):
                dconv[s, c, :each, :] = grad_conv[s * each : (s + 1) * each, c * 128 : (c + 1) * 128]
                dconv[s, c, each:, :] = jnp.zeros((LEAD, 128), f32)
        for c in range(cols):
            lanes = slice(c * 128, (c + 1) * 128)
            taps = vec_ref[0:32, lanes]

            def step(i, sums):
                s = i // (each // 8)
                t = (i % (each // 8)) * 8
                here = dconv[s, c, pl.ds(pl.multiple_of(t, 8), 8), :]
                total = jnp.zeros((8, 128), f32)
                new = []
                for k in range(KERNEL):
                    new.append(sums[k] + here * gated_ref[s, c, pl.ds(t + k + LEAD - KERNEL + 1, 8), :])
                    total = total + taps[k : k + 1] * dconv[s, c, pl.ds(t + KERNEL - 1 - k, 8), :]
                dgated[pl.ds(pl.multiple_of(i * 8, 8), 8), lanes] = total
                return tuple(new)

            sums = lax.fori_loop(0, rows // 8, step, tuple(jnp.zeros((8, 128), f32) for _ in range(KERNEL)))
            found = [jnp.sum(v, axis=0, keepdims=True) for v in sums]
            taps_out[:, lanes] = jnp.concatenate(found + [jnp.zeros((1, 128), f32)], axis=0)
        grad_gated = dgated[...]
        sig_wide = sig_ref[...]
        linear_sig = jnp.concatenate(
            [
                jnp.concatenate([gated_ref[s, c, LEAD:, :] for c in range(cols)], axis=1)
                for s in range(count)
            ],
            axis=0,
        )
        grad_one = (grad_gated * sig_wide).astype(bf16)
        grad_two = (grad_gated * linear_sig * (1.0 - sig_wide)).astype(bf16)
        entry_low = entry_ref[...]
        put(g_refs, plan, place_ref, dot_rows(entry_low, grad_one), 0, 16, 0)
        put(g_refs, plan, place_ref, dot_rows(entry_low, grad_two), 16, 16, 0)
        grad_entry = dot_cols(grad_one, weight[:, :D]) + dot_cols(grad_two, weight[:, D : 2 * D])
        normed, scale = stats(x_ref[...])
        back, gain_outer = norm_back(grad_entry, normed, scale, vec_ref[33:34, :])
        dx_ref[...] = down + back
        gain_ref[...] = jnp.concatenate([gain_outer, gain_inner, jnp.zeros((6, D), f32)], axis=0)

    return call(
        kernel,
        [
            shape((rows, D), f32),
            shape((8, D), f32),
            shape((32, D), f32),
            *halves(CONV_ROWS),
        ],
        [place, grad, values, vec, entry, gated, sig, conved, act, *parts],
        [smem()] + [vmem()] * (8 + n),
        [
            pltpu.VMEM((D, 3 * D), bf16),
            pltpu.VMEM((count, cols, each + LEAD, 128), f32),
            pltpu.VMEM((rows, D), f32),
        ],
        "convolve_back",
    )


def adam(weight, moment, square, grad):
    new_moment = BETA_FIRST * moment + (1.0 - BETA_FIRST) * grad
    new_square = BETA_SECOND * square + (1.0 - BETA_SECOND) * grad * grad
    first = new_moment * (1.0 / (1.0 - BETA_FIRST**STEP))
    second = new_square * (1.0 / (1.0 - BETA_SECOND**STEP))
    update = first / (jnp.sqrt(second) + ADAM_EPSILON) + WEIGHT_DECAY * weight
    return new_moment, new_square, update


def folded(values):
    squares = jnp.sum((values * values).reshape(-1, values.shape[-1]), axis=0, keepdims=True)
    total = squares[:, :128]
    for c in range(1, values.shape[-1] // 128):
        total = total + squares[:, c * 128 : (c + 1) * 128]
    return total


def update_matrix(layer, pieces, block, spots, states, given, name):
    count = spots.shape[0]
    rows, cols = states[0].shape[1] // count, states[0].shape[2]
    given = given or ()

    def kernel(spot_ref, g0_ref, g1_ref, w_ref, m_ref, q_ref, *rest):
        g_out, u_out, m_out, q_out, sums = rest[len(given) :]

        @pl.when(pl.program_id(0) == 0)
        def _():
            sums[...] = jnp.zeros_like(sums)

        grads = []
        for g_ref in (g0_ref, g1_ref):
            raw = g_ref[0].astype(f32)
            grads.append(jnp.concatenate([raw[k * rows : (k + 1) * rows] for k in range(cols // D)], axis=1))
        grad = jnp.concatenate(grads, axis=0)
        weight = w_ref[0]
        new_moment, new_square, update = adam(weight, m_ref[0], q_ref[0], grad)
        g_out[0] = grad
        u_out[0] = update
        m_out[0] = new_moment
        q_out[0] = new_square
        sums[...] += jnp.concatenate([folded(weight), folded(update), jnp.zeros((6, 128), f32)], axis=0)

    tile = pl.BlockSpec((1, 2 * rows, cols), lambda p, spot: (layer, p, 0))
    return pl.pallas_call(
        kernel,
        out_shape=[shape(states[0].shape, f32)] * 4 + [shape((8, 128), f32)],
        grid_spec=pltpu.PrefetchScalarGridSpec(
            num_scalar_prefetch=1,
            grid=(count // 2,),
            in_specs=[
                pl.BlockSpec((1, 64, D), lambda p, spot: (spot[2 * p], block, 0)),
                pl.BlockSpec((1, 64, D), lambda p, spot: (spot[2 * p + 1], block, 0)),
            ]
            + [tile] * 3
            + [pl.BlockSpec(memory_space=pl.ANY)] * len(given),
            out_specs=[tile] * 4 + [pl.BlockSpec((8, 128), lambda p, spot: (0, 0))],
        ),
        input_output_aliases={6 + k: k for k in range(len(given))},
        compiler_params=pltpu.CompilerParams(vmem_limit_bytes=VMEM_LIMIT),
        name=name,
    )(spots, pieces, pieces, *states, *given)


def move_matrix(layer, weight, update, factor, name):
    _, rows, cols = weight.shape
    steps = 4
    tile = pl.BlockSpec((1, rows // steps, cols), lambda p: (layer, p, 0))

    def kernel(factor_ref, w_ref, u_ref, out_ref):
        out_ref[...] = w_ref[...] - (LEARN_RATE * factor_ref[0]) * u_ref[...]

    return pl.pallas_call(
        kernel,
        out_shape=shape(weight.shape, f32),
        grid=(steps,),
        in_specs=[smem(), tile, tile],
        out_specs=tile,
        input_output_aliases={2: 0},
        name=name,
    )(factor.reshape(1), weight, update)


def update_rest(attn_pieces, conv_pieces, spots, attn, conv):
    count = spots.shape[0]
    rows = 2 * (attn[0].shape[1] // count)

    def kernel(spot_ref, ga0, ga1, gc0, gc1, wa, ma, qa, wc, mc, qc, *outs):
        ga_out, ua_out, ma_out, qa_out, qo_out, gc_out, uc_out, mc_out, qc_out, sums = outs
        index = pl.program_id(0)

        @pl.when(index == 0)
        def _():
            sums[...] = jnp.zeros_like(sums)

        found = []
        for k in range(4):
            grad = jnp.concatenate([g[0, k * 16 : (k + 1) * 16] for g in (ga0, ga1)], axis=0).astype(f32)
            weight = wa[k]
            new_moment, new_square, update = adam(weight, ma[k], qa[k], grad)
            ga_out[k] = grad
            ua_out[k] = update
            ma_out[k] = new_moment
            if k < 3:
                qa_out[k] = new_square
            else:
                qo_out[...] = new_square
            found += [folded(weight), folded(update)]
        for low, high in ((0, 2), (2, 3)):
            lanes = slice(low * D, high * D)
            parts = [
                jnp.concatenate([g[0, k * 16 : (k + 1) * 16] for k in range(low, high)], axis=1) for g in (gc0, gc1)
            ]
            grad = jnp.concatenate(parts, axis=0).astype(f32)
            weight = wc[:, lanes]
            new_moment, new_square, update = adam(weight, mc[:, lanes], qc[:, lanes], grad)
            gc_out[:, lanes] = grad
            uc_out[:, lanes] = update
            mc_out[:, lanes] = new_moment
            qc_out[:, lanes] = new_square
            found += [folded(weight), folded(update)]
        sums[...] += jnp.concatenate(found + [jnp.zeros((4, 128), f32)], axis=0)

    attn_block = pl.BlockSpec((4, rows, D), lambda p, spot: (0, p, 0))
    conv_block = pl.BlockSpec((rows, 3 * D), lambda p, spot: (p, 0))
    three = pl.BlockSpec((3, rows, D), lambda p, spot: (0, p, 0))
    one = pl.BlockSpec((rows, D), lambda p, spot: (p, 0))
    side = attn[0].shape[1]
    return pl.pallas_call(
        kernel,
        out_shape=[shape(attn[0].shape, f32)] * 3
        + [shape((3, side, D), f32), shape((side, D), f32)]
        + [shape(conv[0].shape, f32)] * 4
        + [shape((16, 128), f32)],
        grid_spec=pltpu.PrefetchScalarGridSpec(
            num_scalar_prefetch=1,
            grid=(count // 2,),
            in_specs=[
                pl.BlockSpec((1, height, D), lambda p, spot, k=k: (spot[2 * p + k], 0, 0))
                for height in (ATTN_ROWS, CONV_ROWS)
                for k in range(2)
            ]
            + [attn_block] * 3
            + [conv_block] * 3,
            out_specs=[attn_block] * 3
            + [three, one]
            + [conv_block] * 4
            + [pl.BlockSpec((16, 128), lambda p, spot: (0, 0))],
        ),
        compiler_params=pltpu.CompilerParams(vmem_limit_bytes=VMEM_LIMIT),
        name="update_rest",
    )(spots, attn_pieces, attn_pieces, conv_pieces, conv_pieces, *attn, *conv)


def move(weight, update, factor):
    return weight - LEARN_RATE * factor * update


def ratio_of(sums):
    weight, update = sums[0::2], sums[1::2]
    return jnp.sqrt(weight), jnp.sqrt(update), jnp.sqrt(weight) / jnp.sqrt(update + RATIO_EPSILON)


def body(
    frames,
    lengths,
    cotangent,
    ffn_in,
    ffn_in_moment,
    ffn_in_square,
    ffn_out,
    ffn_out_moment,
    ffn_out_square,
    attn_proj,
    attn_moment,
    attn_square,
    conv_proj,
    conv_moment,
    conv_square,
    vectors,
    vectors_moment,
    vectors_square,
    rel_keys,
    rel_moment,
    rel_square,
):
    groups, shards = lax.axis_size("group"), lax.axis_size("shard")
    plan = Plan(groups, shards)
    group, shard = lax.axis_index("group"), lax.axis_index("shard")
    core = jnp.bitwise_and(group, 1)
    count, each, _ = frames.shape
    mine = jnp.int32(0)
    for step in plan.order:
        bit = jnp.right_shift(group if step[0] == "group" else shard, step[1]) & 1
        mine = mine * 2 + bit
    kept = jnp.int32(0)
    for step in plan.kept:
        kept = kept * 2 + (jnp.right_shift(group, step[1]) & 1)
    spots = jnp.array([plan.kept_place(p) for p in range(plan.owned)], jnp.int32) ^ kept
    place = jnp.stack([shard, core, mine]).astype(jnp.int32)

    win0, wout0, win1, wout1 = (Fetch(w, 0, plan, core, k) for k in range(2) for w in (ffn_in, ffn_out))
    watt, wconv = Fetch(attn_proj, 1, plan, core), Fetch(conv_proj, 0, plan, core)
    win0.near()
    wout0.near()
    vec = lax.all_gather(vectors.astype(bf16), "shard", axis=1, tiled=True) if shards != 2 else None
    if vec is None:
        low = vectors.astype(bf16)
        other = swap(low, ("shard", 0))
        vec = jnp.where(shard == 0, jnp.concatenate([low, other], 1), jnp.concatenate([other, low], 1))
    vec = jnp.concatenate([vec.astype(f32), jnp.zeros((3, D), f32)], axis=0)
    rel_low = rel_keys.astype(bf16)
    table = jnp.concatenate(
        [
            rel_low[BACK:],
            jnp.broadcast_to(rel_low[RELS - 1 :], (each - AHEAD - 1, HEAD)),
            jnp.broadcast_to(rel_low[:1], (each - BACK, HEAD)),
            rel_low[:BACK],
        ],
        axis=0,
    )
    table = jnp.concatenate([table, table], axis=1)

    flat = frames.reshape(count * each, D)
    order((watt, wconv), (win0.value, wout0.value))
    watt.near()
    wconv.near()
    win0, wout0 = win0.far(), wout0.far()
    x1, entry0, hidden0, slope0 = ffn_first(flat, vec, win0, wout0, place, plan)
    order((watt, wconv), (x1,))
    order((win1, wout1), (x1, watt.value, wconv.value))
    watt = watt.far()
    win1.near()
    wout1.near()
    wconv = wconv.far()
    x2, *kept_attn = attend(x1, vec, table, lengths, watt, place, plan)
    order((win1,), (x2,))
    win1 = win1.far()
    x3, *kept_conv = convolve(x2, vec, wconv, place, plan, count)
    order((wout1,), (x3,))
    wout1 = wout1.far()
    output, d3, gains_last, *pieces = ffn_last(
        x3, vec, cotangent.reshape(count * each, D), lengths, win1, wout1, place, plan
    )
    last = Chain(*pieces, plan)
    d2, gains_conv, taps, *pieces = beside(
        [last], lambda d: convolve_back(d, x2, vec, kept_conv, wconv, place, plan, count), d3, 1
    )
    conv = Chain(*pieces, plan)
    d1, gains_attn, rel_wide, *pieces = beside(
        [last, conv], lambda d: attend_back(d, x1, vec, kept_attn, table, watt, place, plan, count), d2, 1
    )
    attn = Chain(*pieces, plan)
    before0, *pieces = beside(
        [last, conv, attn], lambda d: ffn_first_out(d, hidden0, slope0, wout0, place, plan), d1, 0
    )
    first_out = Chain(*pieces, plan)
    d0, gains_first, *pieces = beside(
        [last, conv, attn, first_out], lambda b: ffn_first_in(d1, flat, vec, entry0, b, win0, place, plan), before0, 1
    )
    first_in = Chain(*pieces, plan)

    rel_half = rel_wide[:, :HEAD] + rel_wide[:, HEAD:]
    edge = 2 * each - BACK
    rel_local = jnp.concatenate(
        [
            jnp.sum(rel_half[each : edge + 1], axis=0, keepdims=True),
            rel_half[edge + 1 :],
            rel_half[:AHEAD],
            jnp.sum(rel_half[AHEAD:each], axis=0, keepdims=True),
        ],
        axis=0,
    )
    vec_local = jnp.concatenate(
        [taps[:KERNEL], gains_first[:1], gains_attn[:1], gains_conv[:2], gains_last[:2]], axis=0
    )
    rel_lines = jnp.pad(rel_local.reshape(-1), (0, 10 * D - RELS * HEAD)).reshape(10, D)
    small = Everywhere(jnp.concatenate([vec_local, rel_lines, jnp.zeros((1, D), f32)], axis=0), plan)

    chains = [last, conv, attn, first_out, first_in, small]
    advance(chains, len(last.todo))
    in_states = (ffn_in, ffn_in_moment, ffn_in_square)
    out_states = (ffn_out, ffn_out_moment, ffn_out_square)
    *half_out, sums_out1 = beside(
        chains, lambda v: update_matrix(1, v, 1, spots, out_states, None, "update_out1"), last.kept, -1
    )
    *half_in, sums_in1 = beside(
        chains, lambda v: update_matrix(1, v, 0, spots, in_states, None, "update_in1"), last.kept, -1
    )
    advance(chains, len(attn.todo))
    (attn_grad, attn_up, attn_m, attn_q, attn_qo, conv_grad, conv_up, conv_m, conv_q, sums_rest) = beside(
        chains,
        lambda v: update_rest(
            v,
            conv.kept,
            spots,
            (attn_proj, attn_moment, attn_square),
            (conv_proj, conv_moment, conv_square),
        ),
        attn.kept,
        -1,
    )
    advance(chains, len(first_out.todo))
    out_grad, out_up, out_m, out_q, sums_out0 = beside(
        chains, lambda v: update_matrix(0, v, 0, spots, out_states, half_out, "update_out0"), first_out.kept, -1
    )
    advance(chains, len(first_in.todo))
    in_grad, in_up, in_m, in_q, sums_in0 = update_matrix(
        0, first_in.kept, 0, spots, in_states, half_in, "update_in0"
    )
    small = small.kept
    wide = vectors.shape[1]
    vec_grad = lax.dynamic_slice(small, (0, shard * wide), (KERNEL + 6, wide))
    rel_grad = small[KERNEL + 6 : KERNEL + 16].reshape(-1)[: RELS * HEAD].reshape(RELS, HEAD)
    vec_m, vec_q, vec_up = adam(vectors, vectors_moment, vectors_square, vec_grad)
    rel_m, rel_q, rel_up = adam(rel_keys, rel_moment, rel_square, rel_grad)

    vec_sums = []
    for part in (vectors, vec_up):
        squares = jnp.sum(part * part, axis=1)
        vec_sums.append(jnp.concatenate([jnp.sum(squares[:KERNEL])[None], squares[KERNEL:]]))
    early = sum_shards(jnp.sum(jnp.concatenate([sums_in1[:2], sums_out1[:2], sums_rest[:12]], axis=0), axis=1), plan)
    late = sum_shards(jnp.concatenate([jnp.sum(sums_out0[:2], axis=1), jnp.stack(vec_sums, axis=1).reshape(-1)]), plan)
    final = sum_shards(jnp.sum(sums_in0[:2], axis=1), plan)
    rel_sums = jnp.stack([jnp.sum(rel_keys * rel_keys), jnp.sum(rel_up * rel_up)])
    early_ratio = ratio_of(early)
    late_ratio = ratio_of(jnp.concatenate([late, rel_sums]))
    final_ratio = ratio_of(final)

    def spread(n):
        e, l, f = early_ratio[n], late_ratio[n], final_ratio[n]
        return jnp.concatenate([f, e[0:1], l[0:1], e[1:2], e[2:8], l[1:9]])

    weight_norms, update_norms = spread(0), spread(1)
    fast = early_ratio[2]
    slow = late_ratio[2]
    ffn_in_new = move_matrix(1, ffn_in, in_up, fast[0], "move_in1")
    ffn_in_new = move_matrix(0, ffn_in, ffn_in_new, final_ratio[2][0], "move_in0")
    ffn_out_new = move_matrix(1, ffn_out, out_up, fast[1], "move_out1")
    ffn_out_new = move_matrix(0, ffn_out, ffn_out_new, slow[0], "move_out0")
    conv_factor = jnp.where(jnp.arange(3 * D) < 2 * D, fast[6], fast[7])[None, :]
    vec_factor = jnp.concatenate([jnp.full((KERNEL,), slow[1]), slow[2:8]])[:, None]
    return (
        output.reshape(frames.shape),
        d0.reshape(frames.shape),
        in_grad,
        ffn_in_new,
        in_m,
        in_q,
        out_grad,
        ffn_out_new,
        out_m,
        out_q,
        attn_grad,
        move(attn_proj, attn_up, fast[2:6][:, None, None]),
        attn_m,
        attn_q,
        attn_qo,
        conv_grad,
        move(conv_proj, conv_up, conv_factor),
        conv_m,
        conv_q,
        vec_grad,
        move(vectors, vec_up, vec_factor),
        vec_m,
        vec_q,
        rel_grad,
        move(rel_keys, rel_up, slow[8]),
        rel_m,
        rel_q,
        jnp.stack([weight_norms, update_norms]),
    )


def solution(mesh):
    return jax.shard_map(
        body,
        mesh=mesh,
        in_specs=(
            P(("group", "shard"), None, None),
            P(("group", "shard")),
            P(("group", "shard"), None, None),
            P(None, "shard", None),
            P(None, "shard", None),
            P(None, "shard", None),
            P(None, "shard", None),
            P(None, "shard", None),
            P(None, "shard", None),
            P(None, "shard", None),
            P(None, "shard", None),
            P(None, "shard", None),
            P("shard", None),
            P("shard", None),
            P("shard", None),
            P(None, "shard"),
            P(None, "shard"),
            P(None, "shard"),
            P(),
            P(),
            P(),
        ),
        out_specs=(
            P(("group", "shard"), None, None),
            P(("group", "shard"), None, None),
            P(None, "shard", None),
            P(None, "shard", None),
            P(None, "shard", None),
            P(None, "shard", None),
            P(None, "shard", None),
            P(None, "shard", None),
            P(None, "shard", None),
            P(None, "shard", None),
            P(None, "shard", None),
            P(None, "shard", None),
            P(None, "shard", None),
            P(None, "shard", None),
            P("shard", None),
            P("shard", None),
            P("shard", None),
            P("shard", None),
            P("shard", None),
            P(None, "shard"),
            P(None, "shard"),
            P(None, "shard"),
            P(None, "shard"),
            P(),
            P(),
            P(),
            P(),
            P(),
        ),
        check_vma=False,
    )
```

```python
import math

import jax
import jax.numpy as jnp
from jax import lax
from jax.experimental import pallas as pl
from jax.experimental.pallas import tpu as pltpu
from jax.sharding import PartitionSpec as P

D = 512
FF = 2048
HEADS = 8
HEAD = 64
KERNEL = 31
BACK = 64
AHEAD = 8
RELS = 73
STEP = 10
PIECES = 32
LEAD = 32
FFN_ROWS = 128
ATTN_ROWS = 64
CONV_ROWS = 48

NORM_EPSILON = 1e-05
ADAM_EPSILON = 1e-06
RATIO_EPSILON = 1e-06
BETA_FIRST = 0.9
BETA_SECOND = 0.999
WEIGHT_DECAY = 0.01
LEARN_RATE = 0.5
MASKED_SCORE = -1e30

bf16 = jnp.bfloat16
f32 = jnp.float32
VMEM_LIMIT = 28 * 1024 * 1024
STREAM_LIMIT = 60 * 1024 * 1024


def vmem():
    return pl.BlockSpec(memory_space=pltpu.VMEM)


def smem():
    return pl.BlockSpec(memory_space=pltpu.SMEM)


def shape(dims, kind):
    return jax.ShapeDtypeStruct(dims, kind)


def dot(left, right):
    return jnp.dot(left, right, preferred_element_type=f32)


def dot_rows(left, right):
    return lax.dot_general(left, right, (((0,), (0,)), ((), ())), preferred_element_type=f32)


def dot_cols(left, right):
    return lax.dot_general(left, right, (((1,), (1,)), ((), ())), preferred_element_type=f32)


def stats(values):
    centred = values - jnp.mean(values, axis=-1, keepdims=True)
    scale = lax.rsqrt(jnp.mean(centred * centred, axis=-1, keepdims=True) + NORM_EPSILON)
    return centred * scale, scale


def norm_back(grad, normed, scale, gain):
    grad_gain = jnp.sum(grad * normed, axis=0, keepdims=True)
    scaled = grad * gain
    inner = jnp.mean(scaled * normed, axis=-1, keepdims=True)
    back = scale * (scaled - jnp.mean(scaled, axis=-1, keepdims=True) - normed * inner)
    return back, grad_gain


def logistic(values):
    return 1.0 / (1.0 + jnp.exp(-values))


def slope_of(values, sig):
    return sig * (1.0 + values * (1.0 - sig))


class Plan:
    def __init__(self, groups, shards):
        self.groups, self.shards = groups, shards
        shard_bits = shards.bit_length() - 1
        group_bits = groups.bit_length() - 1
        self.used = min(5 - shard_bits, group_bits)
        self.owned = PIECES // shards
        order = [("group", 0)] + [("shard", b) for b in range(shard_bits)]
        order += [("group", b) for b in range(1, self.used)]
        self.order = order
        self.rest = [("group", b) for b in range(self.used, group_bits)]
        self.shard_bits = [("shard", b) for b in range(shard_bits)]
        self.kept = [step for step in order if step[0] == "group"]

    def piece_bit(self, step):
        return step[1] if step[0] == "group" else self.used + step[1]

    def place(self, piece):
        out = 0
        for step in self.order:
            out = out * 2 + ((piece >> self.piece_bit(step)) & 1)
        return out

    def kept_place(self, piece):
        out = 0
        for step in self.kept:
            out = out * 2 + ((piece >> step[1]) & 1)
        return out


def swap(values, step):
    axis, bit = step
    count = lax.axis_size(axis)
    return lax.ppermute(values, axis, [(i, i ^ (1 << bit)) for i in range(count)])


def add_low(left, right):
    return (left.astype(f32) + right.astype(f32)).astype(bf16)


class Chain:
    def __init__(self, kept, sent, plan):
        self.todo = [("halve", s) for s in plan.order] + [("add", s) for s in plan.rest]
        self.todo += [("keep", s) for s in reversed(plan.kept)]
        self.kept, self.sent = kept, sent

    def start(self):
        if self.todo:
            self.found = swap(self.sent, self.todo[0][1])

    def finish(self):
        if not self.todo:
            return
        kind, _ = self.todo.pop(0)
        if not self.todo:
            self.kept = (self.kept, self.found)
        elif kind == "keep":
            self.kept = jnp.concatenate([self.kept, self.found], axis=0)
            self.sent = self.kept
        elif self.todo[0][0] == "halve":
            half = self.kept.shape[0] // 2
            low = add_low(self.kept[:half], self.found[:half])
            self.sent = add_low(self.kept[half:], self.found[half:])
            self.kept = low
        else:
            self.kept = add_low(self.kept, self.found)
            self.sent = self.kept


def merged(one, two, plan):
    both = Chain(
        jnp.concatenate([one.kept, two.kept], axis=1), jnp.concatenate([one.sent, two.sent], axis=1), plan
    )
    both.todo = list(one.todo)
    return both


class Everywhere:
    def __init__(self, values, plan):
        self.todo = plan.order + plan.rest
        self.kept = self.sent = values

    def start(self):
        if self.todo:
            self.found = swap(self.sent, self.todo[0])

    def finish(self):
        if self.todo:
            self.todo = self.todo[1:]
            self.kept = self.sent = self.kept + self.found


def gate(values, signs):
    held = lax.optimization_barrier((tuple(values), tuple(signs)))
    return held[0]


def beside(chains, run, first, sign):
    chains = [chain for chain in chains if chain.todo]
    first = gate(first, [chain.sent for chain in chains])
    for chain in chains:
        chain.start()
    outs = run(*first)
    for chain, value in zip(chains, gate([chain.kept for chain in chains], [outs[sign]])):
        chain.kept = value
    for chain in chains:
        chain.finish()
    return outs


def advance(chains, rounds):
    for _ in range(rounds):
        busy = [chain for chain in chains if chain.todo]
        for chain, value in zip(busy, gate([chain.sent for chain in busy], [])):
            chain.sent = value
        for chain in busy:
            chain.start()
        for chain in busy:
            chain.finish()


def sum_shards(values, plan):
    for step in plan.shard_bits:
        values = values + swap(values, step)
    return values


def rounded_halves(plan, core, *owns):
    if plan.shards != 2:
        return [None] * len(owns)
    ins, specs, outs, out_specs = [], [], [], []
    for own, dim, layer in owns:
        dims = list(own.shape)
        dims[dim] //= 2
        if layer is not None:
            dims[0] = 1
        axes = len(dims)
        ins.append(own)

        def at(i, core_ref, axes=axes, dim=dim, layer=layer):
            return tuple(core_ref[0] if d == dim else (layer or 0) if d == 0 else 0 for d in range(axes))

        specs.append(pl.BlockSpec(tuple(dims), at))
        outs.append(shape(tuple(dims), bf16))
        out_specs.append(pl.BlockSpec(tuple(dims), lambda i, core_ref, axes=axes: (0,) * axes))

    def kernel(core_ref, *refs):
        for k in range(len(owns)):
            refs[len(owns) + k][...] = refs[k][...].astype(bf16)

    found = pl.pallas_call(
        kernel,
        out_shape=outs,
        grid_spec=pltpu.PrefetchScalarGridSpec(
            num_scalar_prefetch=1, grid=(1,), in_specs=specs, out_specs=out_specs
        ),
        compiler_params=pltpu.CompilerParams(vmem_limit_bytes=STREAM_LIMIT),
        name="rounded_halves",
    )(core.reshape(1).astype(jnp.int32), *ins)
    return [v if layer is None else v[0] for v, (_, _, layer) in zip(found, owns)]


class Fetch:
    def __init__(self, own, dim, plan, half, layer=None):
        self.own, self.plan, self.dim = own, plan, dim
        if plan.shards == 2:
            self.value = half
        else:
            one = own if layer is None else own[layer]
            self.value = lax.all_gather(one.astype(bf16), "shard", axis=dim, tiled=True)

    def near(self):
        if self.plan.shards == 2:
            self.value = swap(self.value, ("shard", 0))

    def far(self):
        if self.plan.shards == 2:
            return (self.own, self.value, swap(self.value, ("group", 0)))
        return (self.value,)


def order(later, signs):
    for fetch, value in zip(later, gate([f.value for f in later], signs)):
        fetch.value = value


def part_specs(parts):
    return [pl.BlockSpec(memory_space=pltpu.HBM), vmem(), vmem()] if len(parts) == 3 else [vmem()]


def part_scratch(parts):
    if len(parts) == 1:
        return []
    return [pltpu.VMEM(parts[0].shape[1:], f32), pltpu.SemaphoreType.DMA]


def begin(layer, part_refs, extra):
    if len(part_refs) == 1:
        return part_refs, None
    buffer, semaphore = extra
    copy = pltpu.make_async_copy(part_refs[0].at[layer], buffer, semaphore)
    copy.start()
    return (buffer, *part_refs[1:]), copy


def join(place_ref, part_refs, whole_ref, copy=None):
    if len(part_refs) == 1:
        whole_ref[...] = part_refs[0][...]
        return
    own, near, far = part_refs
    rows = own.shape[-2]
    half = rows // 2
    shard, core = place_ref[0], place_ref[1]
    first = pl.multiple_of(shard * rows, half)
    second = pl.multiple_of((1 - shard) * rows + core * half, half)
    third = pl.multiple_of((1 - shard) * rows + (1 - core) * half, half)
    if len(own.shape) == 2:
        whole_ref[pl.ds(second, half), :] = near[...]
        whole_ref[pl.ds(third, half), :] = far[...]
        if copy is not None:
            copy.wait()
        whole_ref[pl.ds(first, rows), :] = own[...].astype(bf16)
    else:
        for k in range(own.shape[0]):
            whole_ref[k, pl.ds(first, rows), :] = own[k].astype(bf16)
            whole_ref[k, pl.ds(second, half), :] = near[k]
            whole_ref[k, pl.ds(third, half), :] = far[k]


def put(out_refs, plan, place_ref, value, row, rows_each, first):
    kept_ref, sent_ref = out_refs
    low = value.astype(bf16)
    core, mine = place_ref[1] == 0, place_ref[2]
    for k in range(0, value.shape[0] // rows_each, 2):
        even = low[k * rows_each : (k + 1) * rows_each]
        odd = low[(k + 1) * rows_each : (k + 2) * rows_each]
        spot = jnp.bitwise_xor(jnp.int32(plan.place(first + k)), jnp.bitwise_and(mine, PIECES // 2 - 1))
        kept_ref[spot, row : row + rows_each, :] = jnp.where(core, even, odd)
        sent_ref[spot, row : row + rows_each, :] = jnp.where(core, odd, even)


def halves(rows):
    return [shape((PIECES // 2, rows, D), bf16)] * 2


def call(kernel, outs, ins, specs, scratch=(), name=None):
    return pl.pallas_call(
        kernel,
        out_shape=list(outs),
        in_specs=specs,
        out_specs=[vmem()] * len(outs),
        scratch_shapes=list(scratch),
        compiler_params=pltpu.CompilerParams(vmem_limit_bytes=VMEM_LIMIT),
        name=name,
    )(*ins)


def load_pair(layer, place_ref, wins, wouts, win, wout, extra):
    split = len(extra) // 2
    in_refs, in_copy = begin(layer, wins, extra[:split])
    out_refs, out_copy = begin(layer, wouts, extra[split:])
    join(place_ref, in_refs, win, in_copy)
    join(place_ref, out_refs, wout, out_copy)


def ffn_ahead(values, gain, win, wout, entry_ref, hidden_ref, slope_ref):
    normed, _ = stats(values)
    entry = (normed * gain).astype(bf16)
    entry_ref[...] = entry
    total = jnp.zeros(values.shape, f32)
    for b in range(FF // D):
        cols = slice(b * D, (b + 1) * D)
        before = dot(entry, win[:, cols])
        sig = logistic(before)
        hidden = (before * sig).astype(bf16)
        hidden_ref[:, cols] = hidden
        slope_ref[:, cols] = slope_of(before, sig).astype(bf16)
        total = total + dot(hidden, wout[cols, :])
    return total


def ffn_behind(grad, values, gain, win, wout, entry_ref, hidden_ref, slope_ref, out_refs, plan, place_ref):
    normed, scale = stats(values)
    entry = entry_ref[...]
    branch = (0.5 * grad).astype(bf16)
    grad_entry = jnp.zeros(values.shape, f32)
    for b in range(FF // D):
        cols = slice(b * D, (b + 1) * D)
        put(out_refs, plan, place_ref, dot_rows(hidden_ref[:, cols], branch), 64, 64, 8 * b)
        grad_before = (dot_cols(branch, wout[cols, :]) * slope_ref[:, cols].astype(f32)).astype(bf16)
        put(out_refs, plan, place_ref, dot_rows(entry, grad_before), 16 * b, 16, 0)
        grad_entry = grad_entry + dot_cols(grad_before, win[:, cols])
    back, grad_gain = norm_back(grad_entry, normed, scale, gain)
    return grad + back, grad_gain


def ffn_first_up(frames, vec, win_parts, place):
    rows = frames.shape[0]
    n = len(win_parts)

    def kernel(place_ref, x_ref, vec_ref, *rest):
        wins = rest[:n]
        entry_ref, hidden_ref, slope_ref, win, *extra = rest[n:]
        refs, copy = begin(0, wins, extra)
        normed, _ = stats(x_ref[...].astype(f32))
        entry = (normed * vec_ref[31:32, :]).astype(bf16)
        entry_ref[...] = entry
        join(place_ref, refs, win, copy)
        for b in range(FF // D):
            cols = slice(b * D, (b + 1) * D)
            before = dot(entry, win[:, cols])
            sig = logistic(before)
            hidden_ref[:, cols] = (before * sig).astype(bf16)
            slope_ref[:, cols] = slope_of(before, sig).astype(bf16)

    return call(
        kernel,
        [shape((rows, D), bf16), shape((rows, FF), bf16), shape((rows, FF), bf16)],
        [place, frames, vec, *win_parts],
        [smem()] + [vmem()] * 2 + part_specs(win_parts),
        [pltpu.VMEM((D, FF), bf16)] + part_scratch(win_parts),
        "ffn_first_up",
    )


def ffn_first_down(frames, hidden, wout_parts, place):
    rows = frames.shape[0]
    n = len(wout_parts)

    def kernel(place_ref, x_ref, hidden_ref, *rest):
        wouts = rest[:n]
        out_ref, wout, *extra = rest[n:]
        refs, copy = begin(0, wouts, extra)
        join(place_ref, refs, wout, copy)
        out_ref[...] = x_ref[...].astype(f32) + 0.5 * dot(hidden_ref[...], wout[...])

    return call(
        kernel,
        [shape((rows, D), f32)],
        [place, frames, hidden, *wout_parts],
        [smem()] + [vmem()] * 2 + part_specs(wout_parts),
        [pltpu.VMEM((FF, D), bf16)] + part_scratch(wout_parts),
        "ffn_first_down",
    )[0]


def ffn_last(values, vec, cotangent, lengths, win_parts, wout_parts, place, plan):
    rows = values.shape[0]
    count = lengths.shape[0]
    n = len(win_parts)

    def kernel(place_ref, len_ref, x_ref, vec_ref, cot_ref, *rest):
        wins, wouts = rest[:n], rest[n : 2 * n]
        y_ref, dx_ref, gain_ref, *g_refs = rest[2 * n : 2 * n + 5]
        win, wout, entry_ref, hidden_ref, slope_ref, *extra = rest[2 * n + 5 :]
        load_pair(1, place_ref, wins, wouts, win, wout, extra)
        x = x_ref[...]
        gain = vec_ref[35:36, :]
        total = ffn_ahead(x, gain, win, wout, entry_ref, hidden_ref, slope_ref)
        normed, scale = stats(x + 0.5 * total)
        top = vec_ref[36:37, :]
        y_ref[...] = (normed * top).astype(bf16)
        each = rows // count
        grads = []
        for s in range(count):
            spot = lax.broadcasted_iota(jnp.int32, (each, 1), 0)
            part = cot_ref[s * each : (s + 1) * each, :].astype(f32)
            grads.append(jnp.where(spot < len_ref[s], part, 0.0))
        back, grad_top = norm_back(jnp.concatenate(grads, axis=0), normed, scale, top)
        grad, grad_gain = ffn_behind(
            back, x, gain, win, wout, entry_ref, hidden_ref, slope_ref, g_refs, plan, place_ref
        )
        dx_ref[...] = grad
        gain_ref[...] = jnp.concatenate([grad_gain, grad_top, jnp.zeros((6, D), f32)], axis=0)

    return call(
        kernel,
        [shape((rows, D), bf16), shape((rows, D), f32), shape((8, D), f32), *halves(FFN_ROWS)],
        [place, lengths, values, vec, cotangent, *win_parts, *wout_parts],
        [smem(), smem()] + [vmem()] * 3 + part_specs(win_parts) + part_specs(wout_parts),
        [
            pltpu.VMEM((D, FF), bf16),
            pltpu.VMEM((FF, D), bf16),
            pltpu.VMEM((rows, D), bf16),
            pltpu.VMEM((rows, FF), bf16),
            pltpu.VMEM((rows, FF), bf16),
            *part_scratch(win_parts),
            *part_scratch(wout_parts),
        ],
        "ffn_last",
    )


def ffn_first_out(grad, hidden, slope, wout_parts, place, plan):
    rows = grad.shape[0]
    n = len(wout_parts)

    def kernel(place_ref, grad_ref, hidden_ref, slope_ref, *rest):
        wouts = rest[:n]
        before_ref, *g_refs = rest[n : n + 3]
        wout, *extra = rest[n + 3 :]
        refs, copy = begin(0, wouts, extra)
        join(place_ref, refs, wout, copy)
        branch = (0.5 * grad_ref[...]).astype(bf16)
        for b in range(FF // D):
            cols = slice(b * D, (b + 1) * D)
            put(g_refs, plan, place_ref, dot_rows(hidden_ref[:, cols], branch), 0, 64, 8 * b)
            spread = dot_cols(branch, wout[cols, :])
            before_ref[:, cols] = (spread * slope_ref[:, cols].astype(f32)).astype(bf16)

    return call(
        kernel,
        [shape((rows, FF), bf16), *halves(64)],
        [place, grad, hidden, slope, *wout_parts],
        [smem()] + [vmem()] * 3 + part_specs(wout_parts),
        [pltpu.VMEM((FF, D), bf16)] + part_scratch(wout_parts),
        "ffn_first_out",
    )


def ffn_first_in(grad, frames, vec, entry, before, win_parts, place, plan):
    rows = frames.shape[0]
    n = len(win_parts)

    def kernel(place_ref, grad_ref, x_ref, vec_ref, entry_ref, before_ref, *rest):
        wins = rest[:n]
        dx_ref, gain_ref, *g_refs = rest[n : n + 4]
        win, *extra = rest[n + 4 :]
        refs, copy = begin(0, wins, extra)
        join(place_ref, refs, win, copy)
        low = entry_ref[...]
        grad_entry = jnp.zeros((rows, D), f32)
        for b in range(FF // D):
            cols = slice(b * D, (b + 1) * D)
            put(g_refs, plan, place_ref, dot_rows(low, before_ref[:, cols]), 16 * b, 16, 0)
            grad_entry = grad_entry + dot_cols(before_ref[:, cols], win[:, cols])
        normed, scale = stats(x_ref[...].astype(f32))
        back, grad_gain = norm_back(grad_entry, normed, scale, vec_ref[31:32, :])
        dx_ref[...] = (grad_ref[...] + back).astype(bf16)
        gain_ref[...] = jnp.concatenate([grad_gain, jnp.zeros((7, D), f32)], axis=0)

    return call(
        kernel,
        [shape((rows, D), bf16), shape((8, D), f32), *halves(64)],
        [place, grad, frames, vec, entry, before, *win_parts],
        [smem()] + [vmem()] * 5 + part_specs(win_parts),
        [pltpu.VMEM((D, FF), bf16)] + part_scratch(win_parts),
        "ffn_first_in",
    )


def attend(values, vec, rel_table, lengths, parts, place, plan):
    rows = values.shape[0]
    count = lengths.shape[0]
    each = rows // count
    n = len(parts)
    pairs = HEADS // 2

    def kernel(place_ref, len_ref, x_ref, vec_ref, rel_ref, *rest):
        ws = rest[:n]
        out_ref, entry_ref, qkv_ref, prob_ref, mix_ref, weight, mixed = rest[n:]
        join(place_ref, ws, weight)
        x = x_ref[...]
        normed, _ = stats(x)
        entry = (normed * vec_ref[32:33, :]).astype(bf16)
        entry_ref[...] = entry
        for k in range(3):
            heads = dot(entry, weight[k]).astype(bf16)
            for p in range(pairs):
                qkv_ref[k, p] = heads[:, p * 128 : (p + 1) * 128]
        lane = lax.broadcasted_iota(jnp.int32, (1, 128), 1)
        table = rel_ref[...]
        spot = lax.broadcasted_iota(jnp.int32, (1, each), 1)

        def step(i, carry):
            s = i // pairs
            p = i % pairs
            span = pl.ds(pl.multiple_of(s * each, each), each)
            query = qkv_ref[0, p, span, :]
            keys = qkv_ref[1, p, span, :]
            vals = qkv_ref[2, p, span, :]
            valid = spot < len_ref[s]
            both = []
            for h in range(2):
                mask = (lane < HEAD) if h == 0 else (lane >= HEAD)
                mine = jnp.where(mask, query, jnp.zeros_like(query))
                raw = dot_cols(mine, keys)
                skew = pltpu.roll(dot_cols(mine, table), 0, 1, stride=1, stride_axis=0)[:, :each]
                scores = jnp.where(valid, (raw + skew) * 0.125, MASKED_SCORE)
                grown = jnp.exp(scores - jnp.max(scores, axis=-1, keepdims=True))
                low = (grown * (1.0 / jnp.sum(grown, axis=-1, keepdims=True))).astype(bf16)
                prob_ref[2 * i + h] = low
                both.append(dot(low, vals))
            mixed[p, span, :] = jnp.where(lane < HEAD, both[0], both[1]).astype(bf16)
            return carry

        lax.fori_loop(0, count * pairs, step, 0)
        mix = jnp.concatenate([mixed[p] for p in range(pairs)], axis=1)
        mix_ref[...] = mix
        out_ref[...] = x + dot(mix, weight[3])

    return call(
        kernel,
        [
            shape((rows, D), f32),
            shape((rows, D), bf16),
            shape((3, pairs, rows, 128), bf16),
            shape((count * HEADS, each, each), bf16),
            shape((rows, D), bf16),
        ],
        [place, lengths, values, vec, rel_table, *parts],
        [smem(), smem()] + [vmem()] * (3 + n),
        [pltpu.VMEM((4, D, D), bf16), pltpu.VMEM((pairs, rows, 128), bf16)],
        "attend",
    )


def attend_back(grad, values, vec, kept, rel_table, parts, place, plan, count):
    rows = values.shape[0]
    each = rows // count
    n = len(parts)
    pairs = HEADS // 2
    entry, qkv, prob, mix = kept
    width = rel_table.shape[0]

    def kernel(place_ref, grad_ref, x_ref, vec_ref, entry_ref, qkv_ref, prob_ref, mix_ref, rel_ref, *rest):
        ws = rest[:n]
        dx_ref, gain_ref, rel_out, *g_refs = rest[n : n + 5]
        weight, dmix, dqkv = rest[n + 5 :]
        join(place_ref, ws, weight)
        down = grad_ref[...]
        low = down.astype(bf16)
        put(g_refs, plan, place_ref, dot_rows(mix_ref[...], low), 48, 16, 0)
        spread = dot_cols(low, weight[3]).astype(bf16)
        for p in range(pairs):
            dmix[p] = spread[:, p * 128 : (p + 1) * 128]
        lane = lax.broadcasted_iota(jnp.int32, (1, 128), 1)
        table = rel_ref[...]
        flip = (
            lax.broadcasted_iota(jnp.int32, (each, each), 0)
            + lax.broadcasted_iota(jnp.int32, (each, each), 1)
            == each - 1
        ).astype(bf16)
        rel_out[...] = jnp.zeros_like(rel_out)

        def step(i, carry):
            s = i // pairs
            p = i % pairs
            span = pl.ds(pl.multiple_of(s * each, each), each)
            query = qkv_ref[0, p, span, :]
            keys = qkv_ref[1, p, span, :]
            vals = qkv_ref[2, p, span, :]
            outer = dmix[p, span, :]
            grad_q = jnp.zeros((each, 128), f32)
            grad_k = jnp.zeros((each, 128), f32)
            grad_v = jnp.zeros((each, 128), f32)
            grad_r = jnp.zeros((width, 128), f32)
            for h in range(2):
                mask = (lane < HEAD) if h == 0 else (lane >= HEAD)

                def pick(v):
                    return jnp.where(mask, v, jnp.zeros_like(v))

                dout = pick(outer)
                q_own = pick(query)
                prob_low = prob_ref[2 * i + h]
                prob_wide = prob_low.astype(f32)
                dprob = dot_cols(dout, vals)
                inner = jnp.sum(prob_wide * dprob, axis=-1, keepdims=True)
                dscore = (prob_wide * (dprob - inner)).astype(bf16)
                grad_v = grad_v + dot_rows(prob_low, dout)
                grad_k = grad_k + dot_rows(dscore, q_own)
                turned = dot(flip, dscore)
                wide = jnp.concatenate([turned, jnp.zeros((each, width - each), f32)], axis=1)
                skew = pltpu.roll(wide, width - each + 1, 1, stride=1, stride_axis=0).astype(bf16)
                along = dot(flip, skew).astype(bf16)
                grad_q = grad_q + dot(dscore, pick(keys)) + dot(along, pick(table))
                grad_r = grad_r + dot_rows(along, q_own)
            dqkv[0, p, span, :] = (grad_q * 0.125).astype(bf16)
            dqkv[1, p, span, :] = (grad_k * 0.125).astype(bf16)
            dqkv[2, p, span, :] = grad_v.astype(bf16)
            rel_out[...] += grad_r * 0.125
            return carry

        lax.fori_loop(0, count * pairs, step, 0)
        entry_low = entry_ref[...]
        grad_entry = jnp.zeros((rows, D), f32)
        for k in range(3):
            heads = jnp.concatenate([dqkv[k, p] for p in range(pairs)], axis=1)
            put(g_refs, plan, place_ref, dot_rows(entry_low, heads), 16 * k, 16, 0)
            grad_entry = grad_entry + dot_cols(heads, weight[k])
        normed, scale = stats(x_ref[...])
        back, grad_gain = norm_back(grad_entry, normed, scale, vec_ref[32:33, :])
        dx_ref[...] = down + back
        gain_ref[...] = jnp.concatenate([grad_gain, jnp.zeros((7, D), f32)], axis=0)

    return call(
        kernel,
        [
            shape((rows, D), f32),
            shape((8, D), f32),
            shape((width, 128), f32),
            *halves(ATTN_ROWS),
        ],
        [place, grad, values, vec, entry, qkv, prob, mix, rel_table, *parts],
        [smem()] + [vmem()] * (8 + n),
        [
            pltpu.VMEM((4, D, D), bf16),
            pltpu.VMEM((pairs, rows, 128), bf16),
            pltpu.VMEM((3, pairs, rows, 128), bf16),
        ],
        "attend_back",
    )


def convolve(values, vec, parts, place, plan, count):
    rows = values.shape[0]
    each = rows // count
    n = len(parts)
    cols = D // 128
    chunk = 64

    def kernel(place_ref, x_ref, vec_ref, *rest):
        ws = rest[:n]
        out_ref, entry_ref, gated_ref, sig_ref, conv_ref, act_ref, weight = rest[n:]
        join(place_ref, ws, weight)
        x = x_ref[...]
        normed, _ = stats(x)
        entry = (normed * vec_ref[33:34, :]).astype(bf16)
        entry_ref[...] = entry
        linear = dot(entry, weight[:, :D])
        sig = logistic(dot(entry, weight[:, D : 2 * D]))
        sig_ref[...] = sig
        gated = linear * sig
        for s in range(count):
            for c in range(cols):
                gated_ref[s, c, :LEAD, :] = jnp.zeros((LEAD, 128), f32)
                gated_ref[s, c, LEAD:, :] = gated[s * each : (s + 1) * each, c * 128 : (c + 1) * 128]
        for c in range(cols):
            taps = vec_ref[0:32, c * 128 : (c + 1) * 128]

            def step(i, carry):
                s = i // (each // chunk)
                t = (i % (each // chunk)) * chunk
                total = jnp.zeros((chunk, 128), f32)
                for k in range(KERNEL):
                    total = total + taps[k : k + 1] * gated_ref[s, c, pl.ds(t + k + LEAD - KERNEL + 1, chunk), :]
                conv_ref[pl.ds(pl.multiple_of(i * chunk, chunk), chunk), c * 128 : (c + 1) * 128] = total
                return carry

            lax.fori_loop(0, rows // chunk, step, 0)
        inner, _ = stats(conv_ref[...])
        act = inner * vec_ref[34:35, :]
        low = (act * logistic(act)).astype(bf16)
        act_ref[...] = low
        out_ref[...] = x + dot(low, weight[:, 2 * D :])

    return call(
        kernel,
        [
            shape((rows, D), f32),
            shape((rows, D), bf16),
            shape((count, cols, each + LEAD, 128), f32),
            shape((rows, D), f32),
            shape((rows, D), f32),
            shape((rows, D), bf16),
        ],
        [place, values, vec, *parts],
        [smem()] + [vmem()] * (2 + n),
        [pltpu.VMEM((D, 3 * D), bf16)],
        "convolve",
    )


def convolve_back(grad, values, vec, kept, parts, place, plan, count):
    rows = values.shape[0]
    each = rows // count
    n = len(parts)
    cols = D // 128
    entry, gated, sig, conved, act = kept

    def kernel(place_ref, grad_ref, x_ref, vec_ref, entry_ref, gated_ref, sig_ref, conv_ref, act_ref, *rest):
        ws = rest[:n]
        dx_ref, gain_ref, taps_out, *g_refs = rest[n : n + 5]
        weight, dconv, dgated = rest[n + 5 :]
        join(place_ref, ws, weight)
        down = grad_ref[...]
        low = down.astype(bf16)
        put(g_refs, plan, place_ref, dot_rows(act_ref[...], low), 32, 16, 0)
        inner, inner_scale = stats(conv_ref[...])
        inner_gain = vec_ref[34:35, :]
        act_in = inner * inner_gain
        grad_act = dot_cols(low, weight[:, 2 * D :]) * slope_of(act_in, logistic(act_in))
        grad_conv, gain_inner = norm_back(grad_act, inner, inner_scale, inner_gain)
        for s in range(count):
            for c in range(cols):
                dconv[s, c, :each, :] = grad_conv[s * each : (s + 1) * each, c * 128 : (c + 1) * 128]
                dconv[s, c, each:, :] = jnp.zeros((LEAD, 128), f32)
        for c in range(cols):
            lanes = slice(c * 128, (c + 1) * 128)
            taps = vec_ref[0:32, lanes]

            def step(i, sums):
                s = i // (each // 8)
                t = (i % (each // 8)) * 8
                here = dconv[s, c, pl.ds(pl.multiple_of(t, 8), 8), :]
                total = jnp.zeros((8, 128), f32)
                new = []
                for k in range(KERNEL):
                    new.append(sums[k] + here * gated_ref[s, c, pl.ds(t + k + LEAD - KERNEL + 1, 8), :])
                    total = total + taps[k : k + 1] * dconv[s, c, pl.ds(t + KERNEL - 1 - k, 8), :]
                dgated[pl.ds(pl.multiple_of(i * 8, 8), 8), lanes] = total
                return tuple(new)

            sums = lax.fori_loop(0, rows // 8, step, tuple(jnp.zeros((8, 128), f32) for _ in range(KERNEL)))
            found = [jnp.sum(v, axis=0, keepdims=True) for v in sums]
            taps_out[:, lanes] = jnp.concatenate(found + [jnp.zeros((1, 128), f32)], axis=0)
        grad_gated = dgated[...]
        sig_wide = sig_ref[...]
        linear_sig = jnp.concatenate(
            [
                jnp.concatenate([gated_ref[s, c, LEAD:, :] for c in range(cols)], axis=1)
                for s in range(count)
            ],
            axis=0,
        )
        grad_one = (grad_gated * sig_wide).astype(bf16)
        grad_two = (grad_gated * linear_sig * (1.0 - sig_wide)).astype(bf16)
        entry_low = entry_ref[...]
        put(g_refs, plan, place_ref, dot_rows(entry_low, grad_one), 0, 16, 0)
        put(g_refs, plan, place_ref, dot_rows(entry_low, grad_two), 16, 16, 0)
        grad_entry = dot_cols(grad_one, weight[:, :D]) + dot_cols(grad_two, weight[:, D : 2 * D])
        normed, scale = stats(x_ref[...])
        back, gain_outer = norm_back(grad_entry, normed, scale, vec_ref[33:34, :])
        dx_ref[...] = down + back
        gain_ref[...] = jnp.concatenate([gain_outer, gain_inner, jnp.zeros((6, D), f32)], axis=0)

    return call(
        kernel,
        [
            shape((rows, D), f32),
            shape((8, D), f32),
            shape((32, D), f32),
            *halves(CONV_ROWS),
        ],
        [place, grad, values, vec, entry, gated, sig, conved, act, *parts],
        [smem()] + [vmem()] * (8 + n),
        [
            pltpu.VMEM((D, 3 * D), bf16),
            pltpu.VMEM((count, cols, each + LEAD, 128), f32),
            pltpu.VMEM((rows, D), f32),
        ],
        "convolve_back",
    )


def adam(weight, moment, square, grad):
    new_moment = BETA_FIRST * moment + (1.0 - BETA_FIRST) * grad
    new_square = BETA_SECOND * square + (1.0 - BETA_SECOND) * grad * grad
    first = new_moment * (1.0 / (1.0 - BETA_FIRST**STEP))
    second = new_square * (1.0 / (1.0 - BETA_SECOND**STEP))
    update = first / (jnp.sqrt(second) + ADAM_EPSILON) + WEIGHT_DECAY * weight
    return new_moment, new_square, update


def folded(values):
    squares = jnp.sum((values * values).reshape(-1, values.shape[-1]), axis=0, keepdims=True)
    total = squares[:, :128]
    for c in range(1, values.shape[-1] // 128):
        total = total + squares[:, c * 128 : (c + 1) * 128]
    return total


def update_matrix(layer, pieces, block, spots, states, given, name):
    count = spots.shape[0]
    rows, cols = states[0].shape[1] // count, states[0].shape[2]
    given = given or ()

    half = count // 2

    def kernel(spot_ref, g0_near, g0_far, g1_near, g1_far, w_ref, m_ref, q_ref, *rest):
        g_out, u_out, m_out, q_out, sums = rest[len(given) :]
        index = 2 * pl.program_id(0)

        @pl.when(pl.program_id(0) == 0)
        def _():
            sums[...] = jnp.zeros_like(sums)

        grads = []
        for k, near, far in ((0, g0_near, g0_far), (1, g1_near, g1_far)):
            raw = jnp.where(spot_ref[index + k] < half, near[0], far[0]).astype(f32)
            grads.append(jnp.concatenate([raw[k * rows : (k + 1) * rows] for k in range(cols // D)], axis=1))
        grad = jnp.concatenate(grads, axis=0)
        weight = w_ref[0]
        new_moment, new_square, update = adam(weight, m_ref[0], q_ref[0], grad)
        g_out[0] = grad
        u_out[0] = update
        m_out[0] = new_moment
        q_out[0] = new_square
        sums[...] += jnp.concatenate([folded(weight), folded(update), jnp.zeros((6, 128), f32)], axis=0)

    tile = pl.BlockSpec((1, 2 * rows, cols), lambda p, spot: (layer, p, 0))
    return pl.pallas_call(
        kernel,
        out_shape=[shape(states[0].shape, f32)] * 4 + [shape((8, 128), f32)],
        grid_spec=pltpu.PrefetchScalarGridSpec(
            num_scalar_prefetch=1,
            grid=(count // 2,),
            in_specs=[
                pl.BlockSpec((1, 64, D), lambda p, spot, k=k: (spot[2 * p + k] % half, block, 0))
                for k in (0, 0, 1, 1)
            ]
            + [tile] * 3
            + [pl.BlockSpec(memory_space=pl.ANY)] * len(given),
            out_specs=[tile] * 4 + [pl.BlockSpec((8, 128), lambda p, spot: (0, 0))],
        ),
        input_output_aliases={8 + k: k for k in range(len(given))},
        compiler_params=pltpu.CompilerParams(vmem_limit_bytes=STREAM_LIMIT),
        name=name,
    )(spots, *pieces, *pieces, *states, *given)


def move_layer(layer, win, in_update, in_factor, wout, out_update, out_factor):
    steps = 4
    tiles = [pl.BlockSpec((1, w.shape[1] // steps, w.shape[2]), lambda p: (layer, p, 0)) for w in (win, wout)]

    def kernel(factor_ref, w0, u0, w1, u1, out0, out1):
        out0[...] = w0[...] - (LEARN_RATE * factor_ref[0]) * u0[...]
        out1[...] = w1[...] - (LEARN_RATE * factor_ref[1]) * u1[...]

    return pl.pallas_call(
        kernel,
        out_shape=[shape(win.shape, f32), shape(wout.shape, f32)],
        grid=(steps,),
        in_specs=[smem(), tiles[0], tiles[0], tiles[1], tiles[1]],
        out_specs=tiles,
        input_output_aliases={2: 0, 4: 1},
        compiler_params=pltpu.CompilerParams(vmem_limit_bytes=STREAM_LIMIT),
        name="move_layer",
    )(jnp.stack([in_factor, out_factor]), win, in_update, wout, out_update)


def packed(gains_first, gains_attn, gains_conv, gains_last, taps, rel_wide, each):
    edge = 2 * each - BACK

    def kernel(g0, g1, g2, g4, taps_ref, rel_ref, out_ref, rel):
        out_ref[...] = jnp.zeros_like(out_ref)
        out_ref[0:KERNEL, :] = taps_ref[0:KERNEL, :]
        out_ref[31:32, :] = g0[0:1, :]
        out_ref[32:33, :] = g1[0:1, :]
        out_ref[33:35, :] = g2[0:2, :]
        out_ref[35:37, :] = g4[0:2, :]
        half = rel_ref[:, :HEAD] + rel_ref[:, HEAD:]
        rel[...] = jnp.zeros_like(rel)
        rel[0:1, :] = jnp.sum(half[each : edge + 8] * (lax.broadcasted_iota(jnp.int32, (each - BACK + 8, 1), 0) <= each - BACK), axis=0, keepdims=True)
        rel[0:BACK, :] = rel[0:BACK, :] + half[edge:] * (lax.broadcasted_iota(jnp.int32, (BACK, 1), 0) > 0)
        rel[BACK : BACK + AHEAD, :] = half[:AHEAD]
        rel[RELS - 1 : RELS, :] = jnp.sum(half[AHEAD:each], axis=0, keepdims=True)
        for b in range(5):
            out_ref[40:56, b * HEAD : (b + 1) * HEAD] = rel[b * 16 : b * 16 + 16, :]

    return call(
        kernel,
        [shape((56, D), f32)],
        [gains_first, gains_attn, gains_conv, gains_last, taps, rel_wide],
        [vmem()] * 6,
        [pltpu.VMEM((80, HEAD), f32)],
        "packed",
    )[0]


def update_rest(pieces, spots, attn, conv):
    count = spots.shape[0]
    rows = 2 * (attn[0].shape[1] // count)

    half = count // 2

    def kernel(spot_ref, g0_near, g0_far, g1_near, g1_far, wa, ma, qa, wc, mc, qc, *outs):
        ga_out, ua_out, ma_out, qa_out, qo_out, gc_out, uc_out, mc_out, qc_out, sums = outs
        index = pl.program_id(0)

        @pl.when(index == 0)
        def _():
            sums[...] = jnp.zeros_like(sums)

        raws = [
            jnp.where(spot_ref[2 * index + k] < half, near[0], far[0])
            for k, near, far in ((0, g0_near, g0_far), (1, g1_near, g1_far))
        ]
        found = []
        for k in range(4):
            low = CONV_ROWS + k * 16
            grad = jnp.concatenate([g[low : low + 16] for g in raws], axis=0).astype(f32)
            weight = wa[k]
            new_moment, new_square, update = adam(weight, ma[k], qa[k], grad)
            ga_out[k] = grad
            ua_out[k] = update
            ma_out[k] = new_moment
            if k < 3:
                qa_out[k] = new_square
            else:
                qo_out[...] = new_square
            found += [folded(weight), folded(update)]
        for low, high in ((0, 2), (2, 3)):
            lanes = slice(low * D, high * D)
            parts = [
                jnp.concatenate([g[k * 16 : (k + 1) * 16] for k in range(low, high)], axis=1) for g in raws
            ]
            grad = jnp.concatenate(parts, axis=0).astype(f32)
            weight = wc[:, lanes]
            new_moment, new_square, update = adam(weight, mc[:, lanes], qc[:, lanes], grad)
            gc_out[:, lanes] = grad
            uc_out[:, lanes] = update
            mc_out[:, lanes] = new_moment
            qc_out[:, lanes] = new_square
            found += [folded(weight), folded(update)]
        sums[...] += jnp.concatenate(found + [jnp.zeros((4, 128), f32)], axis=0)

    attn_block = pl.BlockSpec((4, rows, D), lambda p, spot: (0, p, 0))
    conv_block = pl.BlockSpec((rows, 3 * D), lambda p, spot: (p, 0))
    three = pl.BlockSpec((3, rows, D), lambda p, spot: (0, p, 0))
    one = pl.BlockSpec((rows, D), lambda p, spot: (p, 0))
    side = attn[0].shape[1]
    return pl.pallas_call(
        kernel,
        out_shape=[shape(attn[0].shape, f32)] * 3
        + [shape((3, side, D), f32), shape((side, D), f32)]
        + [shape(conv[0].shape, f32)] * 4
        + [shape((16, 128), f32)],
        grid_spec=pltpu.PrefetchScalarGridSpec(
            num_scalar_prefetch=1,
            grid=(count // 2,),
            in_specs=[
                pl.BlockSpec((1, CONV_ROWS + ATTN_ROWS, D), lambda p, spot, k=k: (spot[2 * p + k] % half, 0, 0))
                for k in (0, 0, 1, 1)
            ]
            + [attn_block] * 3
            + [conv_block] * 3,
            out_specs=[attn_block] * 3
            + [three, one]
            + [conv_block] * 4
            + [pl.BlockSpec((16, 128), lambda p, spot: (0, 0))],
        ),
        compiler_params=pltpu.CompilerParams(vmem_limit_bytes=STREAM_LIMIT),
        name="update_rest",
    )(spots, *pieces, *pieces, *attn, *conv)


def move(weight, update, factor):
    return weight - LEARN_RATE * factor * update


def ratio_of(sums):
    weight, update = sums[0::2], sums[1::2]
    return jnp.sqrt(weight), jnp.sqrt(update), jnp.sqrt(weight) / jnp.sqrt(update + RATIO_EPSILON)


def body(
    frames,
    lengths,
    cotangent,
    ffn_in,
    ffn_in_moment,
    ffn_in_square,
    ffn_out,
    ffn_out_moment,
    ffn_out_square,
    attn_proj,
    attn_moment,
    attn_square,
    conv_proj,
    conv_moment,
    conv_square,
    vectors,
    vectors_moment,
    vectors_square,
    rel_keys,
    rel_moment,
    rel_square,
):
    groups, shards = lax.axis_size("group"), lax.axis_size("shard")
    plan = Plan(groups, shards)
    group, shard = lax.axis_index("group"), lax.axis_index("shard")
    core = jnp.bitwise_and(group, 1)
    count, each, _ = frames.shape
    mine = jnp.int32(0)
    for step in plan.order:
        bit = jnp.right_shift(group if step[0] == "group" else shard, step[1]) & 1
        mine = mine * 2 + bit
    kept = jnp.int32(0)
    for step in plan.kept:
        kept = kept * 2 + (jnp.right_shift(group, step[1]) & 1)
    spots = jnp.array([plan.kept_place(p) for p in range(plan.owned)], jnp.int32) ^ kept
    place = jnp.stack([shard, core, mine]).astype(jnp.int32)

    first_halves = rounded_halves(plan, core, (ffn_in, 1, 0), (ffn_out, 1, 0))
    other_halves = rounded_halves(
        plan, core, (attn_proj, 1, None), (conv_proj, 0, None), (ffn_in, 1, 1), (ffn_out, 1, 1)
    )
    win0, wout0 = (Fetch(w, 0, plan, v, 0) for w, v in zip((ffn_in, ffn_out), first_halves))
    watt, wconv = Fetch(attn_proj, 1, plan, other_halves[0]), Fetch(conv_proj, 0, plan, other_halves[1])
    win1, wout1 = (Fetch(w, 0, plan, v, 1) for w, v in zip((ffn_in, ffn_out), other_halves[2:]))
    win0.near()
    vec = lax.all_gather(vectors.astype(bf16), "shard", axis=1, tiled=True) if shards != 2 else None
    if vec is None:
        low = vectors.astype(bf16)
        other = swap(low, ("shard", 0))
        order((wout0,), (other,))
        vec = jnp.where(shard == 0, jnp.concatenate([low, other], 1), jnp.concatenate([other, low], 1))
    vec = jnp.concatenate([vec.astype(f32), jnp.zeros((3, D), f32)], axis=0)
    wout0.near()
    rel_low = rel_keys.astype(bf16)
    table = jnp.concatenate(
        [
            rel_low[BACK:],
            jnp.broadcast_to(rel_low[RELS - 1 :], (each - AHEAD - 1, HEAD)),
            jnp.broadcast_to(rel_low[:1], (each - BACK, HEAD)),
            rel_low[:BACK],
        ],
        axis=0,
    )
    table = jnp.concatenate([table, table], axis=1)

    flat = frames.reshape(count * each, D)
    win0_near = win0.value
    win0 = win0.far()
    entry0, hidden0, slope0 = ffn_first_up(flat, vec, win0, place)
    order((watt, wconv), (wout0.value,))
    order((wout0,), (entry0,))
    watt.near()
    wconv.near()
    wout0 = wout0.far()
    x1 = ffn_first_down(flat, hidden0, wout0, place)
    order((watt,), (x1,))
    order((wconv,), (x1,))
    order((win1, wout1), (watt.value,))
    watt = watt.far()
    win1.near()
    wout1.near()
    wconv = wconv.far()
    x2, *kept_attn = attend(x1, vec, table, lengths, watt, place, plan)
    order((win1,), (x2,))
    win1 = win1.far()
    x3, *kept_conv = convolve(x2, vec, wconv, place, plan, count)
    order((wout1,), (x3,))
    wout1 = wout1.far()
    output, d3, gains_last, *pieces = ffn_last(
        x3, vec, cotangent.reshape(count * each, D), lengths, win1, wout1, place, plan
    )
    last = Chain(*pieces, plan)
    d2, gains_conv, taps, *pieces = beside(
        [last], lambda d: convolve_back(d, x2, vec, kept_conv, wconv, place, plan, count), [d3], 1
    )
    conv = Chain(*pieces, plan)
    d1, gains_attn, rel_wide, *pieces = beside(
        [last, conv], lambda d: attend_back(d, x1, vec, kept_attn, table, watt, place, plan, count), [d2], 1
    )
    attn = Chain(*pieces, plan)
    before0, *pieces = beside(
        [last, conv, attn], lambda d: ffn_first_out(d, hidden0, slope0, wout0, place, plan), [d1], 0
    )
    first_out = Chain(*pieces, plan)
    early = [last, attn, first_out] if len(conv.todo) < len(attn.todo) else [last, conv, attn, first_out]
    d0, gains_first, *pieces = beside(
        early, lambda b: ffn_first_in(d1, flat, vec, entry0, b, win0, place, plan), [before0], 1
    )
    first_in = Chain(*pieces, plan)
    middle = merged(conv, attn, plan)
    small = Everywhere(packed(gains_first, gains_attn, gains_conv, gains_last, taps, rel_wide, each), plan)
    advance([last, middle, first_out, first_in, small], 1)
    advance([last, middle, first_in, small], 1)
    first = merged(first_out, first_in, plan)
    chains = [last, middle, first, small]
    advance(chains, len(last.todo))
    in_states = (ffn_in, ffn_in_moment, ffn_in_square)
    out_states = (ffn_out, ffn_out_moment, ffn_out_square)
    *half_out, sums_out1 = beside(
        chains, lambda *v: update_matrix(1, v, 1, spots, out_states, None, "update_out1"), last.kept, -1
    )
    *half_in, sums_in1 = beside(
        chains, lambda *v: update_matrix(1, v, 0, spots, in_states, None, "update_in1"), last.kept, -1
    )
    advance(chains, len(middle.todo))
    attn_states = (attn_proj, attn_moment, attn_square)
    conv_states = (conv_proj, conv_moment, conv_square)
    (attn_grad, attn_up, attn_m, attn_q, attn_qo, conv_grad, conv_up, conv_m, conv_q, sums_rest) = beside(
        chains, lambda *v: update_rest(v, spots, attn_states, conv_states), middle.kept, -1
    )
    small = small.kept
    wide = vectors.shape[1]
    vec_grad = lax.dynamic_slice(small, (0, shard * wide), (KERNEL + 6, wide))
    rel_grad = jnp.concatenate([small[40:56, b * HEAD : (b + 1) * HEAD] for b in range(5)], axis=0)[:RELS]
    vec_m, vec_q, vec_up = adam(vectors, vectors_moment, vectors_square, vec_grad)
    rel_m, rel_q, rel_up = adam(rel_keys, rel_moment, rel_square, rel_grad)

    vec_sums = []
    for part in (vectors, vec_up):
        squares = jnp.sum(part * part, axis=1)
        vec_sums.append(jnp.concatenate([jnp.sum(squares[:KERNEL])[None], squares[KERNEL:]]))
    early = jnp.sum(jnp.concatenate([sums_in1[:2], sums_out1[:2], sums_rest[:12]], axis=0), axis=1)
    early = sum_shards(jnp.concatenate([early, jnp.stack(vec_sums, axis=1).reshape(-1)]), plan)
    early_ratio = ratio_of(early)
    fast = early_ratio[2]
    half_in[1], half_out[1] = beside(
        chains,
        lambda u: move_layer(1, ffn_in, u, fast[0], ffn_out, half_out[1], fast[1]),
        [half_in[1]],
        0,
    )
    advance(chains, len(first.todo))
    out_grad, out_up, out_m, out_q, sums_out0 = update_matrix(
        0, first.kept, 0, spots, out_states, half_out, "update_out0"
    )
    in_grad, in_up, in_m, in_q, sums_in0 = update_matrix(
        0, first.kept, 1, spots, in_states, half_in, "update_in0"
    )
    final = sum_shards(jnp.sum(jnp.concatenate([sums_in0[:2], sums_out0[:2]], axis=0), axis=1), plan)
    rel_sums = jnp.stack([jnp.sum(rel_keys * rel_keys), jnp.sum(rel_up * rel_up)])
    late_ratio = ratio_of(rel_sums)
    final_ratio = ratio_of(final)

    def spread(n):
        e, l, f = early_ratio[n], late_ratio[n], final_ratio[n]
        return jnp.concatenate([f[0:1], e[0:1], f[1:2], e[1:2], e[2:15], l[0:1]])

    weight_norms, update_norms = spread(0), spread(1)
    ffn_in_new, ffn_out_new = move_layer(
        0, ffn_in, in_up, final_ratio[2][0], ffn_out, out_up, final_ratio[2][1]
    )
    conv_factor = jnp.where(jnp.arange(3 * D) < 2 * D, fast[6], fast[7])[None, :]
    vec_factor = jnp.concatenate([jnp.full((KERNEL,), fast[8]), fast[9:15]])[:, None]
    return (
        output.reshape(frames.shape),
        d0.reshape(frames.shape),
        in_grad,
        ffn_in_new,
        in_m,
        in_q,
        out_grad,
        ffn_out_new,
        out_m,
        out_q,
        attn_grad,
        move(attn_proj, attn_up, fast[2:6][:, None, None]),
        attn_m,
        attn_q,
        attn_qo,
        conv_grad,
        move(conv_proj, conv_up, conv_factor),
        conv_m,
        conv_q,
        vec_grad,
        move(vectors, vec_up, vec_factor),
        vec_m,
        vec_q,
        rel_grad,
        move(rel_keys, rel_up, late_ratio[2][0]),
        rel_m,
        rel_q,
        jnp.stack([weight_norms, update_norms]),
    )


def solution(mesh):
    return jax.shard_map(
        body,
        mesh=mesh,
        in_specs=(
            P(("group", "shard"), None, None),
            P(("group", "shard")),
            P(("group", "shard"), None, None),
            P(None, "shard", None),
            P(None, "shard", None),
            P(None, "shard", None),
            P(None, "shard", None),
            P(None, "shard", None),
            P(None, "shard", None),
            P(None, "shard", None),
            P(None, "shard", None),
            P(None, "shard", None),
            P("shard", None),
            P("shard", None),
            P("shard", None),
            P(None, "shard"),
            P(None, "shard"),
            P(None, "shard"),
            P(),
            P(),
            P(),
        ),
        out_specs=(
            P(("group", "shard"), None, None),
            P(("group", "shard"), None, None),
            P(None, "shard", None),
            P(None, "shard", None),
            P(None, "shard", None),
            P(None, "shard", None),
            P(None, "shard", None),
            P(None, "shard", None),
            P(None, "shard", None),
            P(None, "shard", None),
            P(None, "shard", None),
            P(None, "shard", None),
            P(None, "shard", None),
            P(None, "shard", None),
            P("shard", None),
            P("shard", None),
            P("shard", None),
            P("shard", None),
            P("shard", None),
            P(None, "shard"),
            P(None, "shard"),
            P(None, "shard"),
            P(None, "shard"),
            P(),
            P(),
            P(),
            P(),
            P(),
        ),
        check_vma=False,
    )
```

```python
import math

import jax
import jax.numpy as jnp
from jax import lax
from jax.experimental import pallas as pl
from jax.experimental.pallas import tpu as pltpu
from jax.sharding import PartitionSpec as P

D = 512
FF = 2048
HEADS = 8
HEAD = 64
KERNEL = 31
BACK = 64
AHEAD = 8
RELS = 73
STEP = 10
PIECES = 32
LEAD = 32
FFN_ROWS = 128
ATTN_ROWS = 64
CONV_ROWS = 48

NORM_EPSILON = 1e-05
ADAM_EPSILON = 1e-06
RATIO_EPSILON = 1e-06
BETA_FIRST = 0.9
BETA_SECOND = 0.999
WEIGHT_DECAY = 0.01
LEARN_RATE = 0.5
MASKED_SCORE = -1e30

bf16 = jnp.bfloat16
f32 = jnp.float32
VMEM_LIMIT = 24 * 1024 * 1024
STREAM_LIMIT = 60 * 1024 * 1024


def vmem():
    return pl.BlockSpec(memory_space=pltpu.VMEM)


def smem():
    return pl.BlockSpec(memory_space=pltpu.SMEM)


def shape(dims, kind):
    return jax.ShapeDtypeStruct(dims, kind)


def dot(left, right):
    return jnp.dot(left, right, preferred_element_type=f32)


def dot_rows(left, right):
    return lax.dot_general(left, right, (((0,), (0,)), ((), ())), preferred_element_type=f32)


def dot_cols(left, right):
    return lax.dot_general(left, right, (((1,), (1,)), ((), ())), preferred_element_type=f32)


def stats(values):
    centred = values - jnp.mean(values, axis=-1, keepdims=True)
    scale = lax.rsqrt(jnp.mean(centred * centred, axis=-1, keepdims=True) + NORM_EPSILON)
    return centred * scale, scale


def norm_back(grad, normed, scale, gain):
    grad_gain = jnp.sum(grad * normed, axis=0, keepdims=True)
    scaled = grad * gain
    inner = jnp.mean(scaled * normed, axis=-1, keepdims=True)
    back = scale * (scaled - jnp.mean(scaled, axis=-1, keepdims=True) - normed * inner)
    return back, grad_gain


def logistic(values):
    return 1.0 / (1.0 + jnp.exp(-values))


def slope_of(values, sig):
    return sig * (1.0 + values * (1.0 - sig))


class Plan:
    def __init__(self, groups, shards):
        self.groups, self.shards = groups, shards
        shard_bits = shards.bit_length() - 1
        group_bits = groups.bit_length() - 1
        self.used = min(5 - shard_bits, group_bits)
        self.owned = PIECES // shards
        order = [("group", 0)] + [("shard", b) for b in range(shard_bits)]
        order += [("group", b) for b in range(1, self.used)]
        self.order = order
        self.rest = [("group", b) for b in range(self.used, group_bits)]
        self.shard_bits = [("shard", b) for b in range(shard_bits)]
        self.kept = [step for step in order if step[0] == "group"]

    def piece_bit(self, step):
        return step[1] if step[0] == "group" else self.used + step[1]

    def place(self, piece):
        out = 0
        for step in self.order:
            out = out * 2 + ((piece >> self.piece_bit(step)) & 1)
        return out

    def kept_place(self, piece):
        out = 0
        for step in self.kept:
            out = out * 2 + ((piece >> step[1]) & 1)
        return out


def swap(values, step):
    axis, bit = step
    count = lax.axis_size(axis)
    return lax.ppermute(values, axis, [(i, i ^ (1 << bit)) for i in range(count)])


def add_low(left, right):
    return (left.astype(f32) + right.astype(f32)).astype(bf16)


class Chain:
    def __init__(self, kept, sent, plan):
        order, back = list(plan.order), list(reversed(plan.kept))
        self.todo = [("halve", step) for step in order]
        self.todo += [("add", step) for step in plan.rest] + [("keep", step) for step in back]
        self.kept, self.sent = kept, (sent,)

    def start(self):
        if self.todo:
            self.found = swap(self.sent[0], self.todo[0][1])

    def finish(self):
        if not self.todo:
            return
        kind, _ = self.todo.pop(0)
        coming = self.todo[0][0] if self.todo else None
        if kind == "keep":
            if coming is None:
                self.kept = (self.kept, self.found)
            else:
                self.kept = jnp.concatenate([self.kept, self.found], axis=0)
                self.sent = (self.kept,)
        elif coming == "halve":
            half = self.kept.shape[0] // 2
            low = add_low(self.kept[:half], self.found[:half])
            self.sent = (add_low(self.kept[half:], self.found[half:]),)
            self.kept = low
        else:
            self.kept = add_low(self.kept, self.found)
            self.sent = (self.kept,)


def merged(one, two, plan):
    both = Chain(
        jnp.concatenate([one.kept, two.kept], axis=1),
        jnp.concatenate([one.sent[0], two.sent[0]], axis=1),
        plan,
    )
    both.todo = list(one.todo)
    return both


class Everywhere:
    def __init__(self, values, plan):
        self.todo = plan.order + plan.rest
        self.kept, self.sent = values, (values,)

    def start(self):
        if self.todo:
            self.found = swap(self.sent[0], self.todo[0])

    def finish(self):
        if self.todo:
            self.todo = self.todo[1:]
            self.kept = self.kept + self.found
            self.sent = (self.kept,)


def gate(values, signs):
    held = lax.optimization_barrier((tuple(values), tuple(signs)))
    return held[0]


def beside(chains, run, first, sign):
    chains = [chain for chain in chains if chain.todo]
    first = gate(first, [v for chain in chains for v in chain.sent])
    for chain in chains:
        chain.start()
    outs = run(*first)
    for chain, value in zip(chains, gate([chain.kept for chain in chains], [outs[sign]])):
        chain.kept = value
    for chain in chains:
        chain.finish()
    return outs


def advance(chains, rounds):
    for _ in range(rounds):
        busy = [chain for chain in chains if chain.todo]
        for chain, value in zip(busy, gate([chain.sent for chain in busy], [])):
            chain.sent = tuple(value)
        for chain in busy:
            chain.start()
        for chain in busy:
            chain.finish()


def sum_shards(values, plan):
    for step in plan.shard_bits:
        values = values + swap(values, step)
    return values


def rounded_halves(plan, core, *owns):
    if plan.shards != 2:
        return [None] * len(owns)
    ins, specs, outs, out_specs = [], [], [], []
    for own, dim, layer in owns:
        dims = list(own.shape)
        dims[dim] //= 2
        if layer is not None:
            dims[0] = 1
        axes = len(dims)
        ins.append(own)

        def at(i, core_ref, axes=axes, dim=dim, layer=layer):
            return tuple(core_ref[0] if d == dim else (layer or 0) if d == 0 else 0 for d in range(axes))

        specs.append(pl.BlockSpec(tuple(dims), at))
        outs.append(shape(tuple(dims), bf16))
        out_specs.append(pl.BlockSpec(tuple(dims), lambda i, core_ref, axes=axes: (0,) * axes))

    def kernel(core_ref, *refs):
        for k in range(len(owns)):
            refs[len(owns) + k][...] = refs[k][...].astype(bf16)

    found = pl.pallas_call(
        kernel,
        out_shape=outs,
        grid_spec=pltpu.PrefetchScalarGridSpec(
            num_scalar_prefetch=1, grid=(1,), in_specs=specs, out_specs=out_specs
        ),
        compiler_params=pltpu.CompilerParams(vmem_limit_bytes=STREAM_LIMIT),
        name="rounded_halves",
    )(core.reshape(1).astype(jnp.int32), *ins)
    return [v if layer is None else v[0] for v, (_, _, layer) in zip(found, owns)]


def rounded_rows(plan, core, ffn_in, ffn_out, attn_proj, conv_proj):
    if plan.shards != 2:
        return [None] * 6, [None] * 4
    owns = [(ffn_in, 0), (ffn_out, 0), (ffn_in, 1), (ffn_out, 1)]
    outs = [shape(w.shape[1:], bf16) for w, _ in owns] + [shape(attn_proj.shape, bf16), shape(conv_proj.shape, bf16)]
    halved = [outs[4], outs[5], outs[2], outs[3]]
    for v in halved:
        dims = list(v.shape)
        dims[-2] //= 2
        outs.append(shape(tuple(dims), bf16))

    def kernel(core_ref, in_ref, out_ref, attn_ref, conv_ref, *refs):
        rows = refs[:6]
        for layer in range(2):
            rows[2 * layer][...] = in_ref[layer].astype(bf16)
            rows[2 * layer + 1][...] = out_ref[layer].astype(bf16)
        rows[4][...] = attn_ref[...].astype(bf16)
        rows[5][...] = conv_ref[...].astype(bf16)
        for source, half_ref in zip((rows[4], rows[5], rows[2], rows[3]), refs[6:]):
            half = half_ref.shape[-2]
            span = pl.ds(pl.multiple_of(core_ref[0] * half, half), half)
            half_ref[...] = source[:, span, :] if len(half_ref.shape) == 3 else source[span, :]

    found = call(
        kernel,
        outs,
        [core.reshape(1).astype(jnp.int32), ffn_in, ffn_out, attn_proj, conv_proj],
        [smem()] + [vmem()] * 4,
        (),
        "rounded_rows",
    )
    return found[:6], found[6:]


class Fetch:
    def __init__(self, own, dim, plan, rows, half, layer=None):
        self.own, self.plan, self.dim = rows, plan, dim
        if plan.shards == 2:
            self.value = half
        else:
            one = own if layer is None else own[layer]
            self.value = lax.all_gather(one.astype(bf16), "shard", axis=dim, tiled=True)

    def near(self):
        if self.plan.shards == 2:
            self.value = swap(self.value, ("shard", 0))

    def far(self):
        if self.plan.shards == 2:
            return (self.own, self.value, swap(self.value, ("group", 0)))
        return (self.value,)


def order(later, signs):
    for fetch, value in zip(later, gate([f.value for f in later], signs)):
        fetch.value = value


def join(place_ref, part_refs, whole_ref):
    if len(part_refs) == 1:
        whole_ref[...] = part_refs[0][...]
        return
    own, near, far = part_refs
    rows = own.shape[-2]
    half = rows // 2
    shard, core = place_ref[0], place_ref[1]
    first = pl.multiple_of(shard * rows, half)
    second = pl.multiple_of((1 - shard) * rows + core * half, half)
    third = pl.multiple_of((1 - shard) * rows + (1 - core) * half, half)
    if len(own.shape) == 2:
        whole_ref[pl.ds(second, half), :] = near[...]
        whole_ref[pl.ds(third, half), :] = far[...]
        whole_ref[pl.ds(first, rows), :] = own[...]
    else:
        for k in range(own.shape[0]):
            whole_ref[k, pl.ds(first, rows), :] = own[k]
            whole_ref[k, pl.ds(second, half), :] = near[k]
            whole_ref[k, pl.ds(third, half), :] = far[k]


def put(out_refs, plan, place_ref, value, row, rows_each, first):
    kept_ref, sent_ref = out_refs
    low = value.astype(bf16)
    core, mine = place_ref[1] == 0, place_ref[2]
    for k in range(0, value.shape[0] // rows_each, 2):
        even = low[k * rows_each : (k + 1) * rows_each]
        odd = low[(k + 1) * rows_each : (k + 2) * rows_each]
        spot = jnp.bitwise_xor(jnp.int32(plan.place(first + k)), jnp.bitwise_and(mine, PIECES // 2 - 1))
        kept_ref[spot, row : row + rows_each, :] = jnp.where(core, even, odd)
        sent_ref[spot, row : row + rows_each, :] = jnp.where(core, odd, even)


def halves(rows):
    return [shape((PIECES // 2, rows, D), bf16)] * 2


def call(kernel, outs, ins, specs, scratch=(), name=None):
    return pl.pallas_call(
        kernel,
        out_shape=list(outs),
        in_specs=specs,
        out_specs=[vmem()] * len(outs),
        scratch_shapes=list(scratch),
        compiler_params=pltpu.CompilerParams(vmem_limit_bytes=VMEM_LIMIT),
        name=name,
    )(*ins)


def ffn_ahead(values, gain, win, wout, entry_ref, hidden_ref, slope_ref):
    normed, _ = stats(values)
    entry = (normed * gain).astype(bf16)
    entry_ref[...] = entry
    total = jnp.zeros(values.shape, f32)
    for b in range(FF // D):
        cols = slice(b * D, (b + 1) * D)
        before = dot(entry, win[:, cols])
        sig = logistic(before)
        hidden = (before * sig).astype(bf16)
        hidden_ref[:, cols] = hidden
        slope_ref[:, cols] = slope_of(before, sig).astype(bf16)
        total = total + dot(hidden, wout[cols, :])
    return total


def ffn_behind(grad, values, gain, win, wout, entry_ref, hidden_ref, slope_ref, out_refs, plan, place_ref):
    normed, scale = stats(values)
    entry = entry_ref[...]
    branch = (0.5 * grad).astype(bf16)
    grad_entry = jnp.zeros(values.shape, f32)
    for b in range(FF // D):
        cols = slice(b * D, (b + 1) * D)
        put(out_refs, plan, place_ref, dot_rows(hidden_ref[:, cols], branch), 64, 64, 8 * b)
        grad_before = (dot_cols(branch, wout[cols, :]) * slope_ref[:, cols].astype(f32)).astype(bf16)
        put(out_refs, plan, place_ref, dot_rows(entry, grad_before), 16 * b, 16, 0)
        grad_entry = grad_entry + dot_cols(grad_before, win[:, cols])
    back, grad_gain = norm_back(grad_entry, normed, scale, gain)
    return grad + back, grad_gain


def ffn_first_up(frames, vec, win_parts, place):
    rows = frames.shape[0]
    n = len(win_parts)

    def kernel(place_ref, x_ref, vec_ref, *rest):
        wins = rest[:n]
        entry_ref, hidden_ref, slope_ref, win = rest[n:]
        normed, _ = stats(x_ref[...].astype(f32))
        entry = (normed * vec_ref[31:32, :]).astype(bf16)
        entry_ref[...] = entry
        join(place_ref, wins, win)
        for b in range(FF // D):
            cols = slice(b * D, (b + 1) * D)
            before = dot(entry, win[:, cols])
            sig = logistic(before)
            hidden_ref[:, cols] = (before * sig).astype(bf16)
            slope_ref[:, cols] = slope_of(before, sig).astype(bf16)

    return call(
        kernel,
        [shape((rows, D), bf16), shape((rows, FF), bf16), shape((rows, FF), bf16)],
        [place, frames, vec, *win_parts],
        [smem()] + [vmem()] * 2 + [vmem()] * n,
        [pltpu.VMEM((D, FF), bf16)],
        "ffn_first_up",
    )


def ffn_first_down(frames, hidden, wout_parts, place):
    rows = frames.shape[0]
    n = len(wout_parts)

    def kernel(place_ref, x_ref, hidden_ref, *rest):
        wouts = rest[:n]
        out_ref, wout = rest[n:]
        join(place_ref, wouts, wout)
        out_ref[...] = x_ref[...].astype(f32) + 0.5 * dot(hidden_ref[...], wout[...])

    return call(
        kernel,
        [shape((rows, D), f32)],
        [place, frames, hidden, *wout_parts],
        [smem()] + [vmem()] * 2 + [vmem()] * n,
        [pltpu.VMEM((FF, D), bf16)],
        "ffn_first_down",
    )[0]


def ffn_last(values, vec, cotangent, lengths, win_parts, wout_parts, place, plan):
    rows = values.shape[0]
    count = lengths.shape[0]
    n = len(win_parts)

    def kernel(place_ref, len_ref, x_ref, vec_ref, cot_ref, *rest):
        wins, wouts = rest[:n], rest[n : 2 * n]
        y_ref, dx_ref, gain_ref, *g_refs = rest[2 * n : 2 * n + 5]
        win, wout, entry_ref, hidden_ref, slope_ref = rest[2 * n + 5 :]
        join(place_ref, wins, win)
        join(place_ref, wouts, wout)
        x = x_ref[...]
        gain = vec_ref[35:36, :]
        total = ffn_ahead(x, gain, win, wout, entry_ref, hidden_ref, slope_ref)
        normed, scale = stats(x + 0.5 * total)
        top = vec_ref[36:37, :]
        y_ref[...] = (normed * top).astype(bf16)
        each = rows // count
        grads = []
        for s in range(count):
            spot = lax.broadcasted_iota(jnp.int32, (each, 1), 0)
            part = cot_ref[s * each : (s + 1) * each, :].astype(f32)
            grads.append(jnp.where(spot < len_ref[s], part, 0.0))
        back, grad_top = norm_back(jnp.concatenate(grads, axis=0), normed, scale, top)
        grad, grad_gain = ffn_behind(
            back, x, gain, win, wout, entry_ref, hidden_ref, slope_ref, g_refs, plan, place_ref
        )
        dx_ref[...] = grad
        gain_ref[...] = jnp.concatenate([grad_gain, grad_top, jnp.zeros((6, D), f32)], axis=0)

    return call(
        kernel,
        [shape((rows, D), bf16), shape((rows, D), f32), shape((8, D), f32), *halves(FFN_ROWS)],
        [place, lengths, values, vec, cotangent, *win_parts, *wout_parts],
        [smem(), smem()] + [vmem()] * 3 + [vmem()] * (2 * n),
        [
            pltpu.VMEM((D, FF), bf16),
            pltpu.VMEM((FF, D), bf16),
            pltpu.VMEM((rows, D), bf16),
            pltpu.VMEM((rows, FF), bf16),
            pltpu.VMEM((rows, FF), bf16),
        ],
        "ffn_last",
    )


def ffn_first_out(grad, hidden, slope, wout_parts, place, plan):
    rows = grad.shape[0]
    n = len(wout_parts)

    def kernel(place_ref, grad_ref, hidden_ref, slope_ref, *rest):
        wouts = rest[:n]
        before_ref, *g_refs = rest[n : n + 3]
        (wout,) = rest[n + 3 :]
        join(place_ref, wouts, wout)
        branch = (0.5 * grad_ref[...]).astype(bf16)
        for b in range(FF // D):
            cols = slice(b * D, (b + 1) * D)
            put(g_refs, plan, place_ref, dot_rows(hidden_ref[:, cols], branch), 0, 64, 8 * b)
            spread = dot_cols(branch, wout[cols, :])
            before_ref[:, cols] = (spread * slope_ref[:, cols].astype(f32)).astype(bf16)

    return call(
        kernel,
        [shape((rows, FF), bf16), *halves(64)],
        [place, grad, hidden, slope, *wout_parts],
        [smem()] + [vmem()] * 3 + [vmem()] * n,
        [pltpu.VMEM((FF, D), bf16)],
        "ffn_first_out",
    )


def ffn_first_in(grad, frames, vec, entry, before, win_parts, place, plan):
    rows = frames.shape[0]
    n = len(win_parts)

    def kernel(place_ref, grad_ref, x_ref, vec_ref, entry_ref, before_ref, *rest):
        wins = rest[:n]
        dx_ref, gain_ref, *g_refs = rest[n : n + 4]
        (win,) = rest[n + 4 :]
        join(place_ref, wins, win)
        low = entry_ref[...]
        grad_entry = jnp.zeros((rows, D), f32)
        for b in range(FF // D):
            cols = slice(b * D, (b + 1) * D)
            put(g_refs, plan, place_ref, dot_rows(low, before_ref[:, cols]), 16 * b, 16, 0)
            grad_entry = grad_entry + dot_cols(before_ref[:, cols], win[:, cols])
        normed, scale = stats(x_ref[...].astype(f32))
        back, grad_gain = norm_back(grad_entry, normed, scale, vec_ref[31:32, :])
        dx_ref[...] = (grad_ref[...] + back).astype(bf16)
        gain_ref[...] = jnp.concatenate([grad_gain, jnp.zeros((7, D), f32)], axis=0)

    return call(
        kernel,
        [shape((rows, D), bf16), shape((8, D), f32), *halves(64)],
        [place, grad, frames, vec, entry, before, *win_parts],
        [smem()] + [vmem()] * 5 + [vmem()] * n,
        [pltpu.VMEM((D, FF), bf16)],
        "ffn_first_in",
    )


def attend(values, vec, rel_table, lengths, parts, place, plan):
    rows = values.shape[0]
    count = lengths.shape[0]
    each = rows // count
    n = len(parts)
    pairs = HEADS // 2

    def kernel(place_ref, len_ref, x_ref, vec_ref, rel_ref, *rest):
        ws = rest[:n]
        out_ref, entry_ref, qkv_ref, prob_ref, mix_ref, weight, mixed = rest[n:]
        join(place_ref, ws, weight)
        x = x_ref[...]
        normed, _ = stats(x)
        entry = (normed * vec_ref[32:33, :]).astype(bf16)
        entry_ref[...] = entry
        for k in range(3):
            heads = dot(entry, weight[k]).astype(bf16)
            for p in range(pairs):
                qkv_ref[k, p] = heads[:, p * 128 : (p + 1) * 128]
        lane = lax.broadcasted_iota(jnp.int32, (1, 128), 1)
        table = rel_ref[...]
        spot = lax.broadcasted_iota(jnp.int32, (1, each), 1)

        def step(i, carry):
            s = i // pairs
            p = i % pairs
            span = pl.ds(pl.multiple_of(s * each, each), each)
            query = qkv_ref[0, p, span, :]
            keys = qkv_ref[1, p, span, :]
            vals = qkv_ref[2, p, span, :]
            valid = spot < len_ref[s]
            both = []
            for h in range(2):
                mask = (lane < HEAD) if h == 0 else (lane >= HEAD)
                mine = jnp.where(mask, query, jnp.zeros_like(query))
                raw = dot_cols(mine, keys)
                skew = pltpu.roll(dot_cols(mine, table), 0, 1, stride=1, stride_axis=0)[:, :each]
                scores = jnp.where(valid, (raw + skew) * 0.125, MASKED_SCORE)
                grown = jnp.exp(scores - jnp.max(scores, axis=-1, keepdims=True))
                low = (grown * (1.0 / jnp.sum(grown, axis=-1, keepdims=True))).astype(bf16)
                prob_ref[2 * i + h] = low
                both.append(dot(low, vals))
            mixed[p, span, :] = jnp.where(lane < HEAD, both[0], both[1]).astype(bf16)
            return carry

        lax.fori_loop(0, count * pairs, step, 0)
        mix = jnp.concatenate([mixed[p] for p in range(pairs)], axis=1)
        mix_ref[...] = mix
        out_ref[...] = x + dot(mix, weight[3])

    return call(
        kernel,
        [
            shape((rows, D), f32),
            shape((rows, D), bf16),
            shape((3, pairs, rows, 128), bf16),
            shape((count * HEADS, each, each), bf16),
            shape((rows, D), bf16),
        ],
        [place, lengths, values, vec, rel_table, *parts],
        [smem(), smem()] + [vmem()] * (3 + n),
        [pltpu.VMEM((4, D, D), bf16), pltpu.VMEM((pairs, rows, 128), bf16)],
        "attend",
    )


def attend_back(grad, values, vec, kept, rel_table, parts, place, plan, count):
    rows = values.shape[0]
    each = rows // count
    n = len(parts)
    pairs = HEADS // 2
    entry, qkv, prob, mix = kept
    width = rel_table.shape[0]

    def kernel(place_ref, grad_ref, x_ref, vec_ref, entry_ref, qkv_ref, prob_ref, mix_ref, rel_ref, *rest):
        ws = rest[:n]
        dx_ref, gain_ref, rel_out, *g_refs = rest[n : n + 5]
        weight, dmix, dqkv = rest[n + 5 :]
        join(place_ref, ws, weight)
        down = grad_ref[...]
        low = down.astype(bf16)
        put(g_refs, plan, place_ref, dot_rows(mix_ref[...], low), 48, 16, 0)
        spread = dot_cols(low, weight[3]).astype(bf16)
        for p in range(pairs):
            dmix[p] = spread[:, p * 128 : (p + 1) * 128]
        lane = lax.broadcasted_iota(jnp.int32, (1, 128), 1)
        table = rel_ref[...]
        flip = (
            lax.broadcasted_iota(jnp.int32, (each, each), 0)
            + lax.broadcasted_iota(jnp.int32, (each, each), 1)
            == each - 1
        ).astype(bf16)
        rel_out[...] = jnp.zeros_like(rel_out)

        def step(i, carry):
            s = i // pairs
            p = i % pairs
            span = pl.ds(pl.multiple_of(s * each, each), each)
            query = qkv_ref[0, p, span, :]
            keys = qkv_ref[1, p, span, :]
            vals = qkv_ref[2, p, span, :]
            outer = dmix[p, span, :]
            grad_q = jnp.zeros((each, 128), f32)
            grad_k = jnp.zeros((each, 128), f32)
            grad_v = jnp.zeros((each, 128), f32)
            grad_r = jnp.zeros((width, 128), f32)
            for h in range(2):
                mask = (lane < HEAD) if h == 0 else (lane >= HEAD)

                def pick(v):
                    return jnp.where(mask, v, jnp.zeros_like(v))

                dout = pick(outer)
                q_own = pick(query)
                prob_low = prob_ref[2 * i + h]
                prob_wide = prob_low.astype(f32)
                dprob = dot_cols(dout, vals)
                inner = jnp.sum(prob_wide * dprob, axis=-1, keepdims=True)
                dscore = (prob_wide * (dprob - inner)).astype(bf16)
                grad_v = grad_v + dot_rows(prob_low, dout)
                grad_k = grad_k + dot_rows(dscore, q_own)
                turned = dot(flip, dscore)
                wide = jnp.concatenate([turned, jnp.zeros((each, width - each), f32)], axis=1)
                skew = pltpu.roll(wide, width - each + 1, 1, stride=1, stride_axis=0).astype(bf16)
                along = dot(flip, skew).astype(bf16)
                grad_q = grad_q + dot(dscore, pick(keys)) + dot(along, pick(table))
                grad_r = grad_r + dot_rows(along, q_own)
            dqkv[0, p, span, :] = (grad_q * 0.125).astype(bf16)
            dqkv[1, p, span, :] = (grad_k * 0.125).astype(bf16)
            dqkv[2, p, span, :] = grad_v.astype(bf16)
            rel_out[...] += grad_r * 0.125
            return carry

        lax.fori_loop(0, count * pairs, step, 0)
        entry_low = entry_ref[...]
        grad_entry = jnp.zeros((rows, D), f32)
        for k in range(3):
            heads = jnp.concatenate([dqkv[k, p] for p in range(pairs)], axis=1)
            put(g_refs, plan, place_ref, dot_rows(entry_low, heads), 16 * k, 16, 0)
            grad_entry = grad_entry + dot_cols(heads, weight[k])
        normed, scale = stats(x_ref[...])
        back, grad_gain = norm_back(grad_entry, normed, scale, vec_ref[32:33, :])
        dx_ref[...] = down + back
        gain_ref[...] = jnp.concatenate([grad_gain, jnp.zeros((7, D), f32)], axis=0)

    return call(
        kernel,
        [
            shape((rows, D), f32),
            shape((8, D), f32),
            shape((width, 128), f32),
            *halves(ATTN_ROWS),
        ],
        [place, grad, values, vec, entry, qkv, prob, mix, rel_table, *parts],
        [smem()] + [vmem()] * (8 + n),
        [
            pltpu.VMEM((4, D, D), bf16),
            pltpu.VMEM((pairs, rows, 128), bf16),
            pltpu.VMEM((3, pairs, rows, 128), bf16),
        ],
        "attend_back",
    )


def convolve(values, vec, parts, place, plan, count):
    rows = values.shape[0]
    each = rows // count
    n = len(parts)
    cols = D // 128
    chunk = 64

    def kernel(place_ref, x_ref, vec_ref, *rest):
        ws = rest[:n]
        out_ref, entry_ref, gated_ref, sig_ref, conv_ref, act_ref, weight = rest[n:]
        join(place_ref, ws, weight)
        x = x_ref[...]
        normed, _ = stats(x)
        entry = (normed * vec_ref[33:34, :]).astype(bf16)
        entry_ref[...] = entry
        linear = dot(entry, weight[:, :D])
        sig = logistic(dot(entry, weight[:, D : 2 * D]))
        sig_ref[...] = sig
        gated = linear * sig
        for s in range(count):
            for c in range(cols):
                gated_ref[s, c, :LEAD, :] = jnp.zeros((LEAD, 128), f32)
                gated_ref[s, c, LEAD:, :] = gated[s * each : (s + 1) * each, c * 128 : (c + 1) * 128]
        for c in range(cols):
            taps = vec_ref[0:32, c * 128 : (c + 1) * 128]

            def step(i, carry):
                s = i // (each // chunk)
                t = (i % (each // chunk)) * chunk
                total = jnp.zeros((chunk, 128), f32)
                for k in range(KERNEL):
                    total = total + taps[k : k + 1] * gated_ref[s, c, pl.ds(t + k + LEAD - KERNEL + 1, chunk), :]
                conv_ref[pl.ds(pl.multiple_of(i * chunk, chunk), chunk), c * 128 : (c + 1) * 128] = total
                return carry

            lax.fori_loop(0, rows // chunk, step, 0)
        inner, _ = stats(conv_ref[...])
        act = inner * vec_ref[34:35, :]
        low = (act * logistic(act)).astype(bf16)
        act_ref[...] = low
        out_ref[...] = x + dot(low, weight[:, 2 * D :])

    return call(
        kernel,
        [
            shape((rows, D), f32),
            shape((rows, D), bf16),
            shape((count, cols, each + LEAD, 128), f32),
            shape((rows, D), f32),
            shape((rows, D), f32),
            shape((rows, D), bf16),
        ],
        [place, values, vec, *parts],
        [smem()] + [vmem()] * (2 + n),
        [pltpu.VMEM((D, 3 * D), bf16)],
        "convolve",
    )


def convolve_back(grad, values, vec, kept, parts, place, plan, count):
    rows = values.shape[0]
    each = rows // count
    n = len(parts)
    cols = D // 128
    entry, gated, sig, conved, act = kept

    def kernel(place_ref, grad_ref, x_ref, vec_ref, entry_ref, gated_ref, sig_ref, conv_ref, act_ref, *rest):
        ws = rest[:n]
        dx_ref, gain_ref, taps_out, *g_refs = rest[n : n + 5]
        weight, dconv, dgated = rest[n + 5 :]
        join(place_ref, ws, weight)
        down = grad_ref[...]
        low = down.astype(bf16)
        put(g_refs, plan, place_ref, dot_rows(act_ref[...], low), 32, 16, 0)
        inner, inner_scale = stats(conv_ref[...])
        inner_gain = vec_ref[34:35, :]
        act_in = inner * inner_gain
        grad_act = dot_cols(low, weight[:, 2 * D :]) * slope_of(act_in, logistic(act_in))
        grad_conv, gain_inner = norm_back(grad_act, inner, inner_scale, inner_gain)
        for s in range(count):
            for c in range(cols):
                dconv[s, c, :each, :] = grad_conv[s * each : (s + 1) * each, c * 128 : (c + 1) * 128]
                dconv[s, c, each:, :] = jnp.zeros((LEAD, 128), f32)
        for c in range(cols):
            lanes = slice(c * 128, (c + 1) * 128)
            taps = vec_ref[0:32, lanes]

            def step(i, sums):
                s = i // (each // 8)
                t = (i % (each // 8)) * 8
                here = dconv[s, c, pl.ds(pl.multiple_of(t, 8), 8), :]
                total = jnp.zeros((8, 128), f32)
                new = []
                for k in range(KERNEL):
                    new.append(sums[k] + here * gated_ref[s, c, pl.ds(t + k + LEAD - KERNEL + 1, 8), :])
                    total = total + taps[k : k + 1] * dconv[s, c, pl.ds(t + KERNEL - 1 - k, 8), :]
                dgated[pl.ds(pl.multiple_of(i * 8, 8), 8), lanes] = total
                return tuple(new)

            sums = lax.fori_loop(0, rows // 8, step, tuple(jnp.zeros((8, 128), f32) for _ in range(KERNEL)))
            found = [jnp.sum(v, axis=0, keepdims=True) for v in sums]
            taps_out[:, lanes] = jnp.concatenate(found + [jnp.zeros((1, 128), f32)], axis=0)
        grad_gated = dgated[...]
        sig_wide = sig_ref[...]
        linear_sig = jnp.concatenate(
            [
                jnp.concatenate([gated_ref[s, c, LEAD:, :] for c in range(cols)], axis=1)
                for s in range(count)
            ],
            axis=0,
        )
        grad_one = (grad_gated * sig_wide).astype(bf16)
        grad_two = (grad_gated * linear_sig * (1.0 - sig_wide)).astype(bf16)
        entry_low = entry_ref[...]
        put(g_refs, plan, place_ref, dot_rows(entry_low, grad_one), 0, 16, 0)
        put(g_refs, plan, place_ref, dot_rows(entry_low, grad_two), 16, 16, 0)
        grad_entry = dot_cols(grad_one, weight[:, :D]) + dot_cols(grad_two, weight[:, D : 2 * D])
        normed, scale = stats(x_ref[...])
        back, gain_outer = norm_back(grad_entry, normed, scale, vec_ref[33:34, :])
        dx_ref[...] = down + back
        gain_ref[...] = jnp.concatenate([gain_outer, gain_inner, jnp.zeros((6, D), f32)], axis=0)

    return call(
        kernel,
        [
            shape((rows, D), f32),
            shape((8, D), f32),
            shape((32, D), f32),
            *halves(CONV_ROWS),
        ],
        [place, grad, values, vec, entry, gated, sig, conved, act, *parts],
        [smem()] + [vmem()] * (8 + n),
        [
            pltpu.VMEM((D, 3 * D), bf16),
            pltpu.VMEM((count, cols, each + LEAD, 128), f32),
            pltpu.VMEM((rows, D), f32),
        ],
        "convolve_back",
    )


def adam(weight, moment, square, grad):
    new_moment = BETA_FIRST * moment + (1.0 - BETA_FIRST) * grad
    new_square = BETA_SECOND * square + (1.0 - BETA_SECOND) * grad * grad
    first = new_moment * (1.0 / (1.0 - BETA_FIRST**STEP))
    second = new_square * (1.0 / (1.0 - BETA_SECOND**STEP))
    update = first / (jnp.sqrt(second) + ADAM_EPSILON) + WEIGHT_DECAY * weight
    return new_moment, new_square, update


def folded(values):
    squares = jnp.sum((values * values).reshape(-1, values.shape[-1]), axis=0, keepdims=True)
    total = squares[:, :128]
    for c in range(1, values.shape[-1] // 128):
        total = total + squares[:, c * 128 : (c + 1) * 128]
    return total


def update_matrix(layer, pieces, block, spots, states, given, name):
    count = spots.shape[0]
    rows, cols = states[0].shape[1] // count, states[0].shape[2]
    given = given or ()

    half = count // 2

    def kernel(spot_ref, g0_near, g0_far, g1_near, g1_far, w_ref, m_ref, q_ref, *rest):
        g_out, u_out, m_out, q_out, sums = rest[len(given) :]
        index = 2 * pl.program_id(0)

        @pl.when(pl.program_id(0) == 0)
        def _():
            sums[...] = jnp.zeros_like(sums)

        grads = []
        for k, near, far in ((0, g0_near, g0_far), (1, g1_near, g1_far)):
            raw = jnp.where(spot_ref[index + k] < half, near[0], far[0]).astype(f32)
            grads.append(jnp.concatenate([raw[k * rows : (k + 1) * rows] for k in range(cols // D)], axis=1))
        grad = jnp.concatenate(grads, axis=0)
        weight = w_ref[0]
        new_moment, new_square, update = adam(weight, m_ref[0], q_ref[0], grad)
        g_out[0] = grad
        u_out[0] = update
        m_out[0] = new_moment
        q_out[0] = new_square
        sums[...] += jnp.concatenate([folded(weight), folded(update), jnp.zeros((6, 128), f32)], axis=0)

    tile = pl.BlockSpec((1, 2 * rows, cols), lambda p, spot: (layer, p, 0))
    return pl.pallas_call(
        kernel,
        out_shape=[shape(states[0].shape, f32)] * 4 + [shape((8, 128), f32)],
        grid_spec=pltpu.PrefetchScalarGridSpec(
            num_scalar_prefetch=1,
            grid=(count // 2,),
            in_specs=[
                pl.BlockSpec((1, 64, D), lambda p, spot, k=k: (spot[2 * p + k] % half, block, 0))
                for k in (0, 0, 1, 1)
            ]
            + [tile] * 3
            + [pl.BlockSpec(memory_space=pl.ANY)] * len(given),
            out_specs=[tile] * 4 + [pl.BlockSpec((8, 128), lambda p, spot: (0, 0))],
        ),
        input_output_aliases={8 + k: k for k in range(len(given))},
        compiler_params=pltpu.CompilerParams(vmem_limit_bytes=STREAM_LIMIT),
        name=name,
    )(spots, *pieces, *pieces, *states, *given)


def move_layer(layer, win, in_update, in_factor, wout, out_update, out_factor):
    steps = 4
    tiles = [pl.BlockSpec((1, w.shape[1] // steps, w.shape[2]), lambda p: (layer, p, 0)) for w in (win, wout)]

    def kernel(factor_ref, w0, u0, w1, u1, out0, out1):
        out0[...] = w0[...] - (LEARN_RATE * factor_ref[0]) * u0[...]
        out1[...] = w1[...] - (LEARN_RATE * factor_ref[1]) * u1[...]

    return pl.pallas_call(
        kernel,
        out_shape=[shape(win.shape, f32), shape(wout.shape, f32)],
        grid=(steps,),
        in_specs=[smem(), tiles[0], tiles[0], tiles[1], tiles[1]],
        out_specs=tiles,
        input_output_aliases={2: 0, 4: 1},
        compiler_params=pltpu.CompilerParams(vmem_limit_bytes=STREAM_LIMIT),
        name="move_layer",
    )(jnp.stack([in_factor, out_factor]), win, in_update, wout, out_update)


def move_rest(attn, attn_update, conv, conv_update, factors):
    steps = 4
    rows = attn.shape[1] // steps
    attn_tile = pl.BlockSpec((4, rows, D), lambda p: (0, p, 0))
    conv_tile = pl.BlockSpec((rows, 3 * D), lambda p: (p, 0))

    def kernel(factor_ref, w0, u0, w1, u1, out0, out1):
        for k in range(4):
            out0[k] = w0[k] - (LEARN_RATE * factor_ref[k]) * u0[k]
        for k, lanes in ((4, slice(0, 2 * D)), (5, slice(2 * D, 3 * D))):
            out1[:, lanes] = w1[:, lanes] - (LEARN_RATE * factor_ref[k]) * u1[:, lanes]

    return pl.pallas_call(
        kernel,
        out_shape=[shape(attn.shape, f32), shape(conv.shape, f32)],
        grid=(steps,),
        in_specs=[smem(), attn_tile, attn_tile, conv_tile, conv_tile],
        out_specs=[attn_tile, conv_tile],
        input_output_aliases={2: 0, 4: 1},
        compiler_params=pltpu.CompilerParams(vmem_limit_bytes=STREAM_LIMIT),
        name="move_rest",
    )(factors, attn, attn_update, conv, conv_update)


def packed(gains_first, gains_attn, gains_conv, gains_last, taps, rel_wide, each):
    edge = 2 * each - BACK

    def kernel(g0, g1, g2, g4, taps_ref, rel_ref, out_ref, rel):
        out_ref[...] = jnp.zeros_like(out_ref)
        out_ref[0:KERNEL, :] = taps_ref[0:KERNEL, :]
        out_ref[31:32, :] = g0[0:1, :]
        out_ref[32:33, :] = g1[0:1, :]
        out_ref[33:35, :] = g2[0:2, :]
        out_ref[35:37, :] = g4[0:2, :]
        half = rel_ref[:, :HEAD] + rel_ref[:, HEAD:]
        rel[...] = jnp.zeros_like(rel)
        rel[0:1, :] = jnp.sum(half[each : edge + 8] * (lax.broadcasted_iota(jnp.int32, (each - BACK + 8, 1), 0) <= each - BACK), axis=0, keepdims=True)
        rel[0:BACK, :] = rel[0:BACK, :] + half[edge:] * (lax.broadcasted_iota(jnp.int32, (BACK, 1), 0) > 0)
        rel[BACK : BACK + AHEAD, :] = half[:AHEAD]
        rel[RELS - 1 : RELS, :] = jnp.sum(half[AHEAD:each], axis=0, keepdims=True)
        for b in range(5):
            out_ref[40:56, b * HEAD : (b + 1) * HEAD] = rel[b * 16 : b * 16 + 16, :]

    return call(
        kernel,
        [shape((56, D), f32)],
        [gains_first, gains_attn, gains_conv, gains_last, taps, rel_wide],
        [vmem()] * 6,
        [pltpu.VMEM((80, HEAD), f32)],
        "packed",
    )[0]


def update_rest(pieces, spots, attn, conv):
    count = spots.shape[0]
    rows = 2 * (attn[0].shape[1] // count)

    half = count // 2

    def kernel(spot_ref, g0_near, g0_far, g1_near, g1_far, wa, ma, qa, wc, mc, qc, *outs):
        ga_out, ua_out, ma_out, qa_out, qo_out, gc_out, uc_out, mc_out, qc_out, sums = outs
        index = pl.program_id(0)

        @pl.when(index == 0)
        def _():
            sums[...] = jnp.zeros_like(sums)

        raws = [
            jnp.where(spot_ref[2 * index + k] < half, near[0], far[0])
            for k, near, far in ((0, g0_near, g0_far), (1, g1_near, g1_far))
        ]
        found = []
        for k in range(4):
            low = CONV_ROWS + k * 16
            grad = jnp.concatenate([g[low : low + 16] for g in raws], axis=0).astype(f32)
            weight = wa[k]
            new_moment, new_square, update = adam(weight, ma[k], qa[k], grad)
            ga_out[k] = grad
            ua_out[k] = update
            ma_out[k] = new_moment
            if k < 3:
                qa_out[k] = new_square
            else:
                qo_out[...] = new_square
            found += [folded(weight), folded(update)]
        for low, high in ((0, 2), (2, 3)):
            lanes = slice(low * D, high * D)
            parts = [
                jnp.concatenate([g[k * 16 : (k + 1) * 16] for k in range(low, high)], axis=1) for g in raws
            ]
            grad = jnp.concatenate(parts, axis=0).astype(f32)
            weight = wc[:, lanes]
            new_moment, new_square, update = adam(weight, mc[:, lanes], qc[:, lanes], grad)
            gc_out[:, lanes] = grad
            uc_out[:, lanes] = update
            mc_out[:, lanes] = new_moment
            qc_out[:, lanes] = new_square
            found += [folded(weight), folded(update)]
        sums[...] += jnp.concatenate(found + [jnp.zeros((4, 128), f32)], axis=0)

    attn_block = pl.BlockSpec((4, rows, D), lambda p, spot: (0, p, 0))
    conv_block = pl.BlockSpec((rows, 3 * D), lambda p, spot: (p, 0))
    three = pl.BlockSpec((3, rows, D), lambda p, spot: (0, p, 0))
    one = pl.BlockSpec((rows, D), lambda p, spot: (p, 0))
    side = attn[0].shape[1]
    return pl.pallas_call(
        kernel,
        out_shape=[shape(attn[0].shape, f32)] * 3
        + [shape((3, side, D), f32), shape((side, D), f32)]
        + [shape(conv[0].shape, f32)] * 4
        + [shape((16, 128), f32)],
        grid_spec=pltpu.PrefetchScalarGridSpec(
            num_scalar_prefetch=1,
            grid=(count // 2,),
            in_specs=[
                pl.BlockSpec((1, CONV_ROWS + ATTN_ROWS, D), lambda p, spot, k=k: (spot[2 * p + k] % half, 0, 0))
                for k in (0, 0, 1, 1)
            ]
            + [attn_block] * 3
            + [conv_block] * 3,
            out_specs=[attn_block] * 3
            + [three, one]
            + [conv_block] * 4
            + [pl.BlockSpec((16, 128), lambda p, spot: (0, 0))],
        ),
        compiler_params=pltpu.CompilerParams(vmem_limit_bytes=STREAM_LIMIT),
        name="update_rest",
    )(spots, *pieces, *pieces, *attn, *conv)


def move(weight, update, factor):
    return weight - LEARN_RATE * factor * update


def ratio_of(sums):
    weight, update = sums[0::2], sums[1::2]
    return jnp.sqrt(weight), jnp.sqrt(update), jnp.sqrt(weight) / jnp.sqrt(update + RATIO_EPSILON)


def body(
    frames,
    lengths,
    cotangent,
    ffn_in,
    ffn_in_moment,
    ffn_in_square,
    ffn_out,
    ffn_out_moment,
    ffn_out_square,
    attn_proj,
    attn_moment,
    attn_square,
    conv_proj,
    conv_moment,
    conv_square,
    vectors,
    vectors_moment,
    vectors_square,
    rel_keys,
    rel_moment,
    rel_square,
):
    groups, shards = lax.axis_size("group"), lax.axis_size("shard")
    plan = Plan(groups, shards)
    group, shard = lax.axis_index("group"), lax.axis_index("shard")
    core = jnp.bitwise_and(group, 1)
    count, each, _ = frames.shape
    mine = jnp.int32(0)
    for step in plan.order:
        bit = jnp.right_shift(group if step[0] == "group" else shard, step[1]) & 1
        mine = mine * 2 + bit
    kept = jnp.int32(0)
    for step in plan.kept:
        kept = kept * 2 + (jnp.right_shift(group, step[1]) & 1)
    spots = jnp.array([plan.kept_place(p) for p in range(plan.owned)], jnp.int32) ^ kept
    place = jnp.stack([shard, core, mine]).astype(jnp.int32)

    first_halves = rounded_halves(plan, core, (ffn_in, 1, 0), (ffn_out, 1, 0))
    rows, halves_left = rounded_rows(plan, core, ffn_in, ffn_out, attn_proj, conv_proj)
    win0, wout0 = (Fetch(w, 0, plan, r, v, 0) for w, r, v in zip((ffn_in, ffn_out), rows, first_halves))
    watt = Fetch(attn_proj, 1, plan, rows[4], halves_left[0])
    wconv = Fetch(conv_proj, 0, plan, rows[5], halves_left[1])
    win1, wout1 = (Fetch(w, 0, plan, r, v, 1) for w, r, v in zip((ffn_in, ffn_out), rows[2:4], halves_left[2:]))
    win0.near()
    vec = lax.all_gather(vectors.astype(bf16), "shard", axis=1, tiled=True) if shards != 2 else None
    if vec is None:
        (low,) = gate([vectors.astype(bf16)], [first_halves[0]])
        other = swap(low, ("shard", 0))
        vec = jnp.where(shard == 0, jnp.concatenate([low, other], 1), jnp.concatenate([other, low], 1))
    vec = jnp.concatenate([vec.astype(f32), jnp.zeros((3, D), f32)], axis=0)
    rel_low = rel_keys.astype(bf16)
    table = jnp.concatenate(
        [
            rel_low[BACK:],
            jnp.broadcast_to(rel_low[RELS - 1 :], (each - AHEAD - 1, HEAD)),
            jnp.broadcast_to(rel_low[:1], (each - BACK, HEAD)),
            rel_low[:BACK],
        ],
        axis=0,
    )
    table = jnp.concatenate([table, table], axis=1)

    flat = frames.reshape(count * each, D)
    if shards == 2:
        order((win0,), (rows[0],))
    order((wout0,), (win0.value, vec))
    wout0.near()
    win0 = win0.far()
    entry0, hidden0, slope0 = ffn_first_up(flat, vec, win0, place)
    order((watt,), (wout0.value, entry0))
    watt.near()
    order((wout0,), (entry0,))
    order((wconv,), (watt.value,))
    order((win1,), (watt.value,))
    wconv.near()
    win1.near()
    wout0 = wout0.far()
    hidden0, watt.value = gate([hidden0, watt.value], [entry0])
    watt = watt.far()
    x1 = ffn_first_down(flat, hidden0, wout0, place)
    x2, *kept_attn = attend(x1, vec, table, lengths, watt, place, plan)
    order((wconv,), (x2,))
    order((wout1,), (x2,))
    wout1.near()
    wconv = wconv.far()
    x3, *kept_conv = convolve(x2, vec, wconv, place, plan, count)
    order((win1,), (x3,))
    win1 = win1.far()
    order((wout1,), (x3,))
    wout1 = wout1.far()
    output, d3, gains_last, *pieces = ffn_last(
        x3, vec, cotangent.reshape(count * each, D), lengths, win1, wout1, place, plan
    )
    last = Chain(*pieces, plan)
    d2, gains_conv, taps, *pieces = beside(
        [last], lambda d: convolve_back(d, x2, vec, kept_conv, wconv, place, plan, count), [d3], 1
    )
    conv = Chain(*pieces, plan)
    d1, gains_attn, rel_wide, *pieces = beside(
        [last, conv], lambda d: attend_back(d, x1, vec, kept_attn, table, watt, place, plan, count), [d2], 1
    )
    attn = Chain(*pieces, plan)
    before0, *pieces = beside(
        [last, conv, attn], lambda d: ffn_first_out(d, hidden0, slope0, wout0, place, plan), [d1], 0
    )
    first_out = Chain(*pieces, plan)
    early = [last, attn, first_out] if len(conv.todo) < len(attn.todo) else [last, conv, attn, first_out]
    d0, gains_first, *pieces = beside(
        early, lambda b: ffn_first_in(d1, flat, vec, entry0, b, win0, place, plan), [before0], 1
    )
    first_in = Chain(*pieces, plan)
    middle = merged(conv, attn, plan)
    small = Everywhere(packed(gains_first, gains_attn, gains_conv, gains_last, taps, rel_wide, each), plan)
    advance([last, middle, first_out, first_in, small], 1)
    advance([last, middle, first_in, small], 1)
    first = merged(first_out, first_in, plan)
    chains = [last, middle, first, small]
    advance(chains, len(last.todo))
    in_states = (ffn_in, ffn_in_moment, ffn_in_square)
    out_states = (ffn_out, ffn_out_moment, ffn_out_square)
    *half_out, sums_out1 = beside(
        chains, lambda *v: update_matrix(1, v, 1, spots, out_states, None, "update_out1"), last.kept, -1
    )
    *half_in, sums_in1 = beside(
        chains, lambda *v: update_matrix(1, v, 0, spots, in_states, None, "update_in1"), last.kept, -1
    )
    advance(chains, len(middle.todo))
    attn_states = (attn_proj, attn_moment, attn_square)
    conv_states = (conv_proj, conv_moment, conv_square)
    (attn_grad, attn_up, attn_m, attn_q, attn_qo, conv_grad, conv_up, conv_m, conv_q, sums_rest) = beside(
        chains, lambda *v: update_rest(v, spots, attn_states, conv_states), middle.kept, -1
    )
    advance([small], len(small.todo))
    small = small.kept
    wide = vectors.shape[1]
    vec_grad = lax.dynamic_slice(small, (0, shard * wide), (KERNEL + 6, wide))
    rel_grad = jnp.concatenate([small[40:56, b * HEAD : (b + 1) * HEAD] for b in range(5)], axis=0)[:RELS]
    vec_m, vec_q, vec_up = adam(vectors, vectors_moment, vectors_square, vec_grad)
    rel_m, rel_q, rel_up = adam(rel_keys, rel_moment, rel_square, rel_grad)

    vec_sums = []
    for part in (vectors, vec_up):
        squares = jnp.sum(part * part, axis=1)
        vec_sums.append(jnp.concatenate([jnp.sum(squares[:KERNEL])[None], squares[KERNEL:]]))
    early = jnp.sum(jnp.concatenate([sums_in1[:2], sums_out1[:2], sums_rest[:12]], axis=0), axis=1)
    early = sum_shards(jnp.concatenate([early, jnp.stack(vec_sums, axis=1).reshape(-1)]), plan)
    early_ratio = ratio_of(early)
    fast = early_ratio[2]
    half_in[1], half_out[1] = beside(
        chains,
        lambda u: move_layer(1, ffn_in, u, fast[0], ffn_out, half_out[1], fast[1]),
        [half_in[1]],
        0,
    )
    advance(chains, len(first.todo))
    out_grad, out_up, out_m, out_q, sums_out0 = update_matrix(
        0, first.kept, 0, spots, out_states, half_out, "update_out0"
    )
    in_grad, in_up, in_m, in_q, sums_in0 = update_matrix(
        0, first.kept, 1, spots, in_states, half_in, "update_in0"
    )
    final = sum_shards(jnp.sum(jnp.concatenate([sums_in0[:2], sums_out0[:2]], axis=0), axis=1), plan)
    rel_sums = jnp.stack([jnp.sum(rel_keys * rel_keys), jnp.sum(rel_up * rel_up)])
    late_ratio = ratio_of(rel_sums)
    final_ratio = ratio_of(final)

    def spread(n):
        e, l = early_ratio[n], late_ratio[n]
        none = jnp.zeros((1,), f32)
        return jnp.concatenate([none, e[0:1], none, e[1:2], e[2:15], l[0:1]])

    column = lax.broadcasted_iota(jnp.int32, (2, 18), 1)
    last_in = jnp.stack([final_ratio[0][0], final_ratio[1][0]])[:, None]
    last_out = jnp.stack([final_ratio[0][1], final_ratio[1][1]])[:, None]
    known = jnp.stack([spread(0), spread(1)])
    trust_norms = jnp.where(column == 0, last_in, jnp.where(column == 2, last_out, known))
    ffn_in_new, ffn_out_new = move_layer(
        0, ffn_in, in_up, final_ratio[2][0], ffn_out, out_up, final_ratio[2][1]
    )
    attn_new, conv_new = move_rest(attn_proj, attn_up, conv_proj, conv_up, fast[2:8])
    vec_factor = jnp.concatenate([jnp.full((KERNEL,), fast[8]), fast[9:15]])[:, None]
    return (
        output.reshape(frames.shape),
        d0.reshape(frames.shape),
        in_grad,
        ffn_in_new,
        in_m,
        in_q,
        out_grad,
        ffn_out_new,
        out_m,
        out_q,
        attn_grad,
        attn_new,
        attn_m,
        attn_q,
        attn_qo,
        conv_grad,
        conv_new,
        conv_m,
        conv_q,
        vec_grad,
        move(vectors, vec_up, vec_factor),
        vec_m,
        vec_q,
        rel_grad,
        move(rel_keys, rel_up, late_ratio[2][0]),
        rel_m,
        rel_q,
        trust_norms,
    )


def solution(mesh):
    return jax.shard_map(
        body,
        mesh=mesh,
        in_specs=(
            P(("group", "shard"), None, None),
            P(("group", "shard")),
            P(("group", "shard"), None, None),
            P(None, "shard", None),
            P(None, "shard", None),
            P(None, "shard", None),
            P(None, "shard", None),
            P(None, "shard", None),
            P(None, "shard", None),
            P(None, "shard", None),
            P(None, "shard", None),
            P(None, "shard", None),
            P("shard", None),
            P("shard", None),
            P("shard", None),
            P(None, "shard"),
            P(None, "shard"),
            P(None, "shard"),
            P(),
            P(),
            P(),
        ),
        out_specs=(
            P(("group", "shard"), None, None),
            P(("group", "shard"), None, None),
            P(None, "shard", None),
            P(None, "shard", None),
            P(None, "shard", None),
            P(None, "shard", None),
            P(None, "shard", None),
            P(None, "shard", None),
            P(None, "shard", None),
            P(None, "shard", None),
            P(None, "shard", None),
            P(None, "shard", None),
            P(None, "shard", None),
            P(None, "shard", None),
            P("shard", None),
            P("shard", None),
            P("shard", None),
            P("shard", None),
            P("shard", None),
            P(None, "shard"),
            P(None, "shard"),
            P(None, "shard"),
            P(None, "shard"),
            P(),
            P(),
            P(),
            P(),
            P(),
        ),
        check_vma=False,
    )
```

```python
import math

import jax
import jax.numpy as jnp
from jax import lax
from jax.experimental import pallas as pl
from jax.experimental.pallas import tpu as pltpu
from jax.sharding import PartitionSpec as P

D = 512
FF = 2048
HEADS = 8
HEAD = 64
KERNEL = 31
BACK = 64
AHEAD = 8
RELS = 73
STEP = 10
PIECES = 32
LEAD = 32
FFN_ROWS = 128
ATTN_ROWS = 64
CONV_ROWS = 48

NORM_EPSILON = 1e-05
ADAM_EPSILON = 1e-06
RATIO_EPSILON = 1e-06
BETA_FIRST = 0.9
BETA_SECOND = 0.999
WEIGHT_DECAY = 0.01
LEARN_RATE = 0.5
MASKED_SCORE = -1e30

bf16 = jnp.bfloat16
f32 = jnp.float32
VMEM_LIMIT = 24 * 1024 * 1024
STREAM_LIMIT = 60 * 1024 * 1024


def vmem():
    return pl.BlockSpec(memory_space=pltpu.VMEM)


def smem():
    return pl.BlockSpec(memory_space=pltpu.SMEM)


def shape(dims, kind):
    return jax.ShapeDtypeStruct(dims, kind)


def dot(left, right):
    return jnp.dot(left, right, preferred_element_type=f32)


def dot_rows(left, right):
    return lax.dot_general(left, right, (((0,), (0,)), ((), ())), preferred_element_type=f32)


def dot_cols(left, right):
    return lax.dot_general(left, right, (((1,), (1,)), ((), ())), preferred_element_type=f32)


def stats(values):
    centred = values - jnp.mean(values, axis=-1, keepdims=True)
    scale = lax.rsqrt(jnp.mean(centred * centred, axis=-1, keepdims=True) + NORM_EPSILON)
    return centred * scale, scale


def norm_back(grad, normed, scale, gain):
    grad_gain = jnp.sum(grad * normed, axis=0, keepdims=True)
    scaled = grad * gain
    inner = jnp.mean(scaled * normed, axis=-1, keepdims=True)
    back = scale * (scaled - jnp.mean(scaled, axis=-1, keepdims=True) - normed * inner)
    return back, grad_gain


def logistic(values):
    return 1.0 / (1.0 + jnp.exp(-values))


def slope_of(values, sig):
    return sig * (1.0 + values * (1.0 - sig))


class Plan:
    def __init__(self, groups, shards):
        self.groups, self.shards = groups, shards
        shard_bits = shards.bit_length() - 1
        group_bits = groups.bit_length() - 1
        self.used = min(5 - shard_bits, group_bits)
        self.owned = PIECES // shards
        order = [("group", 0)] + [("shard", b) for b in range(shard_bits)]
        order += [("group", b) for b in range(1, self.used)]
        self.order = order
        self.rest = [("group", b) for b in range(self.used, group_bits)]
        self.shard_bits = [("shard", b) for b in range(shard_bits)]
        self.kept = [step for step in order if step[0] == "group"]

    def piece_bit(self, step):
        return step[1] if step[0] == "group" else self.used + step[1]

    def place(self, piece):
        out = 0
        for step in self.order:
            out = out * 2 + ((piece >> self.piece_bit(step)) & 1)
        return out

    def kept_place(self, piece):
        out = 0
        for step in self.kept:
            out = out * 2 + ((piece >> step[1]) & 1)
        return out


def swap(values, step):
    axis, bit = step
    count = lax.axis_size(axis)
    return lax.ppermute(values, axis, [(i, i ^ (1 << bit)) for i in range(count)])


def add_low(left, right):
    return (left.astype(f32) + right.astype(f32)).astype(bf16)


class Chain:
    def __init__(self, kept, sent, plan):
        order, back = list(plan.order), list(reversed(plan.kept))
        self.todo = [("halve", step) for step in order]
        self.todo += [("add", step) for step in plan.rest] + [("keep", step) for step in back]
        self.kept, self.sent = kept, (sent,)

    def start(self):
        if self.todo:
            self.found = swap(self.sent[0], self.todo[0][1])

    def finish(self):
        if not self.todo:
            return
        kind, _ = self.todo.pop(0)
        coming = self.todo[0][0] if self.todo else None
        if kind == "keep":
            if coming is None:
                self.kept = (self.kept, self.found)
            else:
                self.kept = jnp.concatenate([self.kept, self.found], axis=0)
                self.sent = (self.kept,)
        elif coming == "halve":
            half = self.kept.shape[0] // 2
            low = add_low(self.kept[:half], self.found[:half])
            self.sent = (add_low(self.kept[half:], self.found[half:]),)
            self.kept = low
        else:
            self.kept = add_low(self.kept, self.found)
            self.sent = (self.kept,)


def merged(one, two, plan):
    both = Chain(
        jnp.concatenate([one.kept, two.kept], axis=1),
        jnp.concatenate([one.sent[0], two.sent[0]], axis=1),
        plan,
    )
    both.todo = list(one.todo)
    return both


class Everywhere:
    def __init__(self, values, plan):
        self.todo = plan.order + plan.rest
        self.kept, self.sent = values, (values,)

    def start(self):
        if self.todo:
            self.found = swap(self.sent[0], self.todo[0])

    def finish(self):
        if self.todo:
            self.todo = self.todo[1:]
            self.kept = self.kept + self.found
            self.sent = (self.kept,)


def gate(values, signs):
    held = lax.optimization_barrier((tuple(values), tuple(signs)))
    return held[0]


def beside(chains, run, first, sign):
    chains = [chain for chain in chains if chain.todo]
    first = gate(first, [v for chain in chains for v in chain.sent])
    for chain in chains:
        chain.start()
    outs = run(*first)
    for chain, value in zip(chains, gate([chain.kept for chain in chains], [outs[sign]])):
        chain.kept = value
    for chain in chains:
        chain.finish()
    return outs


def advance(chains, rounds):
    for _ in range(rounds):
        busy = [chain for chain in chains if chain.todo]
        for chain, value in zip(busy, gate([chain.sent for chain in busy], [])):
            chain.sent = tuple(value)
        for chain in busy:
            chain.start()
        for chain in busy:
            chain.finish()


def sum_shards(values, plan):
    for step in plan.shard_bits:
        values = values + swap(values, step)
    return values


def rounded_halves(plan, core, *owns):
    if plan.shards != 2:
        return [None] * len(owns)
    ins, specs, outs, out_specs = [], [], [], []
    for own, dim, layer in owns:
        dims = list(own.shape)
        dims[dim] //= 2
        if layer is not None:
            dims[0] = 1
        axes = len(dims)
        ins.append(own)

        def at(i, core_ref, axes=axes, dim=dim, layer=layer):
            return tuple(core_ref[0] if d == dim else (layer or 0) if d == 0 else 0 for d in range(axes))

        specs.append(pl.BlockSpec(tuple(dims), at))
        outs.append(shape(tuple(dims), bf16))
        out_specs.append(pl.BlockSpec(tuple(dims), lambda i, core_ref, axes=axes: (0,) * axes))

    def kernel(core_ref, *refs):
        for k in range(len(owns)):
            refs[len(owns) + k][...] = refs[k][...].astype(bf16)

    found = pl.pallas_call(
        kernel,
        out_shape=outs,
        grid_spec=pltpu.PrefetchScalarGridSpec(
            num_scalar_prefetch=1, grid=(1,), in_specs=specs, out_specs=out_specs
        ),
        compiler_params=pltpu.CompilerParams(vmem_limit_bytes=STREAM_LIMIT),
        name="rounded_halves",
    )(core.reshape(1).astype(jnp.int32), *ins)
    return [v if layer is None else v[0] for v, (_, _, layer) in zip(found, owns)]


def rounded_rows(plan, core, ffn_in, ffn_out, attn_proj, conv_proj):
    if plan.shards != 2:
        return [None] * 6, [None] * 4
    owns = [(ffn_in, 0), (ffn_out, 0), (ffn_in, 1), (ffn_out, 1)]
    outs = [shape(w.shape[1:], bf16) for w, _ in owns] + [shape(attn_proj.shape, bf16), shape(conv_proj.shape, bf16)]
    halved = [outs[4], outs[5], outs[2], outs[3]]
    for v in halved:
        dims = list(v.shape)
        dims[-2] //= 2
        outs.append(shape(tuple(dims), bf16))

    def kernel(core_ref, in_ref, out_ref, attn_ref, conv_ref, *refs):
        rows = refs[:6]
        for layer in range(2):
            rows[2 * layer][...] = in_ref[layer].astype(bf16)
            rows[2 * layer + 1][...] = out_ref[layer].astype(bf16)
        rows[4][...] = attn_ref[...].astype(bf16)
        rows[5][...] = conv_ref[...].astype(bf16)
        for source, half_ref in zip((rows[4], rows[5], rows[2], rows[3]), refs[6:]):
            half = half_ref.shape[-2]
            span = pl.ds(pl.multiple_of(core_ref[0] * half, half), half)
            half_ref[...] = source[:, span, :] if len(half_ref.shape) == 3 else source[span, :]

    found = call(
        kernel,
        outs,
        [core.reshape(1).astype(jnp.int32), ffn_in, ffn_out, attn_proj, conv_proj],
        [smem()] + [vmem()] * 4,
        (),
        "rounded_rows",
    )
    return found[:6], found[6:]


class Fetch:
    def __init__(self, own, dim, plan, rows, half, layer=None):
        self.own, self.plan, self.dim = rows, plan, dim
        if plan.shards == 2:
            self.value = half
        else:
            one = own if layer is None else own[layer]
            self.value = lax.all_gather(one.astype(bf16), "shard", axis=dim, tiled=True)

    def near(self):
        if self.plan.shards == 2:
            self.value = swap(self.value, ("shard", 0))

    def far(self):
        if self.plan.shards == 2:
            return (self.own, self.value, swap(self.value, ("group", 0)))
        return (self.value,)


def order(later, signs):
    for fetch, value in zip(later, gate([f.value for f in later], signs)):
        fetch.value = value


def join(place_ref, part_refs, whole_ref):
    if len(part_refs) == 1:
        whole_ref[...] = part_refs[0][...]
        return
    own, near, far = part_refs
    rows = own.shape[-2]
    half = rows // 2
    shard, core = place_ref[0], place_ref[1]
    first = pl.multiple_of(shard * rows, half)
    second = pl.multiple_of((1 - shard) * rows + core * half, half)
    third = pl.multiple_of((1 - shard) * rows + (1 - core) * half, half)
    if len(own.shape) == 2:
        whole_ref[pl.ds(second, half), :] = near[...]
        whole_ref[pl.ds(third, half), :] = far[...]
        whole_ref[pl.ds(first, rows), :] = own[...]
    else:
        for k in range(own.shape[0]):
            whole_ref[k, pl.ds(first, rows), :] = own[k]
            whole_ref[k, pl.ds(second, half), :] = near[k]
            whole_ref[k, pl.ds(third, half), :] = far[k]


def put(out_refs, plan, place_ref, value, row, rows_each, first, shift=0):
    kept_ref, sent_ref = out_refs
    low = value.astype(bf16)
    core, mine = place_ref[1] == 0, jnp.bitwise_xor(place_ref[2], shift)
    for k in range(0, value.shape[0] // rows_each, 2):
        even = low[k * rows_each : (k + 1) * rows_each]
        odd = low[(k + 1) * rows_each : (k + 2) * rows_each]
        spot = jnp.bitwise_xor(jnp.int32(plan.place(first + k)), jnp.bitwise_and(mine, PIECES // 2 - 1))
        kept_ref[spot, pl.ds(row, rows_each), :] = jnp.where(core, even, odd)
        sent_ref[spot, pl.ds(row, rows_each), :] = jnp.where(core, odd, even)


def halves(rows):
    return [shape((PIECES // 2, rows, D), bf16)] * 2


def call(kernel, outs, ins, specs, scratch=(), name=None):
    return pl.pallas_call(
        kernel,
        out_shape=list(outs),
        in_specs=specs,
        out_specs=[vmem()] * len(outs),
        scratch_shapes=list(scratch),
        compiler_params=pltpu.CompilerParams(vmem_limit_bytes=VMEM_LIMIT),
        name=name,
    )(*ins)


def ffn_ahead(values, gain, win, wout, entry_ref, hidden_ref, slope_ref, sum_ref):
    normed, _ = stats(values)
    entry_ref[...] = (normed * gain).astype(bf16)
    sum_ref[...] = jnp.zeros_like(sum_ref)

    def step(b, carry):
        cols = pl.ds(pl.multiple_of(b * D, D), D)
        before = dot(entry_ref[...], win[:, cols])
        sig = logistic(before)
        hidden = (before * sig).astype(bf16)
        hidden_ref[:, cols] = hidden
        slope_ref[:, cols] = slope_of(before, sig).astype(bf16)
        sum_ref[...] += dot(hidden, wout[cols, :])
        return carry

    lax.fori_loop(0, FF // D, step, 0)
    return sum_ref[...]


def ffn_behind(grad, values, gain, win, wout, entry_ref, hidden_ref, slope_ref, sum_ref, out_refs, plan, place_ref):
    normed, scale = stats(values)
    branch = (0.5 * grad).astype(bf16)
    sum_ref[...] = jnp.zeros_like(sum_ref)

    def step(b, carry):
        cols = pl.ds(pl.multiple_of(b * D, D), D)
        shift = jnp.bitwise_xor((b % 2) * plan.place(8), (b // 2) * plan.place(16))
        put(out_refs, plan, place_ref, dot_rows(hidden_ref[:, cols], branch), 64, 64, 0, shift)
        grad_before = (dot_cols(branch, wout[cols, :]) * slope_ref[:, cols].astype(f32)).astype(bf16)
        put(out_refs, plan, place_ref, dot_rows(entry_ref[...], grad_before), pl.multiple_of(16 * b, 16), 16, 0)
        sum_ref[...] += dot_cols(grad_before, win[:, cols])
        return carry

    lax.fori_loop(0, FF // D, step, 0)
    back, grad_gain = norm_back(sum_ref[...], normed, scale, gain)
    return grad + back, grad_gain


def ffn_first_up(frames, vec, win_parts, place):
    rows = frames.shape[0]
    n = len(win_parts)

    def kernel(place_ref, x_ref, vec_ref, *rest):
        wins = rest[:n]
        entry_ref, hidden_ref, slope_ref, win = rest[n:]
        normed, _ = stats(x_ref[...].astype(f32))
        entry = (normed * vec_ref[31:32, :]).astype(bf16)
        entry_ref[...] = entry
        join(place_ref, wins, win)

        def step(b, carry):
            cols = pl.ds(pl.multiple_of(b * D, D), D)
            before = dot(entry_ref[...], win[:, cols])
            sig = logistic(before)
            hidden_ref[:, cols] = (before * sig).astype(bf16)
            slope_ref[:, cols] = slope_of(before, sig).astype(bf16)
            return carry

        lax.fori_loop(0, FF // D, step, 0)

    return call(
        kernel,
        [shape((rows, D), bf16), shape((rows, FF), bf16), shape((rows, FF), bf16)],
        [place, frames, vec, *win_parts],
        [smem()] + [vmem()] * 2 + [vmem()] * n,
        [pltpu.VMEM((D, FF), bf16)],
        "ffn_first_up",
    )


def ffn_first_down(frames, hidden, wout_parts, place):
    rows = frames.shape[0]
    n = len(wout_parts)

    def kernel(place_ref, x_ref, hidden_ref, *rest):
        wouts = rest[:n]
        out_ref, wout = rest[n:]
        join(place_ref, wouts, wout)
        out_ref[...] = x_ref[...].astype(f32) + 0.5 * dot(hidden_ref[...], wout[...])

    return call(
        kernel,
        [shape((rows, D), f32)],
        [place, frames, hidden, *wout_parts],
        [smem()] + [vmem()] * 2 + [vmem()] * n,
        [pltpu.VMEM((FF, D), bf16)],
        "ffn_first_down",
    )[0]


def ffn_last(values, vec, cotangent, lengths, win_parts, wout_parts, place, plan):
    rows = values.shape[0]
    count = lengths.shape[0]
    n = len(win_parts)

    def kernel(place_ref, len_ref, x_ref, vec_ref, cot_ref, *rest):
        wins, wouts = rest[:n], rest[n : 2 * n]
        y_ref, dx_ref, gain_ref, *g_refs = rest[2 * n : 2 * n + 5]
        win, wout, entry_ref, hidden_ref, slope_ref, sum_ref = rest[2 * n + 5 :]
        join(place_ref, wins, win)
        join(place_ref, wouts, wout)
        x = x_ref[...]
        gain = vec_ref[35:36, :]
        total = ffn_ahead(x, gain, win, wout, entry_ref, hidden_ref, slope_ref, sum_ref)
        normed, scale = stats(x + 0.5 * total)
        top = vec_ref[36:37, :]
        y_ref[...] = (normed * top).astype(bf16)
        each = rows // count
        grads = []
        for s in range(count):
            spot = lax.broadcasted_iota(jnp.int32, (each, 1), 0)
            part = cot_ref[s * each : (s + 1) * each, :].astype(f32)
            grads.append(jnp.where(spot < len_ref[s], part, 0.0))
        back, grad_top = norm_back(jnp.concatenate(grads, axis=0), normed, scale, top)
        grad, grad_gain = ffn_behind(
            back, x, gain, win, wout, entry_ref, hidden_ref, slope_ref, sum_ref, g_refs, plan, place_ref
        )
        dx_ref[...] = grad
        gain_ref[...] = jnp.concatenate([grad_gain, grad_top, jnp.zeros((6, D), f32)], axis=0)

    return call(
        kernel,
        [shape((rows, D), bf16), shape((rows, D), f32), shape((8, D), f32), *halves(FFN_ROWS)],
        [place, lengths, values, vec, cotangent, *win_parts, *wout_parts],
        [smem(), smem()] + [vmem()] * 3 + [vmem()] * (2 * n),
        [
            pltpu.VMEM((D, FF), bf16),
            pltpu.VMEM((FF, D), bf16),
            pltpu.VMEM((rows, D), bf16),
            pltpu.VMEM((rows, FF), bf16),
            pltpu.VMEM((rows, FF), bf16),
            pltpu.VMEM((rows, D), f32),
        ],
        "ffn_last",
    )


def ffn_first_out(grad, hidden, slope, wout_parts, place, plan):
    rows = grad.shape[0]
    n = len(wout_parts)

    def kernel(place_ref, grad_ref, hidden_ref, slope_ref, *rest):
        wouts = rest[:n]
        before_ref, *g_refs = rest[n : n + 3]
        (wout,) = rest[n + 3 :]
        join(place_ref, wouts, wout)
        branch = (0.5 * grad_ref[...]).astype(bf16)

        def step(b, carry):
            cols = pl.ds(pl.multiple_of(b * D, D), D)
            shift = jnp.bitwise_xor((b % 2) * plan.place(8), (b // 2) * plan.place(16))
            put(g_refs, plan, place_ref, dot_rows(hidden_ref[:, cols], branch), 0, 64, 0, shift)
            spread = dot_cols(branch, wout[cols, :])
            before_ref[:, cols] = (spread * slope_ref[:, cols].astype(f32)).astype(bf16)
            return carry

        lax.fori_loop(0, FF // D, step, 0)

    return call(
        kernel,
        [shape((rows, FF), bf16), *halves(64)],
        [place, grad, hidden, slope, *wout_parts],
        [smem()] + [vmem()] * 3 + [vmem()] * n,
        [pltpu.VMEM((FF, D), bf16)],
        "ffn_first_out",
    )


def ffn_first_in(grad, frames, vec, entry, before, win_parts, place, plan):
    rows = frames.shape[0]
    n = len(win_parts)

    def kernel(place_ref, grad_ref, x_ref, vec_ref, entry_ref, before_ref, *rest):
        wins = rest[:n]
        dx_ref, gain_ref, *g_refs = rest[n : n + 4]
        win, sum_ref = rest[n + 4 :]
        join(place_ref, wins, win)
        low = entry_ref[...]
        sum_ref[...] = jnp.zeros_like(sum_ref)

        def step(b, carry):
            cols = pl.ds(pl.multiple_of(b * D, D), D)
            low_row = pl.multiple_of(16 * b, 16)
            put(g_refs, plan, place_ref, dot_rows(low, before_ref[:, cols]), low_row, 16, 0)
            sum_ref[...] += dot_cols(before_ref[:, cols], win[:, cols])
            return carry

        lax.fori_loop(0, FF // D, step, 0)
        normed, scale = stats(x_ref[...].astype(f32))
        back, grad_gain = norm_back(sum_ref[...], normed, scale, vec_ref[31:32, :])
        dx_ref[...] = (grad_ref[...] + back).astype(bf16)
        gain_ref[...] = jnp.concatenate([grad_gain, jnp.zeros((7, D), f32)], axis=0)

    return call(
        kernel,
        [shape((rows, D), bf16), shape((8, D), f32), *halves(64)],
        [place, grad, frames, vec, entry, before, *win_parts],
        [smem()] + [vmem()] * 5 + [vmem()] * n,
        [pltpu.VMEM((D, FF), bf16), pltpu.VMEM((rows, D), f32)],
        "ffn_first_in",
    )


def attend(values, vec, rel_table, lengths, parts, place, plan):
    rows = values.shape[0]
    count = lengths.shape[0]
    each = rows // count
    n = len(parts)
    pairs = HEADS // 2

    def kernel(place_ref, len_ref, x_ref, vec_ref, rel_ref, *rest):
        ws = rest[:n]
        out_ref, entry_ref, qkv_ref, prob_ref, mix_ref, weight, mixed = rest[n:]
        join(place_ref, ws, weight)
        x = x_ref[...]
        normed, _ = stats(x)
        entry = (normed * vec_ref[32:33, :]).astype(bf16)
        entry_ref[...] = entry
        for k in range(3):
            heads = dot(entry, weight[k]).astype(bf16)
            for p in range(pairs):
                qkv_ref[k, p] = heads[:, p * 128 : (p + 1) * 128]
        lane = lax.broadcasted_iota(jnp.int32, (1, 128), 1)
        table = rel_ref[...]
        spot = lax.broadcasted_iota(jnp.int32, (1, each), 1)

        def step(i, carry):
            s = i // pairs
            p = i % pairs
            span = pl.ds(pl.multiple_of(s * each, each), each)
            query = qkv_ref[0, p, span, :]
            keys = qkv_ref[1, p, span, :]
            vals = qkv_ref[2, p, span, :]
            valid = spot < len_ref[s]
            both = []
            for h in range(2):
                mask = (lane < HEAD) if h == 0 else (lane >= HEAD)
                mine = jnp.where(mask, query, jnp.zeros_like(query))
                raw = dot_cols(mine, keys)
                skew = pltpu.roll(dot_cols(mine, table), 0, 1, stride=1, stride_axis=0)[:, :each]
                scores = jnp.where(valid, (raw + skew) * 0.125, MASKED_SCORE)
                grown = jnp.exp(scores - jnp.max(scores, axis=-1, keepdims=True))
                low = (grown * (1.0 / jnp.sum(grown, axis=-1, keepdims=True))).astype(bf16)
                prob_ref[2 * i + h] = low
                both.append(dot(low, vals))
            mixed[p, span, :] = jnp.where(lane < HEAD, both[0], both[1]).astype(bf16)
            return carry

        lax.fori_loop(0, count * pairs, step, 0)
        mix = jnp.concatenate([mixed[p] for p in range(pairs)], axis=1)
        mix_ref[...] = mix
        out_ref[...] = x + dot(mix, weight[3])

    return call(
        kernel,
        [
            shape((rows, D), f32),
            shape((rows, D), bf16),
            shape((3, pairs, rows, 128), bf16),
            shape((count * HEADS, each, each), bf16),
            shape((rows, D), bf16),
        ],
        [place, lengths, values, vec, rel_table, *parts],
        [smem(), smem()] + [vmem()] * (3 + n),
        [pltpu.VMEM((4, D, D), bf16), pltpu.VMEM((pairs, rows, 128), bf16)],
        "attend",
    )


def attend_back(grad, values, vec, kept, rel_table, parts, place, plan, count):
    rows = values.shape[0]
    each = rows // count
    n = len(parts)
    pairs = HEADS // 2
    entry, qkv, prob, mix = kept
    width = rel_table.shape[0]

    def kernel(place_ref, grad_ref, x_ref, vec_ref, entry_ref, qkv_ref, prob_ref, mix_ref, rel_ref, *rest):
        ws = rest[:n]
        dx_ref, gain_ref, rel_out, *g_refs = rest[n : n + 5]
        weight, dmix, dqkv = rest[n + 5 :]
        join(place_ref, ws, weight)
        down = grad_ref[...]
        low = down.astype(bf16)
        put(g_refs, plan, place_ref, dot_rows(mix_ref[...], low), 48, 16, 0)
        spread = dot_cols(low, weight[3]).astype(bf16)
        for p in range(pairs):
            dmix[p] = spread[:, p * 128 : (p + 1) * 128]
        lane = lax.broadcasted_iota(jnp.int32, (1, 128), 1)
        table = rel_ref[...]
        flip = (
            lax.broadcasted_iota(jnp.int32, (each, each), 0)
            + lax.broadcasted_iota(jnp.int32, (each, each), 1)
            == each - 1
        ).astype(bf16)
        rel_out[...] = jnp.zeros_like(rel_out)

        def step(i, carry):
            s = i // pairs
            p = i % pairs
            span = pl.ds(pl.multiple_of(s * each, each), each)
            query = qkv_ref[0, p, span, :]
            keys = qkv_ref[1, p, span, :]
            vals = qkv_ref[2, p, span, :]
            outer = dmix[p, span, :]
            grad_q = jnp.zeros((each, 128), f32)
            grad_k = jnp.zeros((each, 128), f32)
            grad_v = jnp.zeros((each, 128), f32)
            grad_r = jnp.zeros((width, 128), f32)
            for h in range(2):
                mask = (lane < HEAD) if h == 0 else (lane >= HEAD)

                def pick(v):
                    return jnp.where(mask, v, jnp.zeros_like(v))

                dout = pick(outer)
                q_own = pick(query)
                prob_low = prob_ref[2 * i + h]
                prob_wide = prob_low.astype(f32)
                dprob = dot_cols(dout, vals)
                inner = jnp.sum(prob_wide * dprob, axis=-1, keepdims=True)
                dscore = (prob_wide * (dprob - inner)).astype(bf16)
                grad_v = grad_v + dot_rows(prob_low, dout)
                grad_k = grad_k + dot_rows(dscore, q_own)
                turned = dot(flip, dscore)
                wide = jnp.concatenate([turned, jnp.zeros((each, width - each), f32)], axis=1)
                skew = pltpu.roll(wide, width - each + 1, 1, stride=1, stride_axis=0).astype(bf16)
                along = dot(flip, skew).astype(bf16)
                grad_q = grad_q + dot(dscore, pick(keys)) + dot(along, pick(table))
                grad_r = grad_r + dot_rows(along, q_own)
            dqkv[0, p, span, :] = (grad_q * 0.125).astype(bf16)
            dqkv[1, p, span, :] = (grad_k * 0.125).astype(bf16)
            dqkv[2, p, span, :] = grad_v.astype(bf16)
            rel_out[...] += grad_r * 0.125
            return carry

        lax.fori_loop(0, count * pairs, step, 0)
        entry_low = entry_ref[...]
        grad_entry = jnp.zeros((rows, D), f32)
        for k in range(3):
            heads = jnp.concatenate([dqkv[k, p] for p in range(pairs)], axis=1)
            put(g_refs, plan, place_ref, dot_rows(entry_low, heads), 16 * k, 16, 0)
            grad_entry = grad_entry + dot_cols(heads, weight[k])
        normed, scale = stats(x_ref[...])
        back, grad_gain = norm_back(grad_entry, normed, scale, vec_ref[32:33, :])
        dx_ref[...] = down + back
        gain_ref[...] = jnp.concatenate([grad_gain, jnp.zeros((7, D), f32)], axis=0)

    return call(
        kernel,
        [
            shape((rows, D), f32),
            shape((8, D), f32),
            shape((width, 128), f32),
            *halves(ATTN_ROWS),
        ],
        [place, grad, values, vec, entry, qkv, prob, mix, rel_table, *parts],
        [smem()] + [vmem()] * (8 + n),
        [
            pltpu.VMEM((4, D, D), bf16),
            pltpu.VMEM((pairs, rows, 128), bf16),
            pltpu.VMEM((3, pairs, rows, 128), bf16),
        ],
        "attend_back",
    )


def convolve(values, vec, parts, place, plan, count):
    rows = values.shape[0]
    each = rows // count
    n = len(parts)
    cols = D // 128
    chunk = 64

    def kernel(place_ref, x_ref, vec_ref, *rest):
        ws = rest[:n]
        out_ref, entry_ref, gated_ref, sig_ref, conv_ref, act_ref, weight = rest[n:]
        join(place_ref, ws, weight)
        x = x_ref[...]
        normed, _ = stats(x)
        entry = (normed * vec_ref[33:34, :]).astype(bf16)
        entry_ref[...] = entry
        linear = dot(entry, weight[:, :D])
        sig = logistic(dot(entry, weight[:, D : 2 * D]))
        sig_ref[...] = sig
        gated = linear * sig
        for s in range(count):
            for c in range(cols):
                gated_ref[s, c, :LEAD, :] = jnp.zeros((LEAD, 128), f32)
                gated_ref[s, c, LEAD:, :] = gated[s * each : (s + 1) * each, c * 128 : (c + 1) * 128]
        for c in range(cols):
            taps = vec_ref[0:32, c * 128 : (c + 1) * 128]

            def step(i, carry):
                s = i // (each // chunk)
                t = (i % (each // chunk)) * chunk
                total = jnp.zeros((chunk, 128), f32)
                for k in range(KERNEL):
                    total = total + taps[k : k + 1] * gated_ref[s, c, pl.ds(t + k + LEAD - KERNEL + 1, chunk), :]
                conv_ref[pl.ds(pl.multiple_of(i * chunk, chunk), chunk), c * 128 : (c + 1) * 128] = total
                return carry

            lax.fori_loop(0, rows // chunk, step, 0)
        inner, _ = stats(conv_ref[...])
        act = inner * vec_ref[34:35, :]
        low = (act * logistic(act)).astype(bf16)
        act_ref[...] = low
        out_ref[...] = x + dot(low, weight[:, 2 * D :])

    return call(
        kernel,
        [
            shape((rows, D), f32),
            shape((rows, D), bf16),
            shape((count, cols, each + LEAD, 128), f32),
            shape((rows, D), f32),
            shape((rows, D), f32),
            shape((rows, D), bf16),
        ],
        [place, values, vec, *parts],
        [smem()] + [vmem()] * (2 + n),
        [pltpu.VMEM((D, 3 * D), bf16)],
        "convolve",
    )


def convolve_back(grad, values, vec, kept, parts, place, plan, count):
    rows = values.shape[0]
    each = rows // count
    n = len(parts)
    cols = D // 128
    entry, gated, sig, conved, act = kept

    def kernel(place_ref, grad_ref, x_ref, vec_ref, entry_ref, gated_ref, sig_ref, conv_ref, act_ref, *rest):
        ws = rest[:n]
        dx_ref, gain_ref, taps_out, *g_refs = rest[n : n + 5]
        weight, dconv, dgated = rest[n + 5 :]
        join(place_ref, ws, weight)
        down = grad_ref[...]
        low = down.astype(bf16)
        put(g_refs, plan, place_ref, dot_rows(act_ref[...], low), 32, 16, 0)
        inner, inner_scale = stats(conv_ref[...])
        inner_gain = vec_ref[34:35, :]
        act_in = inner * inner_gain
        grad_act = dot_cols(low, weight[:, 2 * D :]) * slope_of(act_in, logistic(act_in))
        grad_conv, gain_inner = norm_back(grad_act, inner, inner_scale, inner_gain)
        for s in range(count):
            for c in range(cols):
                dconv[s, c, :each, :] = grad_conv[s * each : (s + 1) * each, c * 128 : (c + 1) * 128]
                dconv[s, c, each:, :] = jnp.zeros((LEAD, 128), f32)
        for c in range(cols):
            lanes = slice(c * 128, (c + 1) * 128)
            taps = vec_ref[0:32, lanes]

            def step(i, sums):
                s = i // (each // 8)
                t = (i % (each // 8)) * 8
                here = dconv[s, c, pl.ds(pl.multiple_of(t, 8), 8), :]
                total = jnp.zeros((8, 128), f32)
                new = []
                for k in range(KERNEL):
                    new.append(sums[k] + here * gated_ref[s, c, pl.ds(t + k + LEAD - KERNEL + 1, 8), :])
                    total = total + taps[k : k + 1] * dconv[s, c, pl.ds(t + KERNEL - 1 - k, 8), :]
                dgated[pl.ds(pl.multiple_of(i * 8, 8), 8), lanes] = total
                return tuple(new)

            sums = lax.fori_loop(0, rows // 8, step, tuple(jnp.zeros((8, 128), f32) for _ in range(KERNEL)))
            found = [jnp.sum(v, axis=0, keepdims=True) for v in sums]
            taps_out[:, lanes] = jnp.concatenate(found + [jnp.zeros((1, 128), f32)], axis=0)
        grad_gated = dgated[...]
        sig_wide = sig_ref[...]
        linear_sig = jnp.concatenate(
            [
                jnp.concatenate([gated_ref[s, c, LEAD:, :] for c in range(cols)], axis=1)
                for s in range(count)
            ],
            axis=0,
        )
        grad_one = (grad_gated * sig_wide).astype(bf16)
        grad_two = (grad_gated * linear_sig * (1.0 - sig_wide)).astype(bf16)
        entry_low = entry_ref[...]
        put(g_refs, plan, place_ref, dot_rows(entry_low, grad_one), 0, 16, 0)
        put(g_refs, plan, place_ref, dot_rows(entry_low, grad_two), 16, 16, 0)
        grad_entry = dot_cols(grad_one, weight[:, :D]) + dot_cols(grad_two, weight[:, D : 2 * D])
        normed, scale = stats(x_ref[...])
        back, gain_outer = norm_back(grad_entry, normed, scale, vec_ref[33:34, :])
        dx_ref[...] = down + back
        gain_ref[...] = jnp.concatenate([gain_outer, gain_inner, jnp.zeros((6, D), f32)], axis=0)

    return call(
        kernel,
        [
            shape((rows, D), f32),
            shape((8, D), f32),
            shape((32, D), f32),
            *halves(CONV_ROWS),
        ],
        [place, grad, values, vec, entry, gated, sig, conved, act, *parts],
        [smem()] + [vmem()] * (8 + n),
        [
            pltpu.VMEM((D, 3 * D), bf16),
            pltpu.VMEM((count, cols, each + LEAD, 128), f32),
            pltpu.VMEM((rows, D), f32),
        ],
        "convolve_back",
    )


def adam(weight, moment, square, grad):
    new_moment = BETA_FIRST * moment + (1.0 - BETA_FIRST) * grad
    new_square = BETA_SECOND * square + (1.0 - BETA_SECOND) * grad * grad
    first = new_moment * (1.0 / (1.0 - BETA_FIRST**STEP))
    second = new_square * (1.0 / (1.0 - BETA_SECOND**STEP))
    update = first / (jnp.sqrt(second) + ADAM_EPSILON) + WEIGHT_DECAY * weight
    return new_moment, new_square, update


def folded(values):
    squares = jnp.sum((values * values).reshape(-1, values.shape[-1]), axis=0, keepdims=True)
    total = squares[:, :128]
    for c in range(1, values.shape[-1] // 128):
        total = total + squares[:, c * 128 : (c + 1) * 128]
    return total


def update_matrix(layer, pieces, block, spots, states, given, name):
    count = spots.shape[0]
    rows, cols = states[0].shape[1] // count, states[0].shape[2]
    given = given or ()

    half = count // 2

    def kernel(spot_ref, g0_near, g0_far, g1_near, g1_far, w_ref, m_ref, q_ref, *rest):
        g_out, u_out, m_out, q_out, sums = rest[len(given) :]
        index = 2 * pl.program_id(0)

        @pl.when(pl.program_id(0) == 0)
        def _():
            sums[...] = jnp.zeros_like(sums)

        grads = []
        for k, near, far in ((0, g0_near, g0_far), (1, g1_near, g1_far)):
            raw = jnp.where(spot_ref[index + k] < half, near[0], far[0]).astype(f32)
            grads.append(jnp.concatenate([raw[k * rows : (k + 1) * rows] for k in range(cols // D)], axis=1))
        grad = jnp.concatenate(grads, axis=0)
        weight = w_ref[0]
        new_moment, new_square, update = adam(weight, m_ref[0], q_ref[0], grad)
        g_out[0] = grad
        u_out[0] = update
        m_out[0] = new_moment
        q_out[0] = new_square
        sums[...] += jnp.concatenate([folded(weight), folded(update), jnp.zeros((6, 128), f32)], axis=0)

    tile = pl.BlockSpec((1, 2 * rows, cols), lambda p, spot: (layer, p, 0))
    return pl.pallas_call(
        kernel,
        out_shape=[shape(states[0].shape, f32)] * 4 + [shape((8, 128), f32)],
        grid_spec=pltpu.PrefetchScalarGridSpec(
            num_scalar_prefetch=1,
            grid=(count // 2,),
            in_specs=[
                pl.BlockSpec((1, 64, D), lambda p, spot, k=k: (spot[2 * p + k] % half, block, 0))
                for k in (0, 0, 1, 1)
            ]
            + [tile] * 3
            + [pl.BlockSpec(memory_space=pl.ANY)] * len(given),
            out_specs=[tile] * 4 + [pl.BlockSpec((8, 128), lambda p, spot: (0, 0))],
        ),
        input_output_aliases={8 + k: k for k in range(len(given))},
        compiler_params=pltpu.CompilerParams(vmem_limit_bytes=STREAM_LIMIT),
        name=name,
    )(spots, *pieces, *pieces, *states, *given)


def move_layer(layer, win, in_update, in_factor, wout, out_update, out_factor):
    steps = 4
    tiles = [pl.BlockSpec((1, w.shape[1] // steps, w.shape[2]), lambda p: (layer, p, 0)) for w in (win, wout)]

    def kernel(factor_ref, w0, u0, w1, u1, out0, out1):
        out0[...] = w0[...] - (LEARN_RATE * factor_ref[0]) * u0[...]
        out1[...] = w1[...] - (LEARN_RATE * factor_ref[1]) * u1[...]

    return pl.pallas_call(
        kernel,
        out_shape=[shape(win.shape, f32), shape(wout.shape, f32)],
        grid=(steps,),
        in_specs=[smem(), tiles[0], tiles[0], tiles[1], tiles[1]],
        out_specs=tiles,
        input_output_aliases={2: 0, 4: 1},
        compiler_params=pltpu.CompilerParams(vmem_limit_bytes=STREAM_LIMIT),
        name="move_layer",
    )(jnp.stack([in_factor, out_factor]), win, in_update, wout, out_update)


def move_rest(attn, attn_update, conv, conv_update, factors):
    steps = 4
    rows = attn.shape[1] // steps
    attn_tile = pl.BlockSpec((4, rows, D), lambda p: (0, p, 0))
    conv_tile = pl.BlockSpec((rows, 3 * D), lambda p: (p, 0))

    def kernel(factor_ref, w0, u0, w1, u1, out0, out1):
        for k in range(4):
            out0[k] = w0[k] - (LEARN_RATE * factor_ref[k]) * u0[k]
        for k, lanes in ((4, slice(0, 2 * D)), (5, slice(2 * D, 3 * D))):
            out1[:, lanes] = w1[:, lanes] - (LEARN_RATE * factor_ref[k]) * u1[:, lanes]

    return pl.pallas_call(
        kernel,
        out_shape=[shape(attn.shape, f32), shape(conv.shape, f32)],
        grid=(steps,),
        in_specs=[smem(), attn_tile, attn_tile, conv_tile, conv_tile],
        out_specs=[attn_tile, conv_tile],
        input_output_aliases={2: 0, 4: 1},
        compiler_params=pltpu.CompilerParams(vmem_limit_bytes=STREAM_LIMIT),
        name="move_rest",
    )(factors, attn, attn_update, conv, conv_update)


def packed(gains_first, gains_attn, gains_conv, gains_last, taps, rel_wide, each):
    edge = 2 * each - BACK

    def kernel(g0, g1, g2, g4, taps_ref, rel_ref, out_ref, rel):
        out_ref[...] = jnp.zeros_like(out_ref)
        out_ref[0:KERNEL, :] = taps_ref[0:KERNEL, :]
        out_ref[31:32, :] = g0[0:1, :]
        out_ref[32:33, :] = g1[0:1, :]
        out_ref[33:35, :] = g2[0:2, :]
        out_ref[35:37, :] = g4[0:2, :]
        half = rel_ref[:, :HEAD] + rel_ref[:, HEAD:]
        rel[...] = jnp.zeros_like(rel)
        rel[0:1, :] = jnp.sum(half[each : edge + 8] * (lax.broadcasted_iota(jnp.int32, (each - BACK + 8, 1), 0) <= each - BACK), axis=0, keepdims=True)
        rel[0:BACK, :] = rel[0:BACK, :] + half[edge:] * (lax.broadcasted_iota(jnp.int32, (BACK, 1), 0) > 0)
        rel[BACK : BACK + AHEAD, :] = half[:AHEAD]
        rel[RELS - 1 : RELS, :] = jnp.sum(half[AHEAD:each], axis=0, keepdims=True)
        for b in range(5):
            out_ref[40:56, b * HEAD : (b + 1) * HEAD] = rel[b * 16 : b * 16 + 16, :]

    return call(
        kernel,
        [shape((56, D), f32)],
        [gains_first, gains_attn, gains_conv, gains_last, taps, rel_wide],
        [vmem()] * 6,
        [pltpu.VMEM((80, HEAD), f32)],
        "packed",
    )[0]


def update_rest(pieces, spots, attn, conv):
    count = spots.shape[0]
    rows = 2 * (attn[0].shape[1] // count)

    half = count // 2

    def kernel(spot_ref, g0_near, g0_far, g1_near, g1_far, wa, ma, qa, wc, mc, qc, *outs):
        ga_out, ua_out, ma_out, qa_out, qo_out, gc_out, uc_out, mc_out, qc_out, sums = outs
        index = pl.program_id(0)

        @pl.when(index == 0)
        def _():
            sums[...] = jnp.zeros_like(sums)

        raws = [
            jnp.where(spot_ref[2 * index + k] < half, near[0], far[0])
            for k, near, far in ((0, g0_near, g0_far), (1, g1_near, g1_far))
        ]
        found = []
        for k in range(4):
            low = CONV_ROWS + k * 16
            grad = jnp.concatenate([g[low : low + 16] for g in raws], axis=0).astype(f32)
            weight = wa[k]
            new_moment, new_square, update = adam(weight, ma[k], qa[k], grad)
            ga_out[k] = grad
            ua_out[k] = update
            ma_out[k] = new_moment
            if k < 3:
                qa_out[k] = new_square
            else:
                qo_out[...] = new_square
            found += [folded(weight), folded(update)]
        for low, high in ((0, 2), (2, 3)):
            lanes = slice(low * D, high * D)
            parts = [
                jnp.concatenate([g[k * 16 : (k + 1) * 16] for k in range(low, high)], axis=1) for g in raws
            ]
            grad = jnp.concatenate(parts, axis=0).astype(f32)
            weight = wc[:, lanes]
            new_moment, new_square, update = adam(weight, mc[:, lanes], qc[:, lanes], grad)
            gc_out[:, lanes] = grad
            uc_out[:, lanes] = update
            mc_out[:, lanes] = new_moment
            qc_out[:, lanes] = new_square
            found += [folded(weight), folded(update)]
        sums[...] += jnp.concatenate(found + [jnp.zeros((4, 128), f32)], axis=0)

    attn_block = pl.BlockSpec((4, rows, D), lambda p, spot: (0, p, 0))
    conv_block = pl.BlockSpec((rows, 3 * D), lambda p, spot: (p, 0))
    three = pl.BlockSpec((3, rows, D), lambda p, spot: (0, p, 0))
    one = pl.BlockSpec((rows, D), lambda p, spot: (p, 0))
    side = attn[0].shape[1]
    return pl.pallas_call(
        kernel,
        out_shape=[shape(attn[0].shape, f32)] * 3
        + [shape((3, side, D), f32), shape((side, D), f32)]
        + [shape(conv[0].shape, f32)] * 4
        + [shape((16, 128), f32)],
        grid_spec=pltpu.PrefetchScalarGridSpec(
            num_scalar_prefetch=1,
            grid=(count // 2,),
            in_specs=[
                pl.BlockSpec((1, CONV_ROWS + ATTN_ROWS, D), lambda p, spot, k=k: (spot[2 * p + k] % half, 0, 0))
                for k in (0, 0, 1, 1)
            ]
            + [attn_block] * 3
            + [conv_block] * 3,
            out_specs=[attn_block] * 3
            + [three, one]
            + [conv_block] * 4
            + [pl.BlockSpec((16, 128), lambda p, spot: (0, 0))],
        ),
        compiler_params=pltpu.CompilerParams(vmem_limit_bytes=STREAM_LIMIT),
        name="update_rest",
    )(spots, *pieces, *pieces, *attn, *conv)


def move(weight, update, factor):
    return weight - LEARN_RATE * factor * update


def ratio_of(sums):
    weight, update = sums[0::2], sums[1::2]
    return jnp.sqrt(weight), jnp.sqrt(update), jnp.sqrt(weight) / jnp.sqrt(update + RATIO_EPSILON)


def body(
    frames,
    lengths,
    cotangent,
    ffn_in,
    ffn_in_moment,
    ffn_in_square,
    ffn_out,
    ffn_out_moment,
    ffn_out_square,
    attn_proj,
    attn_moment,
    attn_square,
    conv_proj,
    conv_moment,
    conv_square,
    vectors,
    vectors_moment,
    vectors_square,
    rel_keys,
    rel_moment,
    rel_square,
):
    groups, shards = lax.axis_size("group"), lax.axis_size("shard")
    plan = Plan(groups, shards)
    group, shard = lax.axis_index("group"), lax.axis_index("shard")
    core = jnp.bitwise_and(group, 1)
    count, each, _ = frames.shape
    mine = jnp.int32(0)
    for step in plan.order:
        bit = jnp.right_shift(group if step[0] == "group" else shard, step[1]) & 1
        mine = mine * 2 + bit
    kept = jnp.int32(0)
    for step in plan.kept:
        kept = kept * 2 + (jnp.right_shift(group, step[1]) & 1)
    spots = jnp.array([plan.kept_place(p) for p in range(plan.owned)], jnp.int32) ^ kept
    place = jnp.stack([shard, core, mine]).astype(jnp.int32)

    first_halves = rounded_halves(plan, core, (ffn_in, 1, 0), (ffn_out, 1, 0))
    rows, halves_left = rounded_rows(plan, core, ffn_in, ffn_out, attn_proj, conv_proj)
    win0, wout0 = (Fetch(w, 0, plan, r, v, 0) for w, r, v in zip((ffn_in, ffn_out), rows, first_halves))
    watt = Fetch(attn_proj, 1, plan, rows[4], halves_left[0])
    wconv = Fetch(conv_proj, 0, plan, rows[5], halves_left[1])
    win1, wout1 = (Fetch(w, 0, plan, r, v, 1) for w, r, v in zip((ffn_in, ffn_out), rows[2:4], halves_left[2:]))
    win0.near()
    vec = lax.all_gather(vectors.astype(bf16), "shard", axis=1, tiled=True) if shards != 2 else None
    if vec is None:
        (low,) = gate([vectors.astype(bf16)], [first_halves[0]])
        other = swap(low, ("shard", 0))
        vec = jnp.where(shard == 0, jnp.concatenate([low, other], 1), jnp.concatenate([other, low], 1))
    vec = jnp.concatenate([vec.astype(f32), jnp.zeros((3, D), f32)], axis=0)
    rel_low = rel_keys.astype(bf16)
    table = jnp.concatenate(
        [
            rel_low[BACK:],
            jnp.broadcast_to(rel_low[RELS - 1 :], (each - AHEAD - 1, HEAD)),
            jnp.broadcast_to(rel_low[:1], (each - BACK, HEAD)),
            rel_low[:BACK],
        ],
        axis=0,
    )
    table = jnp.concatenate([table, table], axis=1)

    flat = frames.reshape(count * each, D)
    if shards == 2:
        order((win0,), (rows[0],))
    order((wout0,), (win0.value, vec))
    wout0.near()
    win0 = win0.far()
    entry0, hidden0, slope0 = ffn_first_up(flat, vec, win0, place)
    order((watt,), (wout0.value, entry0))
    watt.near()
    order((wout0,), (entry0,))
    order((wconv,), (watt.value,))
    order((win1,), (watt.value,))
    wconv.near()
    win1.near()
    wout0 = wout0.far()
    hidden0, watt.value = gate([hidden0, watt.value], [entry0])
    watt = watt.far()
    x1 = ffn_first_down(flat, hidden0, wout0, place)
    x2, *kept_attn = attend(x1, vec, table, lengths, watt, place, plan)
    order((wconv,), (x2,))
    order((wout1,), (x2,))
    wout1.near()
    wconv = wconv.far()
    x3, *kept_conv = convolve(x2, vec, wconv, place, plan, count)
    order((win1,), (x3,))
    win1 = win1.far()
    order((wout1,), (x3,))
    wout1 = wout1.far()
    output, d3, gains_last, *pieces = ffn_last(
        x3, vec, cotangent.reshape(count * each, D), lengths, win1, wout1, place, plan
    )
    last = Chain(*pieces, plan)
    d2, gains_conv, taps, *pieces = beside(
        [last], lambda d: convolve_back(d, x2, vec, kept_conv, wconv, place, plan, count), [d3], 1
    )
    conv = Chain(*pieces, plan)
    d1, gains_attn, rel_wide, *pieces = beside(
        [last, conv], lambda d: attend_back(d, x1, vec, kept_attn, table, watt, place, plan, count), [d2], 1
    )
    attn = Chain(*pieces, plan)
    before0, *pieces = beside(
        [last, conv, attn], lambda d: ffn_first_out(d, hidden0, slope0, wout0, place, plan), [d1], 0
    )
    first_out = Chain(*pieces, plan)
    early = [last, attn, first_out] if len(conv.todo) < len(attn.todo) else [last, conv, attn, first_out]
    d0, gains_first, *pieces = beside(
        early, lambda b: ffn_first_in(d1, flat, vec, entry0, b, win0, place, plan), [before0], 1
    )
    first_in = Chain(*pieces, plan)
    middle = merged(conv, attn, plan)
    small = Everywhere(packed(gains_first, gains_attn, gains_conv, gains_last, taps, rel_wide, each), plan)
    advance([last, middle, first_out, first_in, small], 1)
    advance([last, middle, first_in, small], 1)
    first = merged(first_out, first_in, plan)
    chains = [last, middle, first, small]
    advance(chains, len(last.todo))
    in_states = (ffn_in, ffn_in_moment, ffn_in_square)
    out_states = (ffn_out, ffn_out_moment, ffn_out_square)
    *half_out, sums_out1 = beside(
        chains, lambda *v: update_matrix(1, v, 1, spots, out_states, None, "update_out1"), last.kept, -1
    )
    *half_in, sums_in1 = beside(
        chains, lambda *v: update_matrix(1, v, 0, spots, in_states, None, "update_in1"), last.kept, -1
    )
    advance(chains, len(middle.todo))
    attn_states = (attn_proj, attn_moment, attn_square)
    conv_states = (conv_proj, conv_moment, conv_square)
    (attn_grad, attn_up, attn_m, attn_q, attn_qo, conv_grad, conv_up, conv_m, conv_q, sums_rest) = beside(
        chains, lambda *v: update_rest(v, spots, attn_states, conv_states), middle.kept, -1
    )
    advance([small], len(small.todo))
    small = small.kept
    wide = vectors.shape[1]
    vec_grad = lax.dynamic_slice(small, (0, shard * wide), (KERNEL + 6, wide))
    rel_grad = jnp.concatenate([small[40:56, b * HEAD : (b + 1) * HEAD] for b in range(5)], axis=0)[:RELS]
    vec_m, vec_q, vec_up = adam(vectors, vectors_moment, vectors_square, vec_grad)
    rel_m, rel_q, rel_up = (
        v.T for v in adam(rel_keys.T, rel_moment.T, rel_square.T, rel_grad.T)
    )

    vec_sums = []
    for part in (vectors, vec_up):
        squares = jnp.sum(part * part, axis=1)
        vec_sums.append(jnp.concatenate([jnp.sum(squares[:KERNEL])[None], squares[KERNEL:]]))
    early = jnp.sum(jnp.concatenate([sums_in1[:2], sums_out1[:2], sums_rest[:12]], axis=0), axis=1)
    early = sum_shards(jnp.concatenate([early, jnp.stack(vec_sums, axis=1).reshape(-1)]), plan)
    early_ratio = ratio_of(early)
    fast = early_ratio[2]
    half_in[1], half_out[1] = beside(
        chains,
        lambda u: move_layer(1, ffn_in, u, fast[0], ffn_out, half_out[1], fast[1]),
        [half_in[1]],
        0,
    )
    advance(chains, len(first.todo))
    out_grad, out_up, out_m, out_q, sums_out0 = update_matrix(
        0, first.kept, 0, spots, out_states, half_out, "update_out0"
    )
    in_grad, in_up, in_m, in_q, sums_in0 = update_matrix(
        0, first.kept, 1, spots, in_states, half_in, "update_in0"
    )
    final = sum_shards(jnp.sum(jnp.concatenate([sums_in0[:2], sums_out0[:2]], axis=0), axis=1), plan)
    rel_sums = jnp.stack([jnp.sum(rel_keys.T * rel_keys.T), jnp.sum(rel_up.T * rel_up.T)])
    late_ratio = ratio_of(rel_sums)
    final_ratio = ratio_of(final)

    def spread(n):
        e, l = early_ratio[n], late_ratio[n]
        none = jnp.zeros((1,), f32)
        return jnp.concatenate([none, e[0:1], none, e[1:2], e[2:15], l[0:1]])

    column = lax.broadcasted_iota(jnp.int32, (2, 18), 1)
    last_in = jnp.stack([final_ratio[0][0], final_ratio[1][0]])[:, None]
    last_out = jnp.stack([final_ratio[0][1], final_ratio[1][1]])[:, None]
    known = jnp.stack([spread(0), spread(1)])
    trust_norms = jnp.where(column == 0, last_in, jnp.where(column == 2, last_out, known))
    ffn_in_new, ffn_out_new = move_layer(
        0, ffn_in, in_up, final_ratio[2][0], ffn_out, out_up, final_ratio[2][1]
    )
    attn_new, conv_new = move_rest(attn_proj, attn_up, conv_proj, conv_up, fast[2:8])
    vec_factor = jnp.concatenate([jnp.full((KERNEL,), fast[8]), fast[9:15]])[:, None]
    return (
        output.reshape(frames.shape),
        d0.reshape(frames.shape),
        in_grad,
        ffn_in_new,
        in_m,
        in_q,
        out_grad,
        ffn_out_new,
        out_m,
        out_q,
        attn_grad,
        attn_new,
        attn_m,
        attn_q,
        attn_qo,
        conv_grad,
        conv_new,
        conv_m,
        conv_q,
        vec_grad,
        move(vectors, vec_up, vec_factor),
        vec_m,
        vec_q,
        rel_grad,
        move(rel_keys.T, rel_up.T, late_ratio[2][0]).T,
        rel_m,
        rel_q,
        trust_norms,
    )


def solution(mesh):
    return jax.shard_map(
        body,
        mesh=mesh,
        in_specs=(
            P(("group", "shard"), None, None),
            P(("group", "shard")),
            P(("group", "shard"), None, None),
            P(None, "shard", None),
            P(None, "shard", None),
            P(None, "shard", None),
            P(None, "shard", None),
            P(None, "shard", None),
            P(None, "shard", None),
            P(None, "shard", None),
            P(None, "shard", None),
            P(None, "shard", None),
            P("shard", None),
            P("shard", None),
            P("shard", None),
            P(None, "shard"),
            P(None, "shard"),
            P(None, "shard"),
            P(),
            P(),
            P(),
        ),
        out_specs=(
            P(("group", "shard"), None, None),
            P(("group", "shard"), None, None),
            P(None, "shard", None),
            P(None, "shard", None),
            P(None, "shard", None),
            P(None, "shard", None),
            P(None, "shard", None),
            P(None, "shard", None),
            P(None, "shard", None),
            P(None, "shard", None),
            P(None, "shard", None),
            P(None, "shard", None),
            P(None, "shard", None),
            P(None, "shard", None),
            P("shard", None),
            P("shard", None),
            P("shard", None),
            P("shard", None),
            P("shard", None),
            P(None, "shard"),
            P(None, "shard"),
            P(None, "shard"),
            P(None, "shard"),
            P(),
            P(),
            P(),
            P(),
            P(),
        ),
        check_vma=False,
    )
```

```python
import math

import jax
import jax.numpy as jnp
from jax import lax
from jax.experimental import pallas as pl
from jax.experimental.pallas import tpu as pltpu
from jax.sharding import PartitionSpec as P

D = 512
FF = 2048
HEADS = 8
HEAD = 64
KERNEL = 31
BACK = 64
AHEAD = 8
RELS = 73
STEP = 10
PIECES = 32
LEAD = 32
FFN_ROWS = 128
ATTN_ROWS = 64
CONV_ROWS = 48

NORM_EPSILON = 1e-05
ADAM_EPSILON = 1e-06
RATIO_EPSILON = 1e-06
BETA_FIRST = 0.9
BETA_SECOND = 0.999
WEIGHT_DECAY = 0.01
LEARN_RATE = 0.5
MASKED_SCORE = -1e30

bf16 = jnp.bfloat16
f32 = jnp.float32
VMEM_LIMIT = 24 * 1024 * 1024
STREAM_LIMIT = 60 * 1024 * 1024


def vmem():
    return pl.BlockSpec(memory_space=pltpu.VMEM)


def smem():
    return pl.BlockSpec(memory_space=pltpu.SMEM)


def shape(dims, kind):
    return jax.ShapeDtypeStruct(dims, kind)


def dot(left, right):
    return jnp.dot(left, right, preferred_element_type=f32)


def dot_rows(left, right):
    return lax.dot_general(left, right, (((0,), (0,)), ((), ())), preferred_element_type=f32)


def dot_cols(left, right):
    return lax.dot_general(left, right, (((1,), (1,)), ((), ())), preferred_element_type=f32)


def stats(values):
    centred = values - jnp.mean(values, axis=-1, keepdims=True)
    scale = lax.rsqrt(jnp.mean(centred * centred, axis=-1, keepdims=True) + NORM_EPSILON)
    return centred * scale, scale


def norm_back(grad, normed, scale, gain):
    grad_gain = jnp.sum(grad * normed, axis=0, keepdims=True)
    scaled = grad * gain
    inner = jnp.mean(scaled * normed, axis=-1, keepdims=True)
    back = scale * (scaled - jnp.mean(scaled, axis=-1, keepdims=True) - normed * inner)
    return back, grad_gain


def logistic(values):
    return 1.0 / (1.0 + jnp.exp(-values))


def slope_of(values, sig):
    return sig * (1.0 + values * (1.0 - sig))


class Plan:
    def __init__(self, groups, shards):
        self.groups, self.shards = groups, shards
        shard_bits = shards.bit_length() - 1
        group_bits = groups.bit_length() - 1
        self.used = min(5 - shard_bits, group_bits)
        self.owned = PIECES // shards
        order = [("group", 0)] + [("shard", b) for b in range(shard_bits)]
        order += [("group", b) for b in range(1, self.used)]
        self.order = order
        self.rest = [("group", b) for b in range(self.used, group_bits)]
        self.shard_bits = [("shard", b) for b in range(shard_bits)]
        self.kept = [step for step in order if step[0] == "group"]

    def piece_bit(self, step):
        return step[1] if step[0] == "group" else self.used + step[1]

    def place(self, piece):
        out = 0
        for step in self.order:
            out = out * 2 + ((piece >> self.piece_bit(step)) & 1)
        return out

    def kept_place(self, piece):
        out = 0
        for step in self.kept:
            out = out * 2 + ((piece >> step[1]) & 1)
        return out


def swap(values, step):
    axis, bit = step
    count = lax.axis_size(axis)
    return lax.ppermute(values, axis, [(i, i ^ (1 << bit)) for i in range(count)])


def add_low(left, right):
    return (left.astype(f32) + right.astype(f32)).astype(bf16)


class Chain:
    def __init__(self, kept, sent, plan):
        order, back = list(plan.order), list(reversed(plan.kept))
        self.todo = [("halve", step) for step in order]
        self.todo += [("add", step) for step in plan.rest] + [("keep", step) for step in back]
        self.kept, self.sent = kept, (sent,)

    def start(self):
        if self.todo:
            self.found = swap(self.sent[0], self.todo[0][1])

    def finish(self):
        if not self.todo:
            return
        kind, _ = self.todo.pop(0)
        coming = self.todo[0][0] if self.todo else None
        if kind == "keep":
            if coming is None:
                self.kept = (self.kept, self.found)
            else:
                self.kept = jnp.concatenate([self.kept, self.found], axis=0)
                self.sent = (self.kept,)
        elif coming == "halve":
            half = self.kept.shape[0] // 2
            low = add_low(self.kept[:half], self.found[:half])
            self.sent = (add_low(self.kept[half:], self.found[half:]),)
            self.kept = low
        else:
            self.kept = add_low(self.kept, self.found)
            self.sent = (self.kept,)


def merged(one, two, plan):
    both = Chain(
        jnp.concatenate([one.kept, two.kept], axis=1),
        jnp.concatenate([one.sent[0], two.sent[0]], axis=1),
        plan,
    )
    both.todo = list(one.todo)
    return both


class Everywhere:
    def __init__(self, values, plan):
        self.todo = plan.order + plan.rest
        self.kept, self.sent = values, (values,)

    def start(self):
        if self.todo:
            self.found = swap(self.sent[0], self.todo[0])

    def finish(self):
        if self.todo:
            self.todo = self.todo[1:]
            self.kept = self.kept + self.found
            self.sent = (self.kept,)


def gate(values, signs):
    held = lax.optimization_barrier((tuple(values), tuple(signs)))
    return held[0]


def beside(chains, run, first, sign):
    chains = [chain for chain in chains if chain.todo]
    first = gate(first, [v for chain in chains for v in chain.sent])
    for chain in chains:
        chain.start()
    outs = run(*first)
    for chain, value in zip(chains, gate([chain.kept for chain in chains], [outs[sign]])):
        chain.kept = value
    for chain in chains:
        chain.finish()
    return outs


def advance(chains, rounds):
    for _ in range(rounds):
        busy = [chain for chain in chains if chain.todo]
        for chain, value in zip(busy, gate([chain.sent for chain in busy], [])):
            chain.sent = tuple(value)
        for chain in busy:
            chain.start()
        for chain in busy:
            chain.finish()


def sum_shards(values, plan):
    for step in plan.shard_bits:
        values = values + swap(values, step)
    return values


def rounded_halves(plan, core, *owns):
    if plan.shards != 2:
        return [None] * len(owns)
    ins, specs, outs, out_specs = [], [], [], []
    for own, dim, layer in owns:
        dims = list(own.shape)
        dims[dim] //= 2
        if layer is not None:
            dims[0] = 1
        axes = len(dims)
        ins.append(own)

        def at(i, core_ref, axes=axes, dim=dim, layer=layer):
            return tuple(core_ref[0] if d == dim else (layer or 0) if d == 0 else 0 for d in range(axes))

        specs.append(pl.BlockSpec(tuple(dims), at))
        outs.append(shape(tuple(dims), bf16))
        out_specs.append(pl.BlockSpec(tuple(dims), lambda i, core_ref, axes=axes: (0,) * axes))

    def kernel(core_ref, *refs):
        for k in range(len(owns)):
            refs[len(owns) + k][...] = refs[k][...].astype(bf16)

    found = pl.pallas_call(
        kernel,
        out_shape=outs,
        grid_spec=pltpu.PrefetchScalarGridSpec(
            num_scalar_prefetch=1, grid=(1,), in_specs=specs, out_specs=out_specs
        ),
        compiler_params=pltpu.CompilerParams(vmem_limit_bytes=STREAM_LIMIT),
        name="rounded_halves",
    )(core.reshape(1).astype(jnp.int32), *ins)
    return [v if layer is None else v[0] for v, (_, _, layer) in zip(found, owns)]


def rounded_rows(plan, core, ffn_in, ffn_out, attn_proj, conv_proj):
    if plan.shards != 2:
        return [None] * 6, [None] * 4
    owns = [(ffn_in, 0), (ffn_out, 0), (ffn_in, 1), (ffn_out, 1)]
    outs = [shape(w.shape[1:], bf16) for w, _ in owns] + [shape(attn_proj.shape, bf16), shape(conv_proj.shape, bf16)]
    halved = [outs[4], outs[5], outs[2], outs[3]]
    for v in halved:
        dims = list(v.shape)
        dims[-2] //= 2
        outs.append(shape(tuple(dims), bf16))

    def kernel(core_ref, in_ref, out_ref, attn_ref, conv_ref, *refs):
        rows = refs[:6]
        for layer in range(2):
            rows[2 * layer][...] = in_ref[layer].astype(bf16)
            rows[2 * layer + 1][...] = out_ref[layer].astype(bf16)
        rows[4][...] = attn_ref[...].astype(bf16)
        rows[5][...] = conv_ref[...].astype(bf16)
        for source, half_ref in zip((rows[4], rows[5], rows[2], rows[3]), refs[6:]):
            half = half_ref.shape[-2]
            span = pl.ds(pl.multiple_of(core_ref[0] * half, half), half)
            half_ref[...] = source[:, span, :] if len(half_ref.shape) == 3 else source[span, :]

    found = call(
        kernel,
        outs,
        [core.reshape(1).astype(jnp.int32), ffn_in, ffn_out, attn_proj, conv_proj],
        [smem()] + [vmem()] * 4,
        (),
        "rounded_rows",
    )
    return found[:6], found[6:]


class Fetch:
    def __init__(self, own, dim, plan, rows, half, layer=None):
        self.own, self.plan, self.dim = rows, plan, dim
        if plan.shards == 2:
            self.value = half
        else:
            one = own if layer is None else own[layer]
            self.value = lax.all_gather(one.astype(bf16), "shard", axis=dim, tiled=True)

    def near(self):
        if self.plan.shards == 2:
            self.value = swap(self.value, ("shard", 0))

    def far(self):
        if self.plan.shards == 2:
            return (self.own, self.value, swap(self.value, ("group", 0)))
        return (self.value,)


def order(later, signs):
    for fetch, value in zip(later, gate([f.value for f in later], signs)):
        fetch.value = value


def join(place_ref, part_refs, whole_ref):
    if len(part_refs) == 1:
        whole_ref[...] = part_refs[0][...]
        return
    own, near, far = part_refs
    rows = own.shape[-2]
    half = rows // 2
    shard, core = place_ref[0], place_ref[1]
    first = pl.multiple_of(shard * rows, half)
    second = pl.multiple_of((1 - shard) * rows + core * half, half)
    third = pl.multiple_of((1 - shard) * rows + (1 - core) * half, half)
    if len(own.shape) == 2:
        whole_ref[pl.ds(second, half), :] = near[...]
        whole_ref[pl.ds(third, half), :] = far[...]
        whole_ref[pl.ds(first, rows), :] = own[...]
    else:
        for k in range(own.shape[0]):
            whole_ref[k, pl.ds(first, rows), :] = own[k]
            whole_ref[k, pl.ds(second, half), :] = near[k]
            whole_ref[k, pl.ds(third, half), :] = far[k]


def put(out_refs, plan, place_ref, value, row, rows_each, first, shift=0):
    kept_ref, sent_ref = out_refs
    low = value.astype(bf16)
    core, mine = place_ref[1] == 0, jnp.bitwise_xor(place_ref[2], shift)
    for k in range(0, value.shape[0] // rows_each, 2):
        even = low[k * rows_each : (k + 1) * rows_each]
        odd = low[(k + 1) * rows_each : (k + 2) * rows_each]
        spot = jnp.bitwise_xor(jnp.int32(plan.place(first + k)), jnp.bitwise_and(mine, PIECES // 2 - 1))
        kept_ref[spot, pl.ds(row, rows_each), :] = jnp.where(core, even, odd)
        sent_ref[spot, pl.ds(row, rows_each), :] = jnp.where(core, odd, even)


def halves(rows):
    return [shape((PIECES // 2, rows, D), bf16)] * 2


def call(kernel, outs, ins, specs, scratch=(), name=None):
    return pl.pallas_call(
        kernel,
        out_shape=list(outs),
        in_specs=specs,
        out_specs=[vmem()] * len(outs),
        scratch_shapes=list(scratch),
        compiler_params=pltpu.CompilerParams(vmem_limit_bytes=VMEM_LIMIT),
        name=name,
    )(*ins)


def ffn_ahead(values, gain, win, wout, entry_ref, hidden_ref, slope_ref, sum_ref):
    normed, _ = stats(values)
    entry_ref[...] = (normed * gain).astype(bf16)
    sum_ref[...] = jnp.zeros_like(sum_ref)

    def step(b, carry):
        cols = pl.ds(pl.multiple_of(b * D, D), D)
        before = dot(entry_ref[...], win[:, cols])
        sig = logistic(before)
        hidden = (before * sig).astype(bf16)
        hidden_ref[:, cols] = hidden
        slope_ref[:, cols] = slope_of(before, sig).astype(bf16)
        sum_ref[...] += dot(hidden, wout[cols, :])
        return carry

    lax.fori_loop(0, FF // D, step, 0)
    return sum_ref[...]


def ffn_behind(grad, values, gain, win, wout, entry_ref, hidden_ref, slope_ref, out_refs, plan, place_ref):
    normed, scale = stats(values)
    entry = entry_ref[...]
    branch = (0.5 * grad).astype(bf16)
    grad_entry = jnp.zeros(values.shape, f32)
    for b in range(FF // D):
        cols = slice(b * D, (b + 1) * D)
        put(out_refs, plan, place_ref, dot_rows(hidden_ref[:, cols], branch), 64, 64, 8 * b)
        grad_before = (dot_cols(branch, wout[cols, :]) * slope_ref[:, cols].astype(f32)).astype(bf16)
        put(out_refs, plan, place_ref, dot_rows(entry, grad_before), 16 * b, 16, 0)
        grad_entry = grad_entry + dot_cols(grad_before, win[:, cols])
    back, grad_gain = norm_back(grad_entry, normed, scale, gain)
    return grad + back, grad_gain


def ffn_first_up(frames, vec, win_parts, place):
    rows = frames.shape[0]
    n = len(win_parts)

    def kernel(place_ref, x_ref, vec_ref, *rest):
        wins = rest[:n]
        entry_ref, hidden_ref, slope_ref, win = rest[n:]
        normed, _ = stats(x_ref[...].astype(f32))
        entry = (normed * vec_ref[31:32, :]).astype(bf16)
        entry_ref[...] = entry
        join(place_ref, wins, win)

        def step(b, carry):
            cols = pl.ds(pl.multiple_of(b * D, D), D)
            before = dot(entry_ref[...], win[:, cols])
            sig = logistic(before)
            hidden_ref[:, cols] = (before * sig).astype(bf16)
            slope_ref[:, cols] = slope_of(before, sig).astype(bf16)
            return carry

        lax.fori_loop(0, FF // D, step, 0)

    return call(
        kernel,
        [shape((rows, D), bf16), shape((rows, FF), bf16), shape((rows, FF), bf16)],
        [place, frames, vec, *win_parts],
        [smem()] + [vmem()] * 2 + [vmem()] * n,
        [pltpu.VMEM((D, FF), bf16)],
        "ffn_first_up",
    )


def ffn_first_down(frames, hidden, wout_parts, place):
    rows = frames.shape[0]
    n = len(wout_parts)

    def kernel(place_ref, x_ref, hidden_ref, *rest):
        wouts = rest[:n]
        out_ref, wout = rest[n:]
        join(place_ref, wouts, wout)
        out_ref[...] = x_ref[...].astype(f32) + 0.5 * dot(hidden_ref[...], wout[...])

    return call(
        kernel,
        [shape((rows, D), f32)],
        [place, frames, hidden, *wout_parts],
        [smem()] + [vmem()] * 2 + [vmem()] * n,
        [pltpu.VMEM((FF, D), bf16)],
        "ffn_first_down",
    )[0]


def ffn_last(values, vec, cotangent, lengths, win_parts, wout_parts, place, plan):
    rows = values.shape[0]
    count = lengths.shape[0]
    n = len(win_parts)

    def kernel(place_ref, len_ref, x_ref, vec_ref, cot_ref, *rest):
        wins, wouts = rest[:n], rest[n : 2 * n]
        y_ref, dx_ref, gain_ref, *g_refs = rest[2 * n : 2 * n + 5]
        win, wout, entry_ref, hidden_ref, slope_ref = rest[2 * n + 5 :]
        join(place_ref, wins, win)
        join(place_ref, wouts, wout)
        x = x_ref[...]
        gain = vec_ref[35:36, :]
        total = ffn_ahead(x, gain, win, wout, entry_ref, hidden_ref, slope_ref, dx_ref)
        normed, scale = stats(x + 0.5 * total)
        top = vec_ref[36:37, :]
        y_ref[...] = (normed * top).astype(bf16)
        each = rows // count
        grads = []
        for s in range(count):
            spot = lax.broadcasted_iota(jnp.int32, (each, 1), 0)
            part = cot_ref[s * each : (s + 1) * each, :].astype(f32)
            grads.append(jnp.where(spot < len_ref[s], part, 0.0))
        back, grad_top = norm_back(jnp.concatenate(grads, axis=0), normed, scale, top)
        grad, grad_gain = ffn_behind(
            back, x, gain, win, wout, entry_ref, hidden_ref, slope_ref, g_refs, plan, place_ref
        )
        dx_ref[...] = grad
        gain_ref[...] = jnp.concatenate([grad_gain, grad_top, jnp.zeros((6, D), f32)], axis=0)

    return call(
        kernel,
        [shape((rows, D), bf16), shape((rows, D), f32), shape((8, D), f32), *halves(FFN_ROWS)],
        [place, lengths, values, vec, cotangent, *win_parts, *wout_parts],
        [smem(), smem()] + [vmem()] * 3 + [vmem()] * (2 * n),
        [
            pltpu.VMEM((D, FF), bf16),
            pltpu.VMEM((FF, D), bf16),
            pltpu.VMEM((rows, D), bf16),
            pltpu.VMEM((rows, FF), bf16),
            pltpu.VMEM((rows, FF), bf16),
        ],
        "ffn_last",
    )


def ffn_first_out(grad, hidden, slope, wout_parts, place, plan):
    rows = grad.shape[0]
    n = len(wout_parts)

    def kernel(place_ref, grad_ref, hidden_ref, slope_ref, *rest):
        wouts = rest[:n]
        before_ref, *g_refs = rest[n : n + 3]
        (wout,) = rest[n + 3 :]
        join(place_ref, wouts, wout)
        branch = (0.5 * grad_ref[...]).astype(bf16)

        def step(b, carry):
            cols = pl.ds(pl.multiple_of(b * D, D), D)
            shift = jnp.bitwise_xor((b % 2) * plan.place(8), (b // 2) * plan.place(16))
            put(g_refs, plan, place_ref, dot_rows(hidden_ref[:, cols], branch), 0, 64, 0, shift)
            spread = dot_cols(branch, wout[cols, :])
            before_ref[:, cols] = (spread * slope_ref[:, cols].astype(f32)).astype(bf16)
            return carry

        lax.fori_loop(0, FF // D, step, 0)

    return call(
        kernel,
        [shape((rows, FF), bf16), *halves(64)],
        [place, grad, hidden, slope, *wout_parts],
        [smem()] + [vmem()] * 3 + [vmem()] * n,
        [pltpu.VMEM((FF, D), bf16)],
        "ffn_first_out",
    )


def ffn_first_in(grad, frames, vec, entry, before, win_parts, place, plan):
    rows = frames.shape[0]
    n = len(win_parts)

    def kernel(place_ref, grad_ref, x_ref, vec_ref, entry_ref, before_ref, *rest):
        wins = rest[:n]
        dx_ref, gain_ref, *g_refs = rest[n : n + 4]
        win, sum_ref = rest[n + 4 :]
        join(place_ref, wins, win)
        low = entry_ref[...]
        sum_ref[...] = jnp.zeros_like(sum_ref)

        def step(b, carry):
            cols = pl.ds(pl.multiple_of(b * D, D), D)
            low_row = pl.multiple_of(16 * b, 16)
            put(g_refs, plan, place_ref, dot_rows(low, before_ref[:, cols]), low_row, 16, 0)
            sum_ref[...] += dot_cols(before_ref[:, cols], win[:, cols])
            return carry

        lax.fori_loop(0, FF // D, step, 0)
        normed, scale = stats(x_ref[...].astype(f32))
        back, grad_gain = norm_back(sum_ref[...], normed, scale, vec_ref[31:32, :])
        dx_ref[...] = (grad_ref[...] + back).astype(bf16)
        gain_ref[...] = jnp.concatenate([grad_gain, jnp.zeros((7, D), f32)], axis=0)

    return call(
        kernel,
        [shape((rows, D), bf16), shape((8, D), f32), *halves(64)],
        [place, grad, frames, vec, entry, before, *win_parts],
        [smem()] + [vmem()] * 5 + [vmem()] * n,
        [pltpu.VMEM((D, FF), bf16), pltpu.VMEM((rows, D), f32)],
        "ffn_first_in",
    )


def attend(values, vec, rel_table, lengths, parts, place, plan):
    rows = values.shape[0]
    count = lengths.shape[0]
    each = rows // count
    n = len(parts)
    pairs = HEADS // 2

    def kernel(place_ref, len_ref, x_ref, vec_ref, rel_ref, *rest):
        ws = rest[:n]
        out_ref, entry_ref, qkv_ref, prob_ref, mix_ref, weight, mixed = rest[n:]
        join(place_ref, ws, weight)
        x = x_ref[...]
        normed, _ = stats(x)
        entry = (normed * vec_ref[32:33, :]).astype(bf16)
        entry_ref[...] = entry

        def project(k, carry):
            heads = dot(entry_ref[...], weight[k]).astype(bf16)
            for p in range(pairs):
                qkv_ref[k, p] = heads[:, p * 128 : (p + 1) * 128]
            return carry

        lax.fori_loop(0, 3, project, 0)
        lane = lax.broadcasted_iota(jnp.int32, (1, 128), 1)
        table = rel_ref[...]
        spot = lax.broadcasted_iota(jnp.int32, (1, each), 1)

        def step(i, carry):
            s = i // pairs
            p = i % pairs
            span = pl.ds(pl.multiple_of(s * each, each), each)
            query = qkv_ref[0, p, span, :]
            keys = qkv_ref[1, p, span, :]
            vals = qkv_ref[2, p, span, :]
            valid = spot < len_ref[s]
            both = []
            for h in range(2):
                mask = (lane < HEAD) if h == 0 else (lane >= HEAD)
                mine = jnp.where(mask, query, jnp.zeros_like(query))
                raw = dot_cols(mine, keys)
                skew = pltpu.roll(dot_cols(mine, table), 0, 1, stride=1, stride_axis=0)[:, :each]
                scores = jnp.where(valid, (raw + skew) * 0.125, MASKED_SCORE)
                grown = jnp.exp(scores - jnp.max(scores, axis=-1, keepdims=True))
                low = (grown * (1.0 / jnp.sum(grown, axis=-1, keepdims=True))).astype(bf16)
                prob_ref[2 * i + h] = low
                both.append(dot(low, vals))
            mixed[p, span, :] = jnp.where(lane < HEAD, both[0], both[1]).astype(bf16)
            return carry

        lax.fori_loop(0, count * pairs, step, 0)
        mix = jnp.concatenate([mixed[p] for p in range(pairs)], axis=1)
        mix_ref[...] = mix
        out_ref[...] = x + dot(mix, weight[3])

    return call(
        kernel,
        [
            shape((rows, D), f32),
            shape((rows, D), bf16),
            shape((3, pairs, rows, 128), bf16),
            shape((count * HEADS, each, each), bf16),
            shape((rows, D), bf16),
        ],
        [place, lengths, values, vec, rel_table, *parts],
        [smem(), smem()] + [vmem()] * (3 + n),
        [pltpu.VMEM((4, D, D), bf16), pltpu.VMEM((pairs, rows, 128), bf16)],
        "attend",
    )


def attend_back(grad, values, vec, kept, rel_table, parts, place, plan, count):
    rows = values.shape[0]
    each = rows // count
    n = len(parts)
    pairs = HEADS // 2
    entry, qkv, prob, mix = kept
    width = rel_table.shape[0]

    def kernel(place_ref, grad_ref, x_ref, vec_ref, entry_ref, qkv_ref, prob_ref, mix_ref, rel_ref, *rest):
        ws = rest[:n]
        dx_ref, gain_ref, rel_out, *g_refs = rest[n : n + 5]
        weight, dmix, dqkv = rest[n + 5 :]
        join(place_ref, ws, weight)
        down = grad_ref[...]
        low = down.astype(bf16)
        put(g_refs, plan, place_ref, dot_rows(mix_ref[...], low), 48, 16, 0)
        spread = dot_cols(low, weight[3]).astype(bf16)
        for p in range(pairs):
            dmix[p] = spread[:, p * 128 : (p + 1) * 128]
        lane = lax.broadcasted_iota(jnp.int32, (1, 128), 1)
        table = rel_ref[...]
        flip = (
            lax.broadcasted_iota(jnp.int32, (each, each), 0)
            + lax.broadcasted_iota(jnp.int32, (each, each), 1)
            == each - 1
        ).astype(bf16)
        rel_out[...] = jnp.zeros_like(rel_out)

        def step(i, carry):
            s = i // pairs
            p = i % pairs
            span = pl.ds(pl.multiple_of(s * each, each), each)
            query = qkv_ref[0, p, span, :]
            keys = qkv_ref[1, p, span, :]
            vals = qkv_ref[2, p, span, :]
            outer = dmix[p, span, :]
            grad_q = jnp.zeros((each, 128), f32)
            grad_k = jnp.zeros((each, 128), f32)
            grad_v = jnp.zeros((each, 128), f32)
            grad_r = jnp.zeros((width, 128), f32)
            for h in range(2):
                mask = (lane < HEAD) if h == 0 else (lane >= HEAD)

                def pick(v):
                    return jnp.where(mask, v, jnp.zeros_like(v))

                dout = pick(outer)
                q_own = pick(query)
                prob_low = prob_ref[2 * i + h]
                prob_wide = prob_low.astype(f32)
                dprob = dot_cols(dout, vals)
                inner = jnp.sum(prob_wide * dprob, axis=-1, keepdims=True)
                dscore = (prob_wide * (dprob - inner)).astype(bf16)
                grad_v = grad_v + dot_rows(prob_low, dout)
                grad_k = grad_k + dot_rows(dscore, q_own)
                turned = dot(flip, dscore)
                wide = jnp.concatenate([turned, jnp.zeros((each, width - each), f32)], axis=1)
                skew = pltpu.roll(wide, width - each + 1, 1, stride=1, stride_axis=0).astype(bf16)
                along = dot(flip, skew).astype(bf16)
                grad_q = grad_q + dot(dscore, pick(keys)) + dot(along, pick(table))
                grad_r = grad_r + dot_rows(along, q_own)
            dqkv[0, p, span, :] = (grad_q * 0.125).astype(bf16)
            dqkv[1, p, span, :] = (grad_k * 0.125).astype(bf16)
            dqkv[2, p, span, :] = grad_v.astype(bf16)
            rel_out[...] += grad_r * 0.125
            return carry

        lax.fori_loop(0, count * pairs, step, 0)
        dx_ref[...] = jnp.zeros_like(dx_ref)

        def project_back(k, carry):
            heads = jnp.concatenate([dqkv[k, p] for p in range(pairs)], axis=1)
            row = pl.multiple_of(16 * k, 16)
            put(g_refs, plan, place_ref, dot_rows(entry_ref[...], heads), row, 16, 0)
            dx_ref[...] += dot_cols(heads, weight[k])
            return carry

        lax.fori_loop(0, 3, project_back, 0)
        grad_entry = dx_ref[...]
        normed, scale = stats(x_ref[...])
        back, grad_gain = norm_back(grad_entry, normed, scale, vec_ref[32:33, :])
        dx_ref[...] = down + back
        gain_ref[...] = jnp.concatenate([grad_gain, jnp.zeros((7, D), f32)], axis=0)

    return call(
        kernel,
        [
            shape((rows, D), f32),
            shape((8, D), f32),
            shape((width, 128), f32),
            *halves(ATTN_ROWS),
        ],
        [place, grad, values, vec, entry, qkv, prob, mix, rel_table, *parts],
        [smem()] + [vmem()] * (8 + n),
        [
            pltpu.VMEM((4, D, D), bf16),
            pltpu.VMEM((pairs, rows, 128), bf16),
            pltpu.VMEM((3, pairs, rows, 128), bf16),
        ],
        "attend_back",
    )


def convolve(values, vec, parts, place, plan, count):
    rows = values.shape[0]
    each = rows // count
    n = len(parts)
    cols = D // 128
    chunk = 64

    def kernel(place_ref, x_ref, vec_ref, *rest):
        ws = rest[:n]
        out_ref, entry_ref, gated_ref, sig_ref, conv_ref, act_ref, weight = rest[n:]
        join(place_ref, ws, weight)
        x = x_ref[...]
        normed, _ = stats(x)
        entry = (normed * vec_ref[33:34, :]).astype(bf16)
        entry_ref[...] = entry
        linear = dot(entry, weight[:, :D])
        sig = logistic(dot(entry, weight[:, D : 2 * D]))
        sig_ref[...] = sig
        gated = linear * sig
        for s in range(count):
            for c in range(cols):
                gated_ref[s, c, :LEAD, :] = jnp.zeros((LEAD, 128), f32)
                gated_ref[s, c, LEAD:, :] = gated[s * each : (s + 1) * each, c * 128 : (c + 1) * 128]
        def column(c, outer):
            lanes = pl.ds(pl.multiple_of(c * 128, 128), 128)
            taps = vec_ref[0:32, lanes]

            def step(i, carry):
                s = i // (each // chunk)
                t = (i % (each // chunk)) * chunk
                total = jnp.zeros((chunk, 128), f32)
                for k in range(KERNEL):
                    total = total + taps[k : k + 1] * gated_ref[s, c, pl.ds(t + k + LEAD - KERNEL + 1, chunk), :]
                conv_ref[pl.ds(pl.multiple_of(i * chunk, chunk), chunk), lanes] = total
                return carry

            lax.fori_loop(0, rows // chunk, step, 0)
            return outer

        lax.fori_loop(0, cols, column, 0)
        inner, _ = stats(conv_ref[...])
        act = inner * vec_ref[34:35, :]
        low = (act * logistic(act)).astype(bf16)
        act_ref[...] = low
        out_ref[...] = x + dot(low, weight[:, 2 * D :])

    return call(
        kernel,
        [
            shape((rows, D), f32),
            shape((rows, D), bf16),
            shape((count, cols, each + LEAD, 128), f32),
            shape((rows, D), f32),
            shape((rows, D), f32),
            shape((rows, D), bf16),
        ],
        [place, values, vec, *parts],
        [smem()] + [vmem()] * (2 + n),
        [pltpu.VMEM((D, 3 * D), bf16)],
        "convolve",
    )


def convolve_back(grad, values, vec, kept, parts, place, plan, count):
    rows = values.shape[0]
    each = rows // count
    n = len(parts)
    cols = D // 128
    entry, gated, sig, conved, act = kept

    def kernel(place_ref, grad_ref, x_ref, vec_ref, entry_ref, gated_ref, sig_ref, conv_ref, act_ref, *rest):
        ws = rest[:n]
        dx_ref, gain_ref, taps_out, *g_refs = rest[n : n + 5]
        weight, dconv, dgated = rest[n + 5 :]
        join(place_ref, ws, weight)
        down = grad_ref[...]
        low = down.astype(bf16)
        put(g_refs, plan, place_ref, dot_rows(act_ref[...], low), 32, 16, 0)
        inner, inner_scale = stats(conv_ref[...])
        inner_gain = vec_ref[34:35, :]
        act_in = inner * inner_gain
        grad_act = dot_cols(low, weight[:, 2 * D :]) * slope_of(act_in, logistic(act_in))
        grad_conv, gain_inner = norm_back(grad_act, inner, inner_scale, inner_gain)
        for s in range(count):
            for c in range(cols):
                dconv[s, c, :each, :] = grad_conv[s * each : (s + 1) * each, c * 128 : (c + 1) * 128]
                dconv[s, c, each:, :] = jnp.zeros((LEAD, 128), f32)
        def column(c, outer):
            lanes = pl.ds(pl.multiple_of(c * 128, 128), 128)
            taps = vec_ref[0:32, lanes]

            def step(i, sums):
                s = i // (each // 8)
                t = (i % (each // 8)) * 8
                here = dconv[s, c, pl.ds(pl.multiple_of(t, 8), 8), :]
                total = jnp.zeros((8, 128), f32)
                new = []
                for k in range(KERNEL):
                    new.append(sums[k] + here * gated_ref[s, c, pl.ds(t + k + LEAD - KERNEL + 1, 8), :])
                    total = total + taps[k : k + 1] * dconv[s, c, pl.ds(t + KERNEL - 1 - k, 8), :]
                dgated[pl.ds(pl.multiple_of(i * 8, 8), 8), lanes] = total
                return tuple(new)

            sums = lax.fori_loop(0, rows // 8, step, tuple(jnp.zeros((8, 128), f32) for _ in range(KERNEL)))
            found = [jnp.sum(v, axis=0, keepdims=True) for v in sums]
            taps_out[:, lanes] = jnp.concatenate(found + [jnp.zeros((1, 128), f32)], axis=0)
            return outer

        lax.fori_loop(0, cols, column, 0)
        grad_gated = dgated[...]
        sig_wide = sig_ref[...]
        linear_sig = jnp.concatenate(
            [
                jnp.concatenate([gated_ref[s, c, LEAD:, :] for c in range(cols)], axis=1)
                for s in range(count)
            ],
            axis=0,
        )
        grad_one = (grad_gated * sig_wide).astype(bf16)
        grad_two = (grad_gated * linear_sig * (1.0 - sig_wide)).astype(bf16)
        entry_low = entry_ref[...]
        put(g_refs, plan, place_ref, dot_rows(entry_low, grad_one), 0, 16, 0)
        put(g_refs, plan, place_ref, dot_rows(entry_low, grad_two), 16, 16, 0)
        grad_entry = dot_cols(grad_one, weight[:, :D]) + dot_cols(grad_two, weight[:, D : 2 * D])
        normed, scale = stats(x_ref[...])
        back, gain_outer = norm_back(grad_entry, normed, scale, vec_ref[33:34, :])
        dx_ref[...] = down + back
        gain_ref[...] = jnp.concatenate([gain_outer, gain_inner, jnp.zeros((6, D), f32)], axis=0)

    return call(
        kernel,
        [
            shape((rows, D), f32),
            shape((8, D), f32),
            shape((32, D), f32),
            *halves(CONV_ROWS),
        ],
        [place, grad, values, vec, entry, gated, sig, conved, act, *parts],
        [smem()] + [vmem()] * (8 + n),
        [
            pltpu.VMEM((D, 3 * D), bf16),
            pltpu.VMEM((count, cols, each + LEAD, 128), f32),
            pltpu.VMEM((rows, D), f32),
        ],
        "convolve_back",
    )


def adam(weight, moment, square, grad):
    new_moment = BETA_FIRST * moment + (1.0 - BETA_FIRST) * grad
    new_square = BETA_SECOND * square + (1.0 - BETA_SECOND) * grad * grad
    first = new_moment * (1.0 / (1.0 - BETA_FIRST**STEP))
    second = new_square * (1.0 / (1.0 - BETA_SECOND**STEP))
    update = first / (jnp.sqrt(second) + ADAM_EPSILON) + WEIGHT_DECAY * weight
    return new_moment, new_square, update


def folded(values):
    squares = jnp.sum((values * values).reshape(-1, values.shape[-1]), axis=0, keepdims=True)
    total = squares[:, :128]
    for c in range(1, values.shape[-1] // 128):
        total = total + squares[:, c * 128 : (c + 1) * 128]
    return total


def update_matrix(layer, pieces, block, spots, states, given, name):
    count = spots.shape[0]
    rows, cols = states[0].shape[1] // count, states[0].shape[2]
    given = given or ()

    half = count // 2

    def kernel(spot_ref, g0_near, g0_far, g1_near, g1_far, w_ref, m_ref, q_ref, *rest):
        g_out, u_out, m_out, q_out, sums = rest[len(given) :]
        index = 2 * pl.program_id(0)

        @pl.when(pl.program_id(0) == 0)
        def _():
            sums[...] = jnp.zeros_like(sums)

        grads = []
        for k, near, far in ((0, g0_near, g0_far), (1, g1_near, g1_far)):
            raw = jnp.where(spot_ref[index + k] < half, near[0], far[0]).astype(f32)
            grads.append(jnp.concatenate([raw[k * rows : (k + 1) * rows] for k in range(cols // D)], axis=1))
        grad = jnp.concatenate(grads, axis=0)
        weight = w_ref[0]
        new_moment, new_square, update = adam(weight, m_ref[0], q_ref[0], grad)
        g_out[0] = grad
        u_out[0] = update
        m_out[0] = new_moment
        q_out[0] = new_square
        sums[...] += jnp.concatenate([folded(weight), folded(update), jnp.zeros((6, 128), f32)], axis=0)

    tile = pl.BlockSpec((1, 2 * rows, cols), lambda p, spot: (layer, p, 0))
    return pl.pallas_call(
        kernel,
        out_shape=[shape(states[0].shape, f32)] * 4 + [shape((8, 128), f32)],
        grid_spec=pltpu.PrefetchScalarGridSpec(
            num_scalar_prefetch=1,
            grid=(count // 2,),
            in_specs=[
                pl.BlockSpec((1, 64, D), lambda p, spot, k=k: (spot[2 * p + k] % half, block, 0))
                for k in (0, 0, 1, 1)
            ]
            + [tile] * 3
            + [pl.BlockSpec(memory_space=pl.ANY)] * len(given),
            out_specs=[tile] * 4 + [pl.BlockSpec((8, 128), lambda p, spot: (0, 0))],
        ),
        input_output_aliases={8 + k: k for k in range(len(given))},
        compiler_params=pltpu.CompilerParams(vmem_limit_bytes=STREAM_LIMIT),
        name=name,
    )(spots, *pieces, *pieces, *states, *given)


def move_layer(layer, win, in_update, in_factor, wout, out_update, out_factor):
    steps = 4
    tiles = [pl.BlockSpec((1, w.shape[1] // steps, w.shape[2]), lambda p: (layer, p, 0)) for w in (win, wout)]

    def kernel(factor_ref, w0, u0, w1, u1, out0, out1):
        out0[...] = w0[...] - (LEARN_RATE * factor_ref[0]) * u0[...]
        out1[...] = w1[...] - (LEARN_RATE * factor_ref[1]) * u1[...]

    return pl.pallas_call(
        kernel,
        out_shape=[shape(win.shape, f32), shape(wout.shape, f32)],
        grid=(steps,),
        in_specs=[smem(), tiles[0], tiles[0], tiles[1], tiles[1]],
        out_specs=tiles,
        input_output_aliases={2: 0, 4: 1},
        compiler_params=pltpu.CompilerParams(vmem_limit_bytes=STREAM_LIMIT),
        name="move_layer",
    )(jnp.stack([in_factor, out_factor]), win, in_update, wout, out_update)


def move_rest(attn, attn_update, conv, conv_update, factors):
    steps = 4
    rows = attn.shape[1] // steps
    attn_tile = pl.BlockSpec((4, rows, D), lambda p: (0, p, 0))
    conv_tile = pl.BlockSpec((rows, 3 * D), lambda p: (p, 0))

    def kernel(factor_ref, w0, u0, w1, u1, out0, out1):
        for k in range(4):
            out0[k] = w0[k] - (LEARN_RATE * factor_ref[k]) * u0[k]
        for k, lanes in ((4, slice(0, 2 * D)), (5, slice(2 * D, 3 * D))):
            out1[:, lanes] = w1[:, lanes] - (LEARN_RATE * factor_ref[k]) * u1[:, lanes]

    return pl.pallas_call(
        kernel,
        out_shape=[shape(attn.shape, f32), shape(conv.shape, f32)],
        grid=(steps,),
        in_specs=[smem(), attn_tile, attn_tile, conv_tile, conv_tile],
        out_specs=[attn_tile, conv_tile],
        input_output_aliases={2: 0, 4: 1},
        compiler_params=pltpu.CompilerParams(vmem_limit_bytes=STREAM_LIMIT),
        name="move_rest",
    )(factors, attn, attn_update, conv, conv_update)


def packed(gains_first, gains_attn, gains_conv, gains_last, taps, rel_wide, each):
    edge = 2 * each - BACK

    def kernel(g0, g1, g2, g4, taps_ref, rel_ref, out_ref, rel):
        out_ref[...] = jnp.zeros_like(out_ref)
        out_ref[0:KERNEL, :] = taps_ref[0:KERNEL, :]
        out_ref[31:32, :] = g0[0:1, :]
        out_ref[32:33, :] = g1[0:1, :]
        out_ref[33:35, :] = g2[0:2, :]
        out_ref[35:37, :] = g4[0:2, :]
        half = rel_ref[:, :HEAD] + rel_ref[:, HEAD:]
        rel[...] = jnp.zeros_like(rel)
        rel[0:1, :] = jnp.sum(half[each : edge + 8] * (lax.broadcasted_iota(jnp.int32, (each - BACK + 8, 1), 0) <= each - BACK), axis=0, keepdims=True)
        rel[0:BACK, :] = rel[0:BACK, :] + half[edge:] * (lax.broadcasted_iota(jnp.int32, (BACK, 1), 0) > 0)
        rel[BACK : BACK + AHEAD, :] = half[:AHEAD]
        rel[RELS - 1 : RELS, :] = jnp.sum(half[AHEAD:each], axis=0, keepdims=True)
        for b in range(5):
            out_ref[40:56, b * HEAD : (b + 1) * HEAD] = rel[b * 16 : b * 16 + 16, :]

    return call(
        kernel,
        [shape((56, D), f32)],
        [gains_first, gains_attn, gains_conv, gains_last, taps, rel_wide],
        [vmem()] * 6,
        [pltpu.VMEM((80, HEAD), f32)],
        "packed",
    )[0]


def update_rest(pieces, spots, attn, conv):
    count = spots.shape[0]
    rows = 2 * (attn[0].shape[1] // count)

    half = count // 2

    def kernel(spot_ref, g0_near, g0_far, g1_near, g1_far, wa, ma, qa, wc, mc, qc, *outs):
        ga_out, ua_out, ma_out, qa_out, qo_out, gc_out, uc_out, mc_out, qc_out, sums = outs
        index = pl.program_id(0)

        @pl.when(index == 0)
        def _():
            sums[...] = jnp.zeros_like(sums)

        raws = [
            jnp.where(spot_ref[2 * index + k] < half, near[0], far[0])
            for k, near, far in ((0, g0_near, g0_far), (1, g1_near, g1_far))
        ]
        found = []
        for k in range(4):
            low = CONV_ROWS + k * 16
            grad = jnp.concatenate([g[low : low + 16] for g in raws], axis=0).astype(f32)
            weight = wa[k]
            new_moment, new_square, update = adam(weight, ma[k], qa[k], grad)
            ga_out[k] = grad
            ua_out[k] = update
            ma_out[k] = new_moment
            if k < 3:
                qa_out[k] = new_square
            else:
                qo_out[...] = new_square
            found += [folded(weight), folded(update)]
        for low, high in ((0, 2), (2, 3)):
            lanes = slice(low * D, high * D)
            parts = [
                jnp.concatenate([g[k * 16 : (k + 1) * 16] for k in range(low, high)], axis=1) for g in raws
            ]
            grad = jnp.concatenate(parts, axis=0).astype(f32)
            weight = wc[:, lanes]
            new_moment, new_square, update = adam(weight, mc[:, lanes], qc[:, lanes], grad)
            gc_out[:, lanes] = grad
            uc_out[:, lanes] = update
            mc_out[:, lanes] = new_moment
            qc_out[:, lanes] = new_square
            found += [folded(weight), folded(update)]
        sums[...] += jnp.concatenate(found + [jnp.zeros((4, 128), f32)], axis=0)

    attn_block = pl.BlockSpec((4, rows, D), lambda p, spot: (0, p, 0))
    conv_block = pl.BlockSpec((rows, 3 * D), lambda p, spot: (p, 0))
    three = pl.BlockSpec((3, rows, D), lambda p, spot: (0, p, 0))
    one = pl.BlockSpec((rows, D), lambda p, spot: (p, 0))
    side = attn[0].shape[1]
    return pl.pallas_call(
        kernel,
        out_shape=[shape(attn[0].shape, f32)] * 3
        + [shape((3, side, D), f32), shape((side, D), f32)]
        + [shape(conv[0].shape, f32)] * 4
        + [shape((16, 128), f32)],
        grid_spec=pltpu.PrefetchScalarGridSpec(
            num_scalar_prefetch=1,
            grid=(count // 2,),
            in_specs=[
                pl.BlockSpec((1, CONV_ROWS + ATTN_ROWS, D), lambda p, spot, k=k: (spot[2 * p + k] % half, 0, 0))
                for k in (0, 0, 1, 1)
            ]
            + [attn_block] * 3
            + [conv_block] * 3,
            out_specs=[attn_block] * 3
            + [three, one]
            + [conv_block] * 4
            + [pl.BlockSpec((16, 128), lambda p, spot: (0, 0))],
        ),
        compiler_params=pltpu.CompilerParams(vmem_limit_bytes=STREAM_LIMIT),
        name="update_rest",
    )(spots, *pieces, *pieces, *attn, *conv)


def move(weight, update, factor):
    return weight - LEARN_RATE * factor * update


def ratio_of(sums):
    weight, update = sums[0::2], sums[1::2]
    return jnp.sqrt(weight), jnp.sqrt(update), jnp.sqrt(weight) / jnp.sqrt(update + RATIO_EPSILON)


def body(
    frames,
    lengths,
    cotangent,
    ffn_in,
    ffn_in_moment,
    ffn_in_square,
    ffn_out,
    ffn_out_moment,
    ffn_out_square,
    attn_proj,
    attn_moment,
    attn_square,
    conv_proj,
    conv_moment,
    conv_square,
    vectors,
    vectors_moment,
    vectors_square,
    rel_keys,
    rel_moment,
    rel_square,
):
    groups, shards = lax.axis_size("group"), lax.axis_size("shard")
    plan = Plan(groups, shards)
    group, shard = lax.axis_index("group"), lax.axis_index("shard")
    core = jnp.bitwise_and(group, 1)
    count, each, _ = frames.shape
    mine = jnp.int32(0)
    for step in plan.order:
        bit = jnp.right_shift(group if step[0] == "group" else shard, step[1]) & 1
        mine = mine * 2 + bit
    kept = jnp.int32(0)
    for step in plan.kept:
        kept = kept * 2 + (jnp.right_shift(group, step[1]) & 1)
    spots = jnp.array([plan.kept_place(p) for p in range(plan.owned)], jnp.int32) ^ kept
    place = jnp.stack([shard, core, mine]).astype(jnp.int32)

    first_halves = rounded_halves(plan, core, (ffn_in, 1, 0), (ffn_out, 1, 0))
    rows, halves_left = rounded_rows(plan, core, ffn_in, ffn_out, attn_proj, conv_proj)
    win0, wout0 = (Fetch(w, 0, plan, r, v, 0) for w, r, v in zip((ffn_in, ffn_out), rows, first_halves))
    watt = Fetch(attn_proj, 1, plan, rows[4], halves_left[0])
    wconv = Fetch(conv_proj, 0, plan, rows[5], halves_left[1])
    win1, wout1 = (Fetch(w, 0, plan, r, v, 1) for w, r, v in zip((ffn_in, ffn_out), rows[2:4], halves_left[2:]))
    win0.near()
    vec = lax.all_gather(vectors.astype(bf16), "shard", axis=1, tiled=True) if shards != 2 else None
    if vec is None:
        (low,) = gate([vectors.astype(bf16)], [first_halves[0]])
        other = swap(low, ("shard", 0))
        vec = jnp.where(shard == 0, jnp.concatenate([low, other], 1), jnp.concatenate([other, low], 1))
    vec = jnp.concatenate([vec.astype(f32), jnp.zeros((3, D), f32)], axis=0)
    rel_low = rel_keys.astype(bf16)
    table = jnp.concatenate(
        [
            rel_low[BACK:],
            jnp.broadcast_to(rel_low[RELS - 1 :], (each - AHEAD - 1, HEAD)),
            jnp.broadcast_to(rel_low[:1], (each - BACK, HEAD)),
            rel_low[:BACK],
        ],
        axis=0,
    )
    table = jnp.concatenate([table, table], axis=1)

    flat = frames.reshape(count * each, D)
    if shards == 2:
        order((win0,), (rows[0],))
    order((wout0,), (win0.value, vec))
    wout0.near()
    win0 = win0.far()
    entry0, hidden0, slope0 = ffn_first_up(flat, vec, win0, place)
    order((watt,), (wout0.value, entry0))
    watt.near()
    order((wout0,), (entry0,))
    order((wconv,), (watt.value,))
    order((win1,), (watt.value,))
    wconv.near()
    win1.near()
    wout0 = wout0.far()
    hidden0, watt.value = gate([hidden0, watt.value], [entry0])
    watt = watt.far()
    x1 = ffn_first_down(flat, hidden0, wout0, place)
    x2, *kept_attn = attend(x1, vec, table, lengths, watt, place, plan)
    order((wconv,), (x2,))
    order((wout1,), (x2,))
    wout1.near()
    wconv = wconv.far()
    x3, *kept_conv = convolve(x2, vec, wconv, place, plan, count)
    order((win1,), (x3,))
    win1 = win1.far()
    order((wout1,), (x3,))
    wout1 = wout1.far()
    output, d3, gains_last, *pieces = ffn_last(
        x3, vec, cotangent.reshape(count * each, D), lengths, win1, wout1, place, plan
    )
    last = Chain(*pieces, plan)
    d2, gains_conv, taps, *pieces = beside(
        [last], lambda d: convolve_back(d, x2, vec, kept_conv, wconv, place, plan, count), [d3], 1
    )
    conv = Chain(*pieces, plan)
    d1, gains_attn, rel_wide, *pieces = beside(
        [last, conv], lambda d: attend_back(d, x1, vec, kept_attn, table, watt, place, plan, count), [d2], 1
    )
    attn = Chain(*pieces, plan)
    before0, *pieces = beside(
        [last, conv, attn], lambda d: ffn_first_out(d, hidden0, slope0, wout0, place, plan), [d1], 0
    )
    first_out = Chain(*pieces, plan)
    early = [last, attn, first_out] if len(conv.todo) < len(attn.todo) else [last, conv, attn, first_out]
    d0, gains_first, *pieces = beside(
        early, lambda b: ffn_first_in(d1, flat, vec, entry0, b, win0, place, plan), [before0], 1
    )
    first_in = Chain(*pieces, plan)
    middle = merged(conv, attn, plan)
    small = Everywhere(packed(gains_first, gains_attn, gains_conv, gains_last, taps, rel_wide, each), plan)
    advance([last, middle, first_out, first_in, small], 1)
    advance([last, middle, first_in, small], 1)
    first = merged(first_out, first_in, plan)
    chains = [last, middle, first, small]
    advance(chains, len(last.todo))
    in_states = (ffn_in, ffn_in_moment, ffn_in_square)
    out_states = (ffn_out, ffn_out_moment, ffn_out_square)
    *half_out, sums_out1 = beside(
        chains, lambda *v: update_matrix(1, v, 1, spots, out_states, None, "update_out1"), last.kept, -1
    )
    *half_in, sums_in1 = beside(
        chains, lambda *v: update_matrix(1, v, 0, spots, in_states, None, "update_in1"), last.kept, -1
    )
    advance(chains, len(middle.todo))
    attn_states = (attn_proj, attn_moment, attn_square)
    conv_states = (conv_proj, conv_moment, conv_square)
    (attn_grad, attn_up, attn_m, attn_q, attn_qo, conv_grad, conv_up, conv_m, conv_q, sums_rest) = beside(
        chains, lambda *v: update_rest(v, spots, attn_states, conv_states), middle.kept, -1
    )
    advance([small], len(small.todo))
    small = small.kept
    wide = vectors.shape[1]
    vec_grad = lax.dynamic_slice(small, (0, shard * wide), (KERNEL + 6, wide))
    rel_grad = jnp.concatenate([small[40:56, b * HEAD : (b + 1) * HEAD] for b in range(5)], axis=0)[:RELS]
    vec_m, vec_q, vec_up = adam(vectors, vectors_moment, vectors_square, vec_grad)
    rel_m, rel_q, rel_up = (
        v.T for v in adam(rel_keys.T, rel_moment.T, rel_square.T, rel_grad.T)
    )

    vec_sums = []
    for part in (vectors, vec_up):
        squares = jnp.sum(part * part, axis=1)
        vec_sums.append(jnp.concatenate([jnp.sum(squares[:KERNEL])[None], squares[KERNEL:]]))
    early = jnp.sum(jnp.concatenate([sums_in1[:2], sums_out1[:2], sums_rest[:12]], axis=0), axis=1)
    early = sum_shards(jnp.concatenate([early, jnp.stack(vec_sums, axis=1).reshape(-1)]), plan)
    early_ratio = ratio_of(early)
    fast = early_ratio[2]
    half_in[1], half_out[1] = beside(
        chains,
        lambda u: move_layer(1, ffn_in, u, fast[0], ffn_out, half_out[1], fast[1]),
        [half_in[1]],
        0,
    )
    advance(chains, len(first.todo))
    out_grad, out_up, out_m, out_q, sums_out0 = update_matrix(
        0, first.kept, 0, spots, out_states, half_out, "update_out0"
    )
    in_grad, in_up, in_m, in_q, sums_in0 = update_matrix(
        0, first.kept, 1, spots, in_states, half_in, "update_in0"
    )
    final = sum_shards(jnp.sum(jnp.concatenate([sums_in0[:2], sums_out0[:2]], axis=0), axis=1), plan)
    rel_sums = jnp.stack([jnp.sum(rel_keys.T * rel_keys.T), jnp.sum(rel_up.T * rel_up.T)])
    late_ratio = ratio_of(rel_sums)
    final_ratio = ratio_of(final)

    def spread(n):
        e, l = early_ratio[n], late_ratio[n]
        none = jnp.zeros((1,), f32)
        return jnp.concatenate([none, e[0:1], none, e[1:2], e[2:15], l[0:1]])

    column = lax.broadcasted_iota(jnp.int32, (2, 18), 1)
    last_in = jnp.stack([final_ratio[0][0], final_ratio[1][0]])[:, None]
    last_out = jnp.stack([final_ratio[0][1], final_ratio[1][1]])[:, None]
    known = jnp.stack([spread(0), spread(1)])
    trust_norms = jnp.where(column == 0, last_in, jnp.where(column == 2, last_out, known))
    ffn_in_new, ffn_out_new = move_layer(
        0, ffn_in, in_up, final_ratio[2][0], ffn_out, out_up, final_ratio[2][1]
    )
    attn_new, conv_new = move_rest(attn_proj, attn_up, conv_proj, conv_up, fast[2:8])
    vec_factor = jnp.concatenate([jnp.full((KERNEL,), fast[8]), fast[9:15]])[:, None]
    return (
        output.reshape(frames.shape),
        d0.reshape(frames.shape),
        in_grad,
        ffn_in_new,
        in_m,
        in_q,
        out_grad,
        ffn_out_new,
        out_m,
        out_q,
        attn_grad,
        attn_new,
        attn_m,
        attn_q,
        attn_qo,
        conv_grad,
        conv_new,
        conv_m,
        conv_q,
        vec_grad,
        move(vectors, vec_up, vec_factor),
        vec_m,
        vec_q,
        rel_grad,
        move(rel_keys.T, rel_up.T, late_ratio[2][0]).T,
        rel_m,
        rel_q,
        trust_norms,
    )


def solution(mesh):
    return jax.shard_map(
        body,
        mesh=mesh,
        in_specs=(
            P(("group", "shard"), None, None),
            P(("group", "shard")),
            P(("group", "shard"), None, None),
            P(None, "shard", None),
            P(None, "shard", None),
            P(None, "shard", None),
            P(None, "shard", None),
            P(None, "shard", None),
            P(None, "shard", None),
            P(None, "shard", None),
            P(None, "shard", None),
            P(None, "shard", None),
            P("shard", None),
            P("shard", None),
            P("shard", None),
            P(None, "shard"),
            P(None, "shard"),
            P(None, "shard"),
            P(),
            P(),
            P(),
        ),
        out_specs=(
            P(("group", "shard"), None, None),
            P(("group", "shard"), None, None),
            P(None, "shard", None),
            P(None, "shard", None),
            P(None, "shard", None),
            P(None, "shard", None),
            P(None, "shard", None),
            P(None, "shard", None),
            P(None, "shard", None),
            P(None, "shard", None),
            P(None, "shard", None),
            P(None, "shard", None),
            P(None, "shard", None),
            P(None, "shard", None),
            P("shard", None),
            P("shard", None),
            P("shard", None),
            P("shard", None),
            P("shard", None),
            P(None, "shard"),
            P(None, "shard"),
            P(None, "shard"),
            P(None, "shard"),
            P(),
            P(),
            P(),
            P(),
            P(),
        ),
        check_vma=False,
    )
```
